32 devices in a mesh: modes: 2 (over x), rows: 16 (over z, y, core).
Axes of the slice: x: 2, y: 2, z: 4, core: 2. Of those that a mesh axis runs over, the one named last changes fastest.
Arguments:
- probe_modes: bfloat16 [4, 2, 2048, 2048], P('modes', None, 'rows'), may hold values from -2.5 to 2.5
- transmission: bfloat16 [2, 2048, 2048], P(None, 'rows'), may hold values from -6 to 6
- hologram: float32 [2048, 2048], P('rows'), may hold values from 0.5 to 4
- phase_cols: float32 [2048], replicated, may hold values from -3.140625 to 3.140625
- phase_rows: float32 [2048], replicated, may hold values from -3.140625 to 3.140625
Outputs:
- new_probe: bfloat16 [4, 2, 2048, 2048], P('modes', None, 'rows')
The draws below stay inside these ranges and needn't reach their ends.
All inputs are finite; a program needn't handle non-finite values.
Results may differ from the reference program's by a relative error of at most 0.018.
Values may be sent and summed in bfloat16 or wider, within the bound.
A program may use at most 64 MiB of HBM per device.

```python
import math
import jax
import jax.numpy as jnp
from jax import lax

N = 2048
FACTOR_A = 128
MODES = 4


def block_scale(rng, shape, split, least, high):
    def one(axis_at, blocks):
        heights = jax.random.uniform(jax.random.fold_in(jax.random.fold_in(rng, 6), axis_at), (blocks,), jnp.float32, least / len(split), high / len(split))
        return jnp.repeat(jnp.exp(heights), shape[axis_at] // blocks).reshape((-1,) + (1,) * (len(shape) - axis_at - 1))

    level = one(*split[0])
    for cut in split[1:]:
        level = level * one(*cut)
    return level


def centred(stream_key, shape, spread, reach, pieces=(), kind=jnp.bfloat16):
    result = spread * jax.random.normal(stream_key, shape, jnp.float32)
    if pieces:
        result = result * block_scale(stream_key, shape, pieces, -0.22, 0.18)
    return jnp.clip(result, -reach, reach).astype(kind)


def setup_inputs(seed: int = 0) -> dict:
    arg_keys = jax.random.split(jax.random.key(seed), 6)
    probe_modes = centred(arg_keys[0], (MODES, 2, N, N), 0.18, 2.5, ((0, 2), (2, 16)))
    transmission = centred(arg_keys[1], (2, N, N), 1.0, 6.0, ((1, 16),))
    hologram = jnp.clip(jnp.exp(math.log(4.0) - 2.0794415 * jax.random.uniform(arg_keys[2], (N, N), jnp.float32) ** block_scale(arg_keys[2], (N, N), ((0, 16),), -0.2, 0.2)), 0.5, 4.0)
    phase_cols = jnp.clip(jax.random.uniform(arg_keys[3], (N,), jnp.float32, -3.140625, 3.140625), -3.140625, 3.140625)
    phase_rows = jnp.clip(jax.random.uniform(arg_keys[4], (N,), jnp.float32, -3.140625, 3.140625), -3.140625, 3.140625)
    return {"probe_modes": probe_modes, "transmission": transmission, "hologram": hologram, "phase_cols": phase_cols, "phase_rows": phase_rows}


def make_block(length, flip):
    indices = jnp.arange(length, dtype=jnp.int32)
    product = indices[:, None] * indices[None, :] % length
    angles = product.astype(jnp.float32) * (2.0 * math.pi / length)
    cosine = jnp.cos(angles)
    sine = flip * jnp.sin(angles)
    matrix = jnp.stack([jnp.stack([cosine, -sine]), jnp.stack([sine, cosine])])
    return matrix.astype(jnp.bfloat16)

def dft_tables(size_b, size_a, inverse):
    flip = 1.0 if inverse else -1.0
    outer = jnp.arange(size_b, dtype=jnp.int32)
    inner = jnp.arange(size_a, dtype=jnp.int32)
    product = outer[:, None] * inner[None, :] % (size_a * size_b)
    angles = product.astype(jnp.float32) * (2.0 * math.pi / (size_a * size_b))
    return (make_block(size_b, flip), make_block(size_a, flip), jnp.cos(angles), flip * jnp.sin(angles))

def phase_tables(phase, size_a, size_b):
    ordered = phase.reshape(size_a, size_b).T
    return (jnp.cos(ordered), jnp.sin(ordered))

def rotate_by(values, cosine, sine):
    real_part = values[:, 0]
    imag_part = values[:, 1]
    return jnp.stack([real_part * cosine - imag_part * sine, real_part * sine + imag_part * cosine], axis=1)

def contract(pattern, matrix, values):
    return jnp.einsum(pattern, matrix.astype(jnp.float32), values.astype(jnp.float32), precision=lax.Precision.HIGHEST)

def transform(values, tables, inverse):
    matrix_b, matrix_a, cosine, sine = tables
    along_b = 'pqkn,mqrna->mprka'
    along_a = 'pqkn,mqrbn->mprbk'
    scale = 1.0 / math.sqrt(matrix_a.shape[-1] * matrix_b.shape[-1])
    if inverse:
        middle = rotate_by(contract(along_a, matrix_a, values), cosine, sine).astype(jnp.bfloat16)
        return contract(along_b, matrix_b, middle) * scale
    middle = rotate_by(contract(along_b, matrix_b, values), cosine, sine).astype(jnp.bfloat16)
    return contract(along_a, matrix_a, middle) * scale

def propagate(field, forward_tables, inverse_tables, cosine, sine):
    full_shape = field.shape
    size_b = forward_tables[0].shape[-1]
    size_a = forward_tables[1].shape[-1]
    split_shape = full_shape[:3] + (size_b, size_a)
    spectrum = transform(field.reshape(split_shape), forward_tables, False)
    spectrum = rotate_by(spectrum, cosine, sine).astype(jnp.bfloat16)
    return transform(spectrum, inverse_tables, True).reshape(full_shape)

def complex_product(field, transmission):
    field_re = field[:, 0].astype(jnp.float32)
    field_im = field[:, 1].astype(jnp.float32)
    trans_re = transmission[0].astype(jnp.float32)
    trans_im = transmission[1].astype(jnp.float32)
    return jnp.stack([field_re * trans_re - field_im * trans_im, field_re * trans_im + field_im * trans_re], axis=1).astype(jnp.bfloat16)

def apply_step(field, transmission, gradient):
    trans_re = transmission[0].astype(jnp.float32)
    trans_im = transmission[1].astype(jnp.float32)
    grad_re = gradient[:, 0]
    grad_im = gradient[:, 1]
    new_re = field[:, 0].astype(jnp.float32) - (trans_re * grad_re + trans_im * grad_im)
    new_im = field[:, 1].astype(jnp.float32) - (trans_re * grad_im - trans_im * grad_re)
    return jnp.stack([new_re, new_im], axis=1).astype(jnp.bfloat16)

def reference(probe_modes, transmission, hologram, phase_cols, phase_rows):
    size_a = FACTOR_A
    size_b = N // FACTOR_A
    forward_tables = dft_tables(size_b, size_a, False)
    inverse_tables = dft_tables(size_b, size_a, True)
    col_cos, col_sin = phase_tables(phase_cols, size_a, size_b)
    row_cos, row_sin = phase_tables(phase_rows, size_a, size_b)

    def detector_of(mode_field):
        exit_wave = complex_product(mode_field[None], transmission)
        after_cols = propagate(exit_wave, forward_tables, inverse_tables, col_cos, col_sin).astype(jnp.bfloat16)
        turned = jnp.swapaxes(after_cols, 2, 3)
        return propagate(turned, forward_tables, inverse_tables, row_cos, row_sin).astype(jnp.bfloat16)

    def accumulate(summed, mode_field):
        detector = detector_of(mode_field).astype(jnp.float32)
        return (summed + lax.optimization_barrier(jnp.sum(detector * detector, axis=(0, 1))), jnp.float32(0.0))
    summed, ignored = lax.scan(accumulate, jnp.zeros((N, N), jnp.float32), probe_modes)
    measured = hologram.T
    factor = 1.0 - jnp.sqrt(measured) / jnp.sqrt(jnp.maximum(summed, 1.0))

    def update(mode_field):
        detector = detector_of(mode_field)
        residual_wave = (detector.astype(jnp.float32) * factor).astype(jnp.bfloat16)
        back_rows = propagate(residual_wave, forward_tables, inverse_tables, row_cos, -row_sin).astype(jnp.bfloat16)
        turned = jnp.swapaxes(back_rows, 2, 3)
        gradient = propagate(turned, forward_tables, inverse_tables, col_cos, -col_sin)
        return apply_step(mode_field[None], transmission, gradient)[0]
    return lax.map(update, probe_modes)
```

```python
import functools
import math

import jax
import jax.numpy as jnp
import numpy as np
from jax import lax
from jax.experimental import pallas as pl
from jax.experimental.pallas import tpu as pltpu
from jax.sharding import PartitionSpec as P

FACTOR_A = 128


def make_block(length, flip):
    indices = jnp.arange(length, dtype=jnp.int32)
    product = indices[:, None] * indices[None, :] % length
    angles = product.astype(jnp.float32) * (2.0 * math.pi / length)
    cosine = jnp.cos(angles)
    sine = flip * jnp.sin(angles)
    matrix = jnp.stack([jnp.stack([cosine, -sine]), jnp.stack([sine, cosine])])
    return matrix.astype(jnp.bfloat16)


def dft_tables(size_b, size_a, inverse):
    flip = 1.0 if inverse else -1.0
    outer = jnp.arange(size_b, dtype=jnp.int32)
    inner = jnp.arange(size_a, dtype=jnp.int32)
    product = outer[:, None] * inner[None, :] % (size_a * size_b)
    angles = product.astype(jnp.float32) * (2.0 * math.pi / (size_a * size_b))
    return (
        make_block(size_b, flip),
        make_block(size_a, flip),
        jnp.cos(angles),
        flip * jnp.sin(angles),
    )


def phase_tables(phase, size_a, size_b):
    ordered = phase.reshape(size_a, size_b).T
    return (jnp.cos(ordered), jnp.sin(ordered))


def rotate_by(values, cosine, sine):
    real_part = values[:, 0]
    imag_part = values[:, 1]
    return jnp.stack(
        [real_part * cosine - imag_part * sine, real_part * sine + imag_part * cosine], axis=1
    )


def transform(values, tables, inverse, layout):
    matrix_b, matrix_a, cosine, sine = tables
    if layout == "cols":
        along_b = "pqkn,mqrna->mprka"
        along_a = "pqkn,mqrbn->mprbk"
    else:
        along_b = "pqkn,mqnas->mpkas"
        along_a = "pqkn,mqbns->mpbks"
        cosine = cosine[:, :, None]
        sine = sine[:, :, None]
    scale = 1.0 / math.sqrt(matrix_a.shape[-1] * matrix_b.shape[-1])
    if inverse:
        middle = jnp.einsum(along_a, matrix_a, values, preferred_element_type=jnp.float32)
        middle = rotate_by(middle, cosine, sine).astype(jnp.bfloat16)
        return jnp.einsum(along_b, matrix_b, middle, preferred_element_type=jnp.float32) * scale
    middle = jnp.einsum(along_b, matrix_b, values, preferred_element_type=jnp.float32)
    middle = rotate_by(middle, cosine, sine).astype(jnp.bfloat16)
    return jnp.einsum(along_a, matrix_a, middle, preferred_element_type=jnp.float32) * scale


def propagate(field, forward_tables, inverse_tables, cosine, sine, layout):
    full_shape = field.shape
    size_b = forward_tables[0].shape[-1]
    size_a = forward_tables[1].shape[-1]
    if layout == "cols":
        split_shape = full_shape[:3] + (size_b, size_a)
        phase_cos, phase_sin = (cosine, sine)
    else:
        split_shape = full_shape[:2] + (size_b, size_a, full_shape[3])
        phase_cos, phase_sin = (cosine[:, :, None], sine[:, :, None])
    spectrum = transform(field.reshape(split_shape), forward_tables, False, layout)
    spectrum = rotate_by(spectrum, phase_cos, phase_sin).astype(jnp.bfloat16)
    return transform(spectrum, inverse_tables, True, layout).reshape(full_shape)


def complex_product(field, transmission):
    field_re = field[:, 0].astype(jnp.float32)
    field_im = field[:, 1].astype(jnp.float32)
    trans_re = transmission[0].astype(jnp.float32)
    trans_im = transmission[1].astype(jnp.float32)
    return jnp.stack(
        [field_re * trans_re - field_im * trans_im, field_re * trans_im + field_im * trans_re],
        axis=1,
    ).astype(jnp.bfloat16)


def apply_step(field, transmission, gradient):
    trans_re = transmission[0].astype(jnp.float32)
    trans_im = transmission[1].astype(jnp.float32)
    grad_re = gradient[:, 0]
    grad_im = gradient[:, 1]
    new_re = field[:, 0].astype(jnp.float32) - (trans_re * grad_re + trans_im * grad_im)
    new_im = field[:, 1].astype(jnp.float32) - (trans_re * grad_im - trans_im * grad_re)
    return jnp.stack([new_re, new_im], axis=1).astype(jnp.bfloat16)


def modulus_factor(detector, measured):
    values = detector.astype(jnp.float32)
    partial_sum = jnp.sum(values * values, axis=(0, 1))
    flattened = partial_sum.reshape(-1)
    measured_flat = measured.reshape(-1)
    summed = lax.psum(flattened.astype(jnp.bfloat16), "modes").astype(jnp.float32)
    factor = 1.0 - jnp.sqrt(measured_flat) / jnp.sqrt(jnp.maximum(summed, 1.0))
    return factor.reshape(partial_sum.shape)


def local(probe_modes, transmission, hologram, phase_cols, phase_rows):
    size_a = FACTOR_A
    size_b = probe_modes.shape[3] // size_a
    forward_tables = dft_tables(size_b, size_a, False)
    inverse_tables = dft_tables(size_b, size_a, True)
    col_cos, col_sin = phase_tables(phase_cols, size_a, size_b)
    row_cos, row_sin = phase_tables(phase_rows, size_a, size_b)
    exit_wave = complex_product(probe_modes, transmission)
    after_cols = propagate(
        exit_wave, forward_tables, inverse_tables, col_cos, col_sin, "cols"
    ).astype(jnp.bfloat16)
    detector_turned = propagate(
        lax.all_to_all(after_cols, "rows", split_axis=3, concat_axis=2, tiled=True),
        forward_tables,
        inverse_tables,
        row_cos,
        row_sin,
        "rows",
    ).astype(jnp.bfloat16)
    measured = lax.all_to_all(
        hologram.astype(jnp.bfloat16), "rows", split_axis=1, concat_axis=0, tiled=True
    ).astype(hologram.dtype)
    factor = modulus_factor(detector_turned, measured)
    residual_wave = (detector_turned.astype(jnp.float32) * factor).astype(jnp.bfloat16)
    back_turned = propagate(
        residual_wave, forward_tables, inverse_tables, row_cos, -row_sin, "rows"
    ).astype(jnp.bfloat16)
    back_rows = lax.all_to_all(back_turned, "rows", split_axis=2, concat_axis=3, tiled=True)
    gradient = propagate(back_rows, forward_tables, inverse_tables, col_cos, -col_sin, "cols")
    return apply_step(probe_modes, transmission, gradient)


MESH = pl.DeviceIdType.MESH
LANES = 128
RADIX = 16
HALVES = 2
PIECES = 4
GROUP = 8
LIMIT_MIB = 60
CHUNK = 16


def rounded(value):
    return float(np.asarray(value, np.float32).astype(jnp.bfloat16).astype(np.float32))


def butterfly4(values, sign):
    (r0, i0), (r1, i1), (r2, i2), (r3, i3) = values
    ar, ai, br, bi = r0 + r2, i0 + i2, r0 - r2, i0 - i2
    cr, ci, dr, di = r1 + r3, i1 + i3, r1 - r3, i1 - i3
    low = (br - di, bi + dr)
    high = (br + di, bi - dr)
    first, third = (low, high) if sign > 0 else (high, low)
    return [(ar + cr, ai + ci), first, (ar - cr, ai - ci), third]


def butterfly16(values, sign):
    middle = [[None] * 4 for _ in range(4)]
    for n0 in range(4):
        for k1, (re, im) in enumerate(butterfly4([values[n0 + 4 * n1] for n1 in range(4)], sign)):
            turn = n0 * k1
            if turn == 4:
                re, im = (-im, re) if sign > 0 else (im, -re)
            elif turn:
                c = rounded(math.cos(2.0 * math.pi * turn / RADIX))
                s = sign * rounded(math.sin(2.0 * math.pi * turn / RADIX))
                re, im = re * c - im * s, re * s + im * c
            middle[n0][k1] = (re, im)
    result = [None] * RADIX
    for k1 in range(4):
        for k0, pair in enumerate(butterfly4([middle[n0][k1] for n0 in range(4)], sign)):
            result[k1 + 4 * k0] = pair
    return result


def turn_by(pair, c, s):
    re, im = pair
    return re * c - im * s, re * s + im * c


def constant_tables(size_a, size_b):
    index = np.arange(size_a)
    angle = (index[:, None] * index[None, :] % size_a).astype(np.float32) * np.float32(2.0 * math.pi / size_a)
    c, s = np.cos(angle), np.sin(angle)
    right_f = np.block([[c, -s], [s, c]])
    right_i = np.block([[c, s], [-s, c]])
    mats = np.stack([right_f, right_i, right_f.T, right_i.T]).astype(jnp.bfloat16)
    size = size_a * size_b
    product = np.arange(size_b)[:, None] * index[None, :] % size
    angle = product.astype(np.float32) * np.float32(2.0 * math.pi / size)
    return mats, np.cos(angle).astype(np.float32), np.sin(angle).astype(np.float32)


def fused_kernel(
    probe_hbm, trans_hbm, holo_hbm, mats_hbm, tw_hbm, twt_hbm, angles_c, angles_r, out,
    probe, trans, holo, mats, tw, twt, phc, pht, snd1, rcv1, snd2, rcv2, hsnd, hbuf, isnd, ircv, uc, ur, det, tables,
    send1, recv1, send2, recv2, hsend, hrecv, xsend, xrecv, isend, irecv, load_sem, piece_sem, out_sem,
):
    f32, bf16 = jnp.float32, jnp.bfloat16
    x, me = lax.axis_index("modes"), lax.axis_index("rows")
    other = 1 - x
    rows = RADIX
    half_rows = probe.shape[2] // PIECES
    per_half = half_rows // CHUNK
    deep = probe.shape[2] // HALVES
    scale = 1.0 / math.sqrt(RADIX * LANES)
    pairs = deep // CHUNK
    lane = lax.broadcasted_iota(jnp.int32, (half_rows, LANES), 1)
    lane_h = lax.broadcasted_iota(jnp.int32, (deep, LANES), 1)
    lane_c = lax.broadcasted_iota(jnp.int32, (CHUNK, LANES), 1)

    def piece_loads(h):
        at = pl.ds(h * half_rows, half_rows)
        return [
            pltpu.make_async_copy(probe_hbm.at[:, :, at], probe.at[:, :, at], piece_sem.at[0, h]),
            pltpu.make_async_copy(trans_hbm.at[:, at], trans.at[:, at], piece_sem.at[1, h]),
        ]

    loads = [piece_loads(h) for h in range(PIECES)]
    load_tw = pltpu.make_async_copy(tw_hbm, tw, load_sem.at[0])
    load_mats = pltpu.make_async_copy(mats_hbm, mats, load_sem.at[1])
    load_twt = pltpu.make_async_copy(twt_hbm, twt, load_sem.at[2])
    load_holo = pltpu.make_async_copy(holo_hbm, holo, load_sem.at[3])
    for copy in [load_holo] + loads[0] + [load_tw, load_mats] + sum(loads[1:], []) + [load_twt]:
        copy.start()

    barrier = pltpu.get_barrier_semaphore()

    @pl.loop(1, rows)
    def _(k):
        pl.semaphore_signal(barrier, inc=1, device_id=(x, lax.rem(me + k, rows)), device_id_type=MESH)

    pl.semaphore_signal(barrier, inc=1, device_id=(other, me), device_id_type=MESH)

    def at_rows(start):
        return pl.ds(pl.multiple_of(start, CHUNK), CHUNK)

    def lanes_of(k):
        return slice(k * LANES, (k + 1) * LANES)

    def dot(a, b):
        return jnp.dot(a, b, preferred_element_type=f32)

    def remote(src, dst, ss, rs, xd, d):
        return pltpu.make_async_remote_copy(
            src_ref=src, dst_ref=dst, send_sem=ss, recv_sem=rs, device_id=(xd, d), device_id_type=MESH
        )

    def send_rows(snd, rcv, ss, rs, g, h):
        pltpu.make_async_copy(snd.at[g, h, me], rcv.at[g, h, me], rs.at[g, h]).start()

        @pl.loop(1, rows)
        def _(k):
            d = lax.rem(me + k, rows)
            remote(snd.at[g, h, d], rcv.at[g, h, me], ss.at[g, h], rs.at[g, h], x, d).start()

    def wait_whole(ref, sem):
        pltpu.make_async_copy(ref, ref, sem).wait()

    def middle_cols(g, sign):
        depth = uc.shape[1]
        base = pl.multiple_of(g * GROUP, GROUP)
        group = pl.ds(base, GROUP)
        y = dot(uc[group].reshape(GROUP * depth, 2 * LANES), mats[0]).reshape(GROUP, depth, 2 * LANES)
        pc, ps = phc[0, group, :][:, None, :], phc[1, group, :][:, None, :] * sign
        re, im = turn_by((y[:, :, :LANES], y[:, :, LANES:]), pc, ps)
        y = jnp.concatenate([re.astype(bf16), im.astype(bf16)], axis=2).reshape(GROUP * depth, 2 * LANES)
        z = dot(y, mats[1]).reshape(GROUP, depth, 2 * LANES)
        c, s = tw[0, group, :][:, None, :] * scale, tw[1, group, :][:, None, :] * scale
        return [turn_by((z[k, :, :LANES], z[k, :, LANES:]), c[k], s[k]) for k in range(GROUP)]

    def cols_forward(h):
        @pl.loop(0, 2 * per_half)
        def _(t):
            mode, j = t // per_half, lax.rem(t, per_half)
            at = at_rows(h * half_rows + j * CHUNK)
            values = []
            for n2 in range(RADIX):
                pr, pi = probe[mode, 0, at, lanes_of(n2)].astype(f32), probe[mode, 1, at, lanes_of(n2)].astype(f32)
                tr, ti = trans[0, at, lanes_of(n2)].astype(f32), trans[1, at, lanes_of(n2)].astype(f32)
                er, ei = pr * tr - pi * ti, pr * ti + pi * tr
                values.append((er.astype(bf16).astype(f32), ei.astype(bf16).astype(f32)))
            dst = at_rows(mode * half_rows + j * CHUNK)
            for k2, pair in enumerate(butterfly16(values, -1)):
                re, im = turn_by(pair, tw[0, k2 : k2 + 1, :], -tw[1, k2 : k2 + 1, :])
                uc[k2, dst, 0:LANES] = re.astype(bf16)
                uc[k2, dst, LANES : 2 * LANES] = im.astype(bf16)

        @pl.loop(0, RADIX // GROUP)
        def _(g):
            for k, pair in enumerate(middle_cols(g, 1.0)):
                k2 = g * GROUP + k
                for part, v in enumerate(pair):
                    a, b = v[:half_rows], v[half_rows:]
                    low = jnp.where(lane < LANES // 2, a, pltpu.roll(b, LANES // 2, 1))
                    high = jnp.where(lane < LANES // 2, pltpu.roll(a, LANES // 2, 1), b)
                    uc[k2, 0:half_rows, lanes_of(part)] = low.astype(bf16)
                    uc[k2, half_rows : 2 * half_rows, lanes_of(part)] = high.astype(bf16)

        @pl.loop(0, 2 * per_half)
        def _(t):
            side, j = t // per_half, lax.rem(t, per_half)
            src = at_rows(side * half_rows + j * CHUNK)
            dst = at_rows(j * CHUNK)
            values = [
                (uc[k2, src, 0:LANES].astype(f32), uc[k2, src, LANES : 2 * LANES].astype(f32)) for k2 in range(RADIX)
            ]
            for n2, (re, im) in enumerate(butterfly16(values, 1)):
                snd1[side, h, n2, 0, dst, :] = re.astype(bf16)
                snd1[side, h, n2, 1, dst, :] = im.astype(bf16)

    def cols_back(h):
        @pl.loop(0, 2 * per_half)
        def _(t):
            side, j = t // per_half, lax.rem(t, per_half)
            at = at_rows(j * CHUNK)
            values = [
                (rcv2[side, h, n2, 0, at, :].astype(f32), rcv2[side, h, n2, 1, at, :].astype(f32))
                for n2 in range(RADIX)
            ]
            dst = at_rows(side * half_rows + j * CHUNK)
            for k2, pair in enumerate(butterfly16(values, -1)):
                c, s = tw[2 + 2 * side, k2 : k2 + 1, :], tw[3 + 2 * side, k2 : k2 + 1, :]
                re, im = turn_by(pair, c, -s)
                uc[k2, dst, 0:LANES] = re.astype(bf16)
                uc[k2, dst, LANES : 2 * LANES] = im.astype(bf16)

        @pl.loop(0, RADIX, unroll=4)
        def _(k2):
            for part in range(2):
                low = uc[k2, 0:half_rows, lanes_of(part)].astype(f32)
                high = uc[k2, half_rows : 2 * half_rows, lanes_of(part)].astype(f32)
                a = jnp.where(lane < LANES // 2, low, pltpu.roll(high, LANES // 2, 1))
                b = jnp.where(lane < LANES // 2, pltpu.roll(low, LANES // 2, 1), high)
                uc[k2, 0:half_rows, lanes_of(part)] = a.astype(bf16)
                uc[k2, half_rows : 2 * half_rows, lanes_of(part)] = b.astype(bf16)

        @pl.loop(0, RADIX // GROUP)
        def _(g):
            for k, pair in enumerate(middle_cols(g, -1.0)):
                for part, v in enumerate(pair):
                    uc[g * GROUP + k, :, lanes_of(part)] = v.astype(bf16)

        @pl.loop(0, 2 * per_half)
        def _(t):
            mode, j = t // per_half, lax.rem(t, per_half)
            src = at_rows(mode * half_rows + j * CHUNK)
            at = at_rows(h * half_rows + j * CHUNK)
            values = [
                (uc[k2, src, 0:LANES].astype(f32), uc[k2, src, LANES : 2 * LANES].astype(f32)) for k2 in range(RADIX)
            ]
            for n2, (gr, gi) in enumerate(butterfly16(values, 1)):
                tr, ti = trans[0, at, lanes_of(n2)].astype(f32), trans[1, at, lanes_of(n2)].astype(f32)
                pr, pi = probe[mode, 0, at, lanes_of(n2)].astype(f32), probe[mode, 1, at, lanes_of(n2)].astype(f32)
                probe[mode, 0, at, lanes_of(n2)] = (pr - (tr * gr + ti * gi)).astype(bf16)
                probe[mode, 1, at, lanes_of(n2)] = (pi - (tr * gi - ti * gr)).astype(bf16)

    def rows_first(load, h):
        @pl.loop(h * per_half, (h + 1) * per_half)
        def _(j):
            at = at_rows(j * CHUNK)
            values = [load(j, n2) for n2 in range(RADIX)]
            for k2, pair in enumerate(butterfly16(values, -1)):
                pick = lanes_of(k2 % 2)
                re, im = turn_by(pair, tables[0, k2 // 2, at, pick], -tables[1, k2 // 2, at, pick])
                ur[k2 // 2, at, pick] = re.astype(bf16)
                ur[k2 // 2, at_rows(LANES + j * CHUNK), pick] = im.astype(bf16)

    def rows_middle(sign):
        @pl.loop(0, RADIX // 2, unroll=2)
        def _(kp):
            y = dot(mats[2], ur[kp])
            re, im = turn_by((y[:LANES], y[LANES:]), tables[2, kp], tables[3, kp] * sign)
            z = dot(mats[3], jnp.concatenate([re.astype(bf16), im.astype(bf16)], axis=0))
            re, im = turn_by((z[:LANES], z[LANES:]), tables[0, kp], tables[1, kp])
            ur[kp, 0:LANES, :] = re.astype(bf16)
            ur[kp, LANES : 2 * LANES, :] = im.astype(bf16)

    def rows_last(store, j):
        at, at_im = at_rows(j * CHUNK), at_rows(LANES + j * CHUNK)
        values = [
            (ur[k2 // 2, at, lanes_of(k2 % 2)].astype(f32), ur[k2 // 2, at_im, lanes_of(k2 % 2)].astype(f32))
            for k2 in range(RADIX)
        ]
        for n2, (re, im) in enumerate(butterfly16(values, 1)):
            store(j, n2, (re * scale).astype(bf16), (im * scale).astype(bf16))

    def own_power(g, n2, at):
        re, im = det[g, n2, 0, at, :].astype(f32), det[g, n2, 1, at, :].astype(f32)
        return re * re + im * im

    def partner(g, j):
        return remote(isnd.at[g, j], ircv.at[g, j], isend.at[g, j], irecv.at[g, j], other, me)

    def rows_forward(g):
        def load(j, n2):
            h, at = j // per_half, at_rows(lax.rem(j, per_half) * CHUNK)
            return rcv1[g, h, n2, 0, at, :].astype(f32), rcv1[g, h, n2, 1, at, :].astype(f32)

        def store(j, n2, re, im):
            det[g, n2, 0, at_rows(j * CHUNK), :] = re
            det[g, n2, 1, at_rows(j * CHUNK), :] = im

        for h in range(PIECES):
            wait_whole(rcv1.at[g, h], recv1.at[g, h])
            rows_first(load, h)
        rows_middle(1.0)

        @pl.loop(0, pairs)
        def _(j):
            rows_last(store, j)
            rows_last(store, j + pairs)
            for n2 in range(RADIX):
                a, b = own_power(g, n2, at_rows(j * CHUNK)), own_power(g, n2, at_rows((j + pairs) * CHUNK))
                first = lane_c < LANES // 2
                total = jnp.where(first, a, b) + pltpu.roll(jnp.where(first, b, a), LANES // 2, 1)
                isnd[g, j, n2] = total.astype(bf16)
            partner(g, j).start()

    def apply_factor(g):
        @pl.loop(0, pairs)
        def _(j):
            wait_whole(ircv.at[g, j], irecv.at[g, j])
            for n2 in range(RADIX):
                total = isnd[g, j, n2].astype(f32) + ircv[g, j, n2].astype(f32)
                measured = hbuf[g, n2, at_rows(j * CHUNK), :].astype(f32)
                factor = 1.0 - jnp.sqrt(measured) * lax.rsqrt(jnp.maximum(total, 1.0))
                swapped = pltpu.roll(factor, LANES // 2, 1)
                first = lane_c < LANES // 2
                for at, f in (
                    (at_rows(j * CHUNK), jnp.where(first, factor, swapped)),
                    (at_rows((j + pairs) * CHUNK), jnp.where(first, swapped, factor)),
                ):
                    for q in range(2):
                        det[g, n2, q, at, :] = (det[g, n2, q, at, :].astype(f32) * f).astype(bf16)

    def rows_back(g):
        def load(j, n2):
            at = at_rows(j * CHUNK)
            return det[g, n2, 0, at, :].astype(f32), det[g, n2, 1, at, :].astype(f32)

        def store(j, n2, re, im):
            h, at = j // per_half, at_rows(lax.rem(j, per_half) * CHUNK)
            snd2[g, h, n2, 0, at, :] = re
            snd2[g, h, n2, 1, at, :] = im

        for h in range(PIECES):
            rows_first(load, h)
        rows_middle(-1.0)
        for h in range(PIECES):
            @pl.loop(h * per_half, (h + 1) * per_half)
            def _(j):
                rows_last(store, j)

            send_rows(snd2, rcv2, send2, recv2, g, h)

    def spectral(natural):
        r = lax.broadcasted_iota(jnp.int32, (rows, LANES), 0)
        c = lax.broadcasted_iota(jnp.int32, (rows, LANES), 1)
        per = LANES // RADIX
        spread = jnp.where(c // per == r, 1.0, 0.0).astype(f32)
        picked = jnp.where(lax.rem(c, RADIX) == r, 1.0, 0.0).astype(f32)
        wide_r = lax.broadcasted_iota(jnp.int32, (LANES, LANES), 0)
        wide_c = lax.broadcasted_iota(jnp.int32, (LANES, LANES), 1)
        exact = lax.Precision.HIGHEST
        full = jnp.dot(natural.T, spread, precision=exact, preferred_element_type=f32)
        full = jnp.where(wide_r // RADIX == lax.rem(wide_c, per), full, 0.0)
        return jnp.dot(picked, full, precision=exact, preferred_element_type=f32)

    load_holo.wait()
    for n2 in range(RADIX):
        upper, lower = holo[0:deep, lanes_of(n2)], holo[deep : 2 * deep, lanes_of(n2)]
        low = jnp.where(lane_h < LANES // 2, upper, pltpu.roll(lower, LANES // 2, 1))
        high = jnp.where(lane_h < LANES // 2, pltpu.roll(upper, LANES // 2, 1), lower)
        hsnd[n2] = jnp.where(x == 0, low, high).astype(bf16)
    angle = spectral(angles_c[...])
    for part, turn in enumerate((jnp.cos, jnp.sin)):
        phc[part] = turn(angle) * scale
    pl.semaphore_wait(barrier, rows)
    pltpu.make_async_copy(hsnd.at[me], hbuf.at[x, me], hrecv).start()

    @pl.loop(1, rows)
    def _(k):
        d = lax.rem(me + k, rows)
        remote(hsnd.at[d], hbuf.at[x, me], hsend, hrecv, x, d).start()

    for copy in [load_tw, load_mats]:
        copy.wait()
    for h in range(PIECES):
        for copy in loads[h]:
            copy.wait()
        cols_forward(h)
        send_rows(snd1, rcv1, send1, recv1, 0, h)
    for h in range(PIECES):
        send_rows(snd1, rcv1, send1, recv1, 1, h)

    wait_whole(hbuf.at[x], hrecv)
    forward = remote(hbuf.at[x], hbuf.at[x], xsend, xrecv, other, me)
    forward.start()

    angle = spectral(angles_r[...])
    for part, turn in enumerate((jnp.cos, jnp.sin)):
        pht[part] = turn(angle).T * scale
    load_twt.wait()
    for k2 in range(RADIX):
        for part in range(2):
            pick = lanes_of(k2 % 2)
            tables[part, k2 // 2, :, pick] = jnp.broadcast_to(twt[part, :, k2 : k2 + 1], (LANES, LANES))
            tables[2 + part, k2 // 2, :, pick] = jnp.broadcast_to(pht[part, :, k2 : k2 + 1], (LANES, LANES))
    wait_whole(hbuf.at[other], xrecv)

    for g in range(HALVES):
        rows_forward(g)
        apply_factor(g)
        rows_back(g)

    stores = []
    for h in range(PIECES):
        for side in range(2):
            wait_whole(rcv2.at[side, h], recv2.at[side, h])
        cols_back(h)
        at = pl.ds(h * half_rows, half_rows)
        stores.append(pltpu.make_async_copy(probe.at[:, :, at], out.at[:, :, at], out_sem.at[h]))
        stores[h].start()

    fewer = pl.ds(0, rows - 1)
    for h in range(PIECES):
        for snd, sem in ((snd1, send1), (snd2, send2)):
            for g in range(2):
                wait_whole(snd.at[g, h, fewer], sem.at[g, h])
    wait_whole(hsnd.at[fewer], hsend)
    forward.wait_send()
    for g in range(2):
        for j in range(pairs):
            partner(g, j).wait_send()
    for copy in stores:
        copy.wait()


def fused_local(probe_modes, transmission, hologram, phase_cols, phase_rows):
    size_a = FACTOR_A
    size_b = probe_modes.shape[3] // size_a
    mats, cosine, sine = constant_tables(size_a, size_b)
    half = size_a // 2
    packed = [np.concatenate([t[:, at : at + half]] * 2, axis=1) for at in (0, half) for t in (cosine, sine)]
    tw = np.stack([cosine, sine] + packed)
    twt = np.stack([cosine.T, sine.T])
    angles = [phase.reshape(size_b, size_a) for phase in (phase_cols, phase_rows)]
    rows = hologram.shape[0]
    field = (2, PIECES, size_b, 2, rows // PIECES, LANES)
    bf16, dma = jnp.bfloat16, pltpu.SemaphoreType.DMA
    vmem, hbm = pl.BlockSpec(memory_space=pltpu.VMEM), pl.BlockSpec(memory_space=pltpu.MemorySpace.HBM)
    shared = (2, rows // HALVES // CHUNK, size_b, CHUNK, LANES)
    return pl.pallas_call(
        fused_kernel,
        out_shape=jax.ShapeDtypeStruct(probe_modes.shape, bf16),
        in_specs=[hbm] * 6 + [vmem] * 2,
        out_specs=hbm,
        scratch_shapes=[
            pltpu.VMEM(probe_modes.shape, bf16),
            pltpu.VMEM(transmission.shape, bf16),
            pltpu.VMEM(hologram.shape, jnp.float32),
            pltpu.VMEM(mats.shape, bf16),
            pltpu.VMEM(tw.shape, jnp.float32),
            pltpu.VMEM(twt.shape, jnp.float32),
            pltpu.VMEM((2, size_b, LANES), jnp.float32),
            pltpu.VMEM((2, LANES, size_b), jnp.float32),
            pltpu.VMEM(field, bf16),
            pltpu.VMEM(field, bf16),
            pltpu.VMEM(field, bf16),
            pltpu.VMEM(field, bf16),
            pltpu.VMEM((size_b, rows // HALVES, LANES), bf16),
            pltpu.VMEM((2, size_b, rows // HALVES, LANES), bf16),
            pltpu.VMEM(shared, bf16),
            pltpu.VMEM(shared, bf16),
            pltpu.VMEM((size_b, 2 * (rows // PIECES), 2 * LANES), bf16),
            pltpu.VMEM((size_b // 2, 2 * LANES, 2 * LANES), bf16),
            pltpu.VMEM((2, size_b, 2, LANES, LANES), bf16),
            pltpu.VMEM((4, size_b // 2, LANES, 2 * LANES), jnp.float32),
            dma((2, PIECES)),
            dma((2, PIECES)),
            dma((2, PIECES)),
            dma((2, PIECES)),
            dma,
            dma,
            dma,
            dma,
            dma(shared[:2]),
            dma(shared[:2]),
            dma((4,)),
            dma((2, PIECES)),
            dma((PIECES,)),
        ],
        compiler_params=pltpu.CompilerParams(
            collective_id=0, has_side_effects=True, vmem_limit_bytes=LIMIT_MIB * 1024 * 1024
        ),
    )(probe_modes, transmission, hologram, jnp.asarray(mats), jnp.asarray(tw), jnp.asarray(twt), *angles)


def chosen(mesh, probe_modes, *others):
    rows, modes = mesh.shape["rows"], mesh.shape["modes"]
    size = probe_modes.shape[3]
    fits = modes == 2 and probe_modes.shape[0] == 2 * modes and size == rows * FACTOR_A == RADIX * LANES
    body = fused_local if fits else local
    return jax.shard_map(
        body,
        mesh=mesh,
        in_specs=(P("modes", None, "rows", None), P(None, "rows", None), P("rows", None), P(), P()),
        out_specs=P("modes", None, "rows", None),
        check_vma=False,
    )(probe_modes, *others)


def solution(mesh):
    return functools.partial(chosen, mesh)
```

```python
import functools
import math

import jax
import jax.numpy as jnp
import numpy as np
from jax import lax
from jax.experimental import pallas as pl
from jax.experimental.pallas import tpu as pltpu
from jax.sharding import PartitionSpec as P

FACTOR_A = 128


def make_block(length, flip):
    indices = jnp.arange(length, dtype=jnp.int32)
    product = indices[:, None] * indices[None, :] % length
    angles = product.astype(jnp.float32) * (2.0 * math.pi / length)
    cosine = jnp.cos(angles)
    sine = flip * jnp.sin(angles)
    matrix = jnp.stack([jnp.stack([cosine, -sine]), jnp.stack([sine, cosine])])
    return matrix.astype(jnp.bfloat16)


def dft_tables(size_b, size_a, inverse):
    flip = 1.0 if inverse else -1.0
    outer = jnp.arange(size_b, dtype=jnp.int32)
    inner = jnp.arange(size_a, dtype=jnp.int32)
    product = outer[:, None] * inner[None, :] % (size_a * size_b)
    angles = product.astype(jnp.float32) * (2.0 * math.pi / (size_a * size_b))
    return (
        make_block(size_b, flip),
        make_block(size_a, flip),
        jnp.cos(angles),
        flip * jnp.sin(angles),
    )


def phase_tables(phase, size_a, size_b):
    ordered = phase.reshape(size_a, size_b).T
    return (jnp.cos(ordered), jnp.sin(ordered))


def rotate_by(values, cosine, sine):
    real_part = values[:, 0]
    imag_part = values[:, 1]
    return jnp.stack(
        [real_part * cosine - imag_part * sine, real_part * sine + imag_part * cosine], axis=1
    )


def transform(values, tables, inverse, layout):
    matrix_b, matrix_a, cosine, sine = tables
    if layout == "cols":
        along_b = "pqkn,mqrna->mprka"
        along_a = "pqkn,mqrbn->mprbk"
    else:
        along_b = "pqkn,mqnas->mpkas"
        along_a = "pqkn,mqbns->mpbks"
        cosine = cosine[:, :, None]
        sine = sine[:, :, None]
    scale = 1.0 / math.sqrt(matrix_a.shape[-1] * matrix_b.shape[-1])
    if inverse:
        middle = jnp.einsum(along_a, matrix_a, values, preferred_element_type=jnp.float32)
        middle = rotate_by(middle, cosine, sine).astype(jnp.bfloat16)
        return jnp.einsum(along_b, matrix_b, middle, preferred_element_type=jnp.float32) * scale
    middle = jnp.einsum(along_b, matrix_b, values, preferred_element_type=jnp.float32)
    middle = rotate_by(middle, cosine, sine).astype(jnp.bfloat16)
    return jnp.einsum(along_a, matrix_a, middle, preferred_element_type=jnp.float32) * scale


def propagate(field, forward_tables, inverse_tables, cosine, sine, layout):
    full_shape = field.shape
    size_b = forward_tables[0].shape[-1]
    size_a = forward_tables[1].shape[-1]
    if layout == "cols":
        split_shape = full_shape[:3] + (size_b, size_a)
        phase_cos, phase_sin = (cosine, sine)
    else:
        split_shape = full_shape[:2] + (size_b, size_a, full_shape[3])
        phase_cos, phase_sin = (cosine[:, :, None], sine[:, :, None])
    spectrum = transform(field.reshape(split_shape), forward_tables, False, layout)
    spectrum = rotate_by(spectrum, phase_cos, phase_sin).astype(jnp.bfloat16)
    return transform(spectrum, inverse_tables, True, layout).reshape(full_shape)


def complex_product(field, transmission):
    field_re = field[:, 0].astype(jnp.float32)
    field_im = field[:, 1].astype(jnp.float32)
    trans_re = transmission[0].astype(jnp.float32)
    trans_im = transmission[1].astype(jnp.float32)
    return jnp.stack(
        [field_re * trans_re - field_im * trans_im, field_re * trans_im + field_im * trans_re],
        axis=1,
    ).astype(jnp.bfloat16)


def apply_step(field, transmission, gradient):
    trans_re = transmission[0].astype(jnp.float32)
    trans_im = transmission[1].astype(jnp.float32)
    grad_re = gradient[:, 0]
    grad_im = gradient[:, 1]
    new_re = field[:, 0].astype(jnp.float32) - (trans_re * grad_re + trans_im * grad_im)
    new_im = field[:, 1].astype(jnp.float32) - (trans_re * grad_im - trans_im * grad_re)
    return jnp.stack([new_re, new_im], axis=1).astype(jnp.bfloat16)


def modulus_factor(detector, measured):
    values = detector.astype(jnp.float32)
    partial_sum = jnp.sum(values * values, axis=(0, 1))
    flattened = partial_sum.reshape(-1)
    measured_flat = measured.reshape(-1)
    summed = lax.psum(flattened.astype(jnp.bfloat16), "modes").astype(jnp.float32)
    factor = 1.0 - jnp.sqrt(measured_flat) / jnp.sqrt(jnp.maximum(summed, 1.0))
    return factor.reshape(partial_sum.shape)


def local(probe_modes, transmission, hologram, phase_cols, phase_rows):
    size_a = FACTOR_A
    size_b = probe_modes.shape[3] // size_a
    forward_tables = dft_tables(size_b, size_a, False)
    inverse_tables = dft_tables(size_b, size_a, True)
    col_cos, col_sin = phase_tables(phase_cols, size_a, size_b)
    row_cos, row_sin = phase_tables(phase_rows, size_a, size_b)
    exit_wave = complex_product(probe_modes, transmission)
    after_cols = propagate(
        exit_wave, forward_tables, inverse_tables, col_cos, col_sin, "cols"
    ).astype(jnp.bfloat16)
    detector_turned = propagate(
        lax.all_to_all(after_cols, "rows", split_axis=3, concat_axis=2, tiled=True),
        forward_tables,
        inverse_tables,
        row_cos,
        row_sin,
        "rows",
    ).astype(jnp.bfloat16)
    measured = lax.all_to_all(
        hologram.astype(jnp.bfloat16), "rows", split_axis=1, concat_axis=0, tiled=True
    ).astype(hologram.dtype)
    factor = modulus_factor(detector_turned, measured)
    residual_wave = (detector_turned.astype(jnp.float32) * factor).astype(jnp.bfloat16)
    back_turned = propagate(
        residual_wave, forward_tables, inverse_tables, row_cos, -row_sin, "rows"
    ).astype(jnp.bfloat16)
    back_rows = lax.all_to_all(back_turned, "rows", split_axis=2, concat_axis=3, tiled=True)
    gradient = propagate(back_rows, forward_tables, inverse_tables, col_cos, -col_sin, "cols")
    return apply_step(probe_modes, transmission, gradient)


MESH = pl.DeviceIdType.MESH
LANES = 128
RADIX = 16
HALVES = 2
PIECES = 4
GROUP = 8
LIMIT_MIB = 40
FINISH_MIB = 12
CHUNK = 16


def rounded(value):
    return float(np.asarray(value, np.float32).astype(jnp.bfloat16).astype(np.float32))


def butterfly4(values, sign):
    (r0, i0), (r1, i1), (r2, i2), (r3, i3) = values
    ar, ai, br, bi = r0 + r2, i0 + i2, r0 - r2, i0 - i2
    cr, ci, dr, di = r1 + r3, i1 + i3, r1 - r3, i1 - i3
    low = (br - di, bi + dr)
    high = (br + di, bi - dr)
    first, third = (low, high) if sign > 0 else (high, low)
    return [(ar + cr, ai + ci), first, (ar - cr, ai - ci), third]


def butterfly16(values, sign):
    middle = [[None] * 4 for _ in range(4)]
    for n0 in range(4):
        for k1, (re, im) in enumerate(butterfly4([values[n0 + 4 * n1] for n1 in range(4)], sign)):
            turn = n0 * k1
            if turn == 4:
                re, im = (-im, re) if sign > 0 else (im, -re)
            elif turn:
                c = rounded(math.cos(2.0 * math.pi * turn / RADIX))
                s = sign * rounded(math.sin(2.0 * math.pi * turn / RADIX))
                re, im = re * c - im * s, re * s + im * c
            middle[n0][k1] = (re, im)
    result = [None] * RADIX
    for k1 in range(4):
        for k0, pair in enumerate(butterfly4([middle[n0][k1] for n0 in range(4)], sign)):
            result[k1 + 4 * k0] = pair
    return result


def turn_by(pair, c, s):
    re, im = pair
    return re * c - im * s, re * s + im * c


def constant_tables(size_a, size_b):
    index = np.arange(size_a)
    angle = (index[:, None] * index[None, :] % size_a).astype(np.float32) * np.float32(2.0 * math.pi / size_a)
    c, s = np.cos(angle), np.sin(angle)
    right_f = np.block([[c, -s], [s, c]])
    right_i = np.block([[c, s], [-s, c]])
    mats = np.stack([right_f, right_i, right_f.T, right_i.T]).astype(jnp.bfloat16)
    size = size_a * size_b
    product = np.arange(size_b)[:, None] * index[None, :] % size
    angle = product.astype(np.float32) * np.float32(2.0 * math.pi / size)
    return mats, np.cos(angle).astype(np.float32), np.sin(angle).astype(np.float32)


def at_rows(start):
    return pl.ds(pl.multiple_of(start, CHUNK), CHUNK)


def lanes_of(k):
    return slice(k * LANES, (k + 1) * LANES)


def dot(a, b):
    return jnp.dot(a, b, preferred_element_type=jnp.float32)


def middle_cols(g, sign, uc, mats, tw, phc):
    bf16 = jnp.bfloat16
    scale = 1.0 / math.sqrt(RADIX * LANES)
    depth = uc.shape[1]
    base = pl.multiple_of(g * GROUP, GROUP)
    group = pl.ds(base, GROUP)
    y = dot(uc[group].reshape(GROUP * depth, 2 * LANES), mats[0]).reshape(GROUP, depth, 2 * LANES)
    pc, ps = phc[0, group, :][:, None, :], phc[1, group, :][:, None, :] * sign
    re, im = turn_by((y[:, :, :LANES], y[:, :, LANES:]), pc, ps)
    y = jnp.concatenate([re.astype(bf16), im.astype(bf16)], axis=2).reshape(GROUP * depth, 2 * LANES)
    z = dot(y, mats[1]).reshape(GROUP, depth, 2 * LANES)
    c, s = tw[0, group, :][:, None, :] * scale, tw[1, group, :][:, None, :] * scale
    return [turn_by((z[k, :, :LANES], z[k, :, LANES:]), c[k], s[k]) for k in range(GROUP)]


def back_piece(load, store, top, height, uc, probe, trans, mats, tw, phc):
    f32, bf16 = jnp.float32, jnp.bfloat16
    chunks = height // CHUNK
    lane = lax.broadcasted_iota(jnp.int32, (height, LANES), 1)

    @pl.loop(0, 2 * chunks)
    def _(t):
        side, j = t // chunks, lax.rem(t, chunks)
        at = at_rows(j * CHUNK)
        values = [(load(side, n2, 0, at).astype(f32), load(side, n2, 1, at).astype(f32)) for n2 in range(RADIX)]
        dst = at_rows(side * height + j * CHUNK)
        for k2, pair in enumerate(butterfly16(values, -1)):
            c, s = tw[2 + 2 * side, k2 : k2 + 1, :], tw[3 + 2 * side, k2 : k2 + 1, :]
            re, im = turn_by(pair, c, -s)
            uc[k2, dst, 0:LANES] = re.astype(bf16)
            uc[k2, dst, LANES : 2 * LANES] = im.astype(bf16)

    @pl.loop(0, RADIX, unroll=4)
    def _(k2):
        for part in range(2):
            low = uc[k2, 0:height, lanes_of(part)].astype(f32)
            high = uc[k2, height : 2 * height, lanes_of(part)].astype(f32)
            a = jnp.where(lane < LANES // 2, low, pltpu.roll(high, LANES // 2, 1))
            b = jnp.where(lane < LANES // 2, pltpu.roll(low, LANES // 2, 1), high)
            uc[k2, 0:height, lanes_of(part)] = a.astype(bf16)
            uc[k2, height : 2 * height, lanes_of(part)] = b.astype(bf16)

    @pl.loop(0, RADIX // GROUP)
    def _(g):
        for k, pair in enumerate(middle_cols(g, -1.0, uc, mats, tw, phc)):
            for part, v in enumerate(pair):
                uc[g * GROUP + k, :, lanes_of(part)] = v.astype(bf16)

    @pl.loop(0, 2 * chunks)
    def _(t):
        mode, j = t // chunks, lax.rem(t, chunks)
        src = at_rows(mode * height + j * CHUNK)
        at = at_rows(top + j * CHUNK)
        values = [
            (uc[k2, src, 0:LANES].astype(f32), uc[k2, src, LANES : 2 * LANES].astype(f32)) for k2 in range(RADIX)
        ]
        for n2, (gr, gi) in enumerate(butterfly16(values, 1)):
            tr, ti = trans[0, at, lanes_of(n2)].astype(f32), trans[1, at, lanes_of(n2)].astype(f32)
            pr, pi = probe[mode, 0, at, lanes_of(n2)].astype(f32), probe[mode, 1, at, lanes_of(n2)].astype(f32)
            store(mode, 0, j, n2, (pr - (tr * gr + ti * gi)).astype(bf16))
            store(mode, 1, j, n2, (pi - (tr * gi - ti * gr)).astype(bf16))


def fused_kernel(
    probe_hbm, trans_hbm, holo_hbm, mats_hbm, tw_hbm, twt_hbm, phase_c_hbm, phase_r_hbm,
    probe, trans, mats, tw, phc, tail,
    angles, holo, twt, pht, snd1, rcv1, snd2, rcv2, hsnd, hbuf, isnd, ircv, uc, ur, det, tables,
    send1, recv1, send2, recv2, hsend, hrecv, xsend, xrecv, isend, irecv, load_sem, piece_sem,
):
    f32, bf16 = jnp.float32, jnp.bfloat16
    x, me = lax.axis_index("modes"), lax.axis_index("rows")
    other = 1 - x
    rows = RADIX
    half_rows = probe.shape[2] // PIECES
    per_half = half_rows // CHUNK
    deep = probe.shape[2] // HALVES
    scale = 1.0 / math.sqrt(RADIX * LANES)
    pairs = deep // CHUNK
    lane = lax.broadcasted_iota(jnp.int32, (half_rows, LANES), 1)
    lane_h = lax.broadcasted_iota(jnp.int32, (deep, LANES), 1)
    lane_c = lax.broadcasted_iota(jnp.int32, (CHUNK, LANES), 1)

    def piece_loads(h):
        at = pl.ds(h * half_rows, half_rows)
        return [
            pltpu.make_async_copy(probe_hbm.at[:, :, at], probe.at[:, :, at], piece_sem.at[0, h]),
            pltpu.make_async_copy(trans_hbm.at[:, at], trans.at[:, at], piece_sem.at[1, h]),
        ]

    loads = [piece_loads(h) for h in range(PIECES)]
    load_tw = pltpu.make_async_copy(tw_hbm, tw, load_sem.at[0])
    load_mats = pltpu.make_async_copy(mats_hbm, mats, load_sem.at[1])
    load_twt = pltpu.make_async_copy(twt_hbm, twt, load_sem.at[2])
    load_holo = pltpu.make_async_copy(holo_hbm, holo, load_sem.at[3])
    load_phases = [
        pltpu.make_async_copy(phase, angles.at[i], load_sem.at[4 + i])
        for i, phase in enumerate((phase_c_hbm, phase_r_hbm))
    ]
    for copy in load_phases + [load_holo] + loads[0] + [load_tw, load_mats] + sum(loads[1:], []) + [load_twt]:
        copy.start()

    barrier = pltpu.get_barrier_semaphore()

    @pl.loop(1, rows)
    def _(k):
        pl.semaphore_signal(barrier, inc=1, device_id=(x, lax.rem(me + k, rows)), device_id_type=MESH)

    pl.semaphore_signal(barrier, inc=1, device_id=(other, me), device_id_type=MESH)

    def remote(src, dst, ss, rs, xd, d):
        return pltpu.make_async_remote_copy(
            src_ref=src, dst_ref=dst, send_sem=ss, recv_sem=rs, device_id=(xd, d), device_id_type=MESH
        )

    def send_rows(snd, rcv, ss, rs, g, h):
        pltpu.make_async_copy(snd.at[g, h, me], rcv.at[g, h, me], rs.at[g, h]).start()

        @pl.loop(1, rows)
        def _(k):
            d = lax.rem(me + k, rows)
            remote(snd.at[g, h, d], rcv.at[g, h, me], ss.at[g, h], rs.at[g, h], x, d).start()

    def wait_whole(ref, sem):
        pltpu.make_async_copy(ref, ref, sem).wait()

    def cols_forward(h):
        @pl.loop(0, 2 * per_half)
        def _(t):
            mode, j = t // per_half, lax.rem(t, per_half)
            at = at_rows(h * half_rows + j * CHUNK)
            values = []
            for n2 in range(RADIX):
                pr, pi = probe[mode, 0, at, lanes_of(n2)].astype(f32), probe[mode, 1, at, lanes_of(n2)].astype(f32)
                tr, ti = trans[0, at, lanes_of(n2)].astype(f32), trans[1, at, lanes_of(n2)].astype(f32)
                er, ei = pr * tr - pi * ti, pr * ti + pi * tr
                values.append((er.astype(bf16).astype(f32), ei.astype(bf16).astype(f32)))
            dst = at_rows(mode * half_rows + j * CHUNK)
            for k2, pair in enumerate(butterfly16(values, -1)):
                re, im = turn_by(pair, tw[0, k2 : k2 + 1, :], -tw[1, k2 : k2 + 1, :])
                uc[k2, dst, 0:LANES] = re.astype(bf16)
                uc[k2, dst, LANES : 2 * LANES] = im.astype(bf16)

        @pl.loop(0, RADIX // GROUP)
        def _(g):
            for k, pair in enumerate(middle_cols(g, 1.0, uc, mats, tw, phc)):
                k2 = g * GROUP + k
                for part, v in enumerate(pair):
                    a, b = v[:half_rows], v[half_rows:]
                    low = jnp.where(lane < LANES // 2, a, pltpu.roll(b, LANES // 2, 1))
                    high = jnp.where(lane < LANES // 2, pltpu.roll(a, LANES // 2, 1), b)
                    uc[k2, 0:half_rows, lanes_of(part)] = low.astype(bf16)
                    uc[k2, half_rows : 2 * half_rows, lanes_of(part)] = high.astype(bf16)

        @pl.loop(0, 2 * per_half)
        def _(t):
            side, j = t // per_half, lax.rem(t, per_half)
            src = at_rows(side * half_rows + j * CHUNK)
            dst = at_rows(j * CHUNK)
            values = [
                (uc[k2, src, 0:LANES].astype(f32), uc[k2, src, LANES : 2 * LANES].astype(f32)) for k2 in range(RADIX)
            ]
            for n2, (re, im) in enumerate(butterfly16(values, 1)):
                snd1[side, h, n2, 0, dst, :] = re.astype(bf16)
                snd1[side, h, n2, 1, dst, :] = im.astype(bf16)

    def cols_back(h):
        def load(side, n2, part, at):
            return rcv2[side, h, n2, part, at, :]

        def store(mode, part, j, n2, value):
            probe[mode, part, at_rows(h * half_rows + j * CHUNK), lanes_of(n2)] = value

        back_piece(load, store, h * half_rows, half_rows, uc, probe, trans, mats, tw, phc)

    def rows_first(load, h):
        @pl.loop(h * per_half, (h + 1) * per_half)
        def _(j):
            at = at_rows(j * CHUNK)
            values = [load(j, n2) for n2 in range(RADIX)]
            for k2, pair in enumerate(butterfly16(values, -1)):
                pick = lanes_of(k2 % 2)
                re, im = turn_by(pair, tables[0, k2 // 2, at, pick], -tables[1, k2 // 2, at, pick])
                ur[k2 // 2, at, pick] = re.astype(bf16)
                ur[k2 // 2, at_rows(LANES + j * CHUNK), pick] = im.astype(bf16)

    def rows_middle(sign):
        @pl.loop(0, RADIX // 2, unroll=2)
        def _(kp):
            y = dot(mats[2], ur[kp])
            re, im = turn_by((y[:LANES], y[LANES:]), tables[2, kp], tables[3, kp] * sign)
            z = dot(mats[3], jnp.concatenate([re.astype(bf16), im.astype(bf16)], axis=0))
            re, im = turn_by((z[:LANES], z[LANES:]), tables[0, kp], tables[1, kp])
            ur[kp, 0:LANES, :] = re.astype(bf16)
            ur[kp, LANES : 2 * LANES, :] = im.astype(bf16)

    def rows_last(store, j):
        at, at_im = at_rows(j * CHUNK), at_rows(LANES + j * CHUNK)
        values = [
            (ur[k2 // 2, at, lanes_of(k2 % 2)].astype(f32), ur[k2 // 2, at_im, lanes_of(k2 % 2)].astype(f32))
            for k2 in range(RADIX)
        ]
        for n2, (re, im) in enumerate(butterfly16(values, 1)):
            store(j, n2, (re * scale).astype(bf16), (im * scale).astype(bf16))

    def own_power(g, n2, at):
        re, im = det[g, n2, 0, at, :].astype(f32), det[g, n2, 1, at, :].astype(f32)
        return re * re + im * im

    def partner(g, j):
        return remote(isnd.at[g, j], ircv.at[g, j], isend.at[g, j], irecv.at[g, j], other, me)

    def rows_forward(g):
        def load(j, n2):
            h, at = j // per_half, at_rows(lax.rem(j, per_half) * CHUNK)
            return rcv1[g, h, n2, 0, at, :].astype(f32), rcv1[g, h, n2, 1, at, :].astype(f32)

        def store(j, n2, re, im):
            det[g, n2, 0, at_rows(j * CHUNK), :] = re
            det[g, n2, 1, at_rows(j * CHUNK), :] = im

        for h in range(PIECES):
            wait_whole(rcv1.at[g, h], recv1.at[g, h])
            rows_first(load, h)
        rows_middle(1.0)

        @pl.loop(0, pairs)
        def _(j):
            rows_last(store, j)
            rows_last(store, j + pairs)
            for n2 in range(RADIX):
                a, b = own_power(g, n2, at_rows(j * CHUNK)), own_power(g, n2, at_rows((j + pairs) * CHUNK))
                first = lane_c < LANES // 2
                total = jnp.where(first, a, b) + pltpu.roll(jnp.where(first, b, a), LANES // 2, 1)
                isnd[g, j, n2] = total.astype(bf16)
            partner(g, j).start()

    def apply_factor(g):
        @pl.loop(0, pairs)
        def _(j):
            wait_whole(ircv.at[g, j], irecv.at[g, j])
            for n2 in range(RADIX):
                total = isnd[g, j, n2].astype(f32) + ircv[g, j, n2].astype(f32)
                measured = hbuf[g, n2, at_rows(j * CHUNK), :].astype(f32)
                factor = 1.0 - jnp.sqrt(measured) * lax.rsqrt(jnp.maximum(total, 1.0))
                swapped = pltpu.roll(factor, LANES // 2, 1)
                first = lane_c < LANES // 2
                for at, f in (
                    (at_rows(j * CHUNK), jnp.where(first, factor, swapped)),
                    (at_rows((j + pairs) * CHUNK), jnp.where(first, swapped, factor)),
                ):
                    for q in range(2):
                        det[g, n2, q, at, :] = (det[g, n2, q, at, :].astype(f32) * f).astype(bf16)

    def rows_back(g):
        def load(j, n2):
            at = at_rows(j * CHUNK)
            return det[g, n2, 0, at, :].astype(f32), det[g, n2, 1, at, :].astype(f32)

        def store(j, n2, re, im):
            h, at = j // per_half, at_rows(lax.rem(j, per_half) * CHUNK)
            snd2[g, h, n2, 0, at, :] = re
            snd2[g, h, n2, 1, at, :] = im

        for h in range(PIECES):
            rows_first(load, h)
        rows_middle(-1.0)
        for h in range(PIECES):
            @pl.loop(h * per_half, (h + 1) * per_half)
            def _(j):
                rows_last(store, j)

            send_rows(snd2, rcv2, send2, recv2, g, h)

    def spectral(natural):
        r = lax.broadcasted_iota(jnp.int32, (rows, LANES), 0)
        c = lax.broadcasted_iota(jnp.int32, (rows, LANES), 1)
        per = LANES // RADIX
        spread = jnp.where(c // per == r, 1.0, 0.0).astype(f32)
        picked = jnp.where(lax.rem(c, RADIX) == r, 1.0, 0.0).astype(f32)
        wide_r = lax.broadcasted_iota(jnp.int32, (LANES, LANES), 0)
        wide_c = lax.broadcasted_iota(jnp.int32, (LANES, LANES), 1)
        exact = lax.Precision.HIGHEST
        full = jnp.dot(natural.T, spread, precision=exact, preferred_element_type=f32)
        full = jnp.where(wide_r // RADIX == lax.rem(wide_c, per), full, 0.0)
        return jnp.dot(picked, full, precision=exact, preferred_element_type=f32)

    load_holo.wait()
    for n2 in range(RADIX):
        upper, lower = holo[0:deep, lanes_of(n2)], holo[deep : 2 * deep, lanes_of(n2)]
        low = jnp.where(lane_h < LANES // 2, upper, pltpu.roll(lower, LANES // 2, 1))
        high = jnp.where(lane_h < LANES // 2, pltpu.roll(upper, LANES // 2, 1), lower)
        hsnd[n2] = jnp.where(x == 0, low, high).astype(bf16)
    for copy in load_phases:
        copy.wait()
    angle = spectral(angles[0])
    for part, turn in enumerate((jnp.cos, jnp.sin)):
        phc[part] = turn(angle) * scale
    pl.semaphore_wait(barrier, rows)
    pltpu.make_async_copy(hsnd.at[me], hbuf.at[x, me], hrecv).start()

    @pl.loop(1, rows)
    def _(k):
        d = lax.rem(me + k, rows)
        remote(hsnd.at[d], hbuf.at[x, me], hsend, hrecv, x, d).start()

    for copy in [load_tw, load_mats]:
        copy.wait()
    for h in range(PIECES):
        for copy in loads[h]:
            copy.wait()
        cols_forward(h)
        send_rows(snd1, rcv1, send1, recv1, 0, h)
    for h in range(PIECES):
        send_rows(snd1, rcv1, send1, recv1, 1, h)

    wait_whole(hbuf.at[x], hrecv)
    forward = remote(hbuf.at[x], hbuf.at[x], xsend, xrecv, other, me)
    forward.start()

    angle = spectral(angles[1])
    for part, turn in enumerate((jnp.cos, jnp.sin)):
        pht[part] = turn(angle).T * scale
    load_twt.wait()
    for k2 in range(RADIX):
        for part in range(2):
            pick = lanes_of(k2 % 2)
            tables[part, k2 // 2, :, pick] = jnp.broadcast_to(twt[part, :, k2 : k2 + 1], (LANES, LANES))
            tables[2 + part, k2 // 2, :, pick] = jnp.broadcast_to(pht[part, :, k2 : k2 + 1], (LANES, LANES))
    wait_whole(hbuf.at[other], xrecv)

    for g in range(HALVES):
        rows_forward(g)
        apply_factor(g)
        rows_back(g)

    for h in range(PIECES):
        for side in range(2):
            wait_whole(rcv2.at[side, h], recv2.at[side, h])
        if h < PIECES - 1:
            cols_back(h)
    keep = pltpu.make_async_copy(rcv2.at[:, PIECES - 1], tail, load_sem.at[0])
    keep.start()

    fewer = pl.ds(0, rows - 1)
    for h in range(PIECES):
        for snd, sem in ((snd1, send1), (snd2, send2)):
            for g in range(2):
                wait_whole(snd.at[g, h, fewer], sem.at[g, h])
    wait_whole(hsnd.at[fewer], hsend)
    forward.wait_send()
    for g in range(2):
        for j in range(pairs):
            partner(g, j).wait_send()
    keep.wait()


def finish_kernel(probe, trans, mats, tw, phc, tail, out, last, uc, sems):
    height = tail.shape[3]
    top = probe.shape[2] - height
    done = pl.ds(0, top)
    early = [
        pltpu.make_async_copy(probe.at[m, :, done], out.at[m, :, done], sems.at[m]) for m in range(probe.shape[0])
    ]
    for copy in early:
        copy.start()

    def load(side, n2, part, at):
        return tail[side, n2, part, at, :]

    def store(mode, part, j, n2, value):
        last[mode, part, at_rows(j * CHUNK), lanes_of(n2)] = value

    back_piece(load, store, top, height, uc, probe, trans, mats, tw, phc)
    late = pltpu.make_async_copy(last, out.at[:, :, pl.ds(top, height)], sems.at[2])
    late.start()
    for copy in early + [late]:
        copy.wait()


def fused_local(probe_modes, transmission, hologram, phase_cols, phase_rows):
    size_a = FACTOR_A
    size_b = probe_modes.shape[3] // size_a
    mats, cosine, sine = constant_tables(size_a, size_b)
    half = size_a // 2
    packed = [np.concatenate([t[:, at : at + half]] * 2, axis=1) for at in (0, half) for t in (cosine, sine)]
    tw = np.stack([cosine, sine] + packed)
    twt = np.stack([cosine.T, sine.T])
    angles = [phase.reshape(size_b, size_a) for phase in (phase_cols, phase_rows)]
    rows = hologram.shape[0]
    field = (2, PIECES, size_b, 2, rows // PIECES, LANES)
    bf16, dma = jnp.bfloat16, pltpu.SemaphoreType.DMA
    vmem, hbm = pl.BlockSpec(memory_space=pltpu.VMEM), pl.BlockSpec(memory_space=pltpu.MemorySpace.HBM)
    shared = (2, rows // HALVES // CHUNK, size_b, CHUNK, LANES)
    piece = rows // PIECES
    large = [probe_modes, transmission, hologram] + [jnp.asarray(table) for table in (mats, tw, twt)] + angles
    large = [pltpu.with_memory_space_constraint(array, pltpu.HBM) for array in large]
    kept = [
        (probe_modes.shape, bf16),
        (transmission.shape, bf16),
        (mats.shape, bf16),
        (tw.shape, jnp.float32),
        ((2, size_b, LANES), jnp.float32),
        ((2, size_b, 2, piece, LANES), bf16),
    ]
    parts = pl.pallas_call(
        fused_kernel,
        out_shape=[pltpu.VMEM(shape, kind) for shape, kind in kept],
        in_specs=[hbm] * len(large),
        out_specs=[vmem] * len(kept),
        scratch_shapes=[
            pltpu.VMEM((2, size_b, size_a), jnp.float32),
            pltpu.VMEM(hologram.shape, jnp.float32),
            pltpu.VMEM(twt.shape, jnp.float32),
            pltpu.VMEM((2, LANES, size_b), jnp.float32),
            pltpu.VMEM(field, bf16),
            pltpu.VMEM(field, bf16),
            pltpu.VMEM(field, bf16),
            pltpu.VMEM(field, bf16),
            pltpu.VMEM((size_b, rows // HALVES, LANES), bf16),
            pltpu.VMEM((2, size_b, rows // HALVES, LANES), bf16),
            pltpu.VMEM(shared, bf16),
            pltpu.VMEM(shared, bf16),
            pltpu.VMEM((size_b, 2 * (rows // PIECES), 2 * LANES), bf16),
            pltpu.VMEM((size_b // 2, 2 * LANES, 2 * LANES), bf16),
            pltpu.VMEM((2, size_b, 2, LANES, LANES), bf16),
            pltpu.VMEM((4, size_b // 2, LANES, 2 * LANES), jnp.float32),
            dma((2, PIECES)),
            dma((2, PIECES)),
            dma((2, PIECES)),
            dma((2, PIECES)),
            dma,
            dma,
            dma,
            dma,
            dma(shared[:2]),
            dma(shared[:2]),
            dma((6,)),
            dma((2, PIECES)),
        ],
        compiler_params=pltpu.CompilerParams(
            collective_id=0, has_side_effects=True, vmem_limit_bytes=LIMIT_MIB * 1024 * 1024
        ),
    )(*large)
    return pl.pallas_call(
        finish_kernel,
        out_shape=jax.ShapeDtypeStruct(probe_modes.shape, bf16),
        in_specs=[vmem] * len(kept),
        out_specs=hbm,
        scratch_shapes=[
            pltpu.VMEM((2, 2, piece, probe_modes.shape[3]), bf16),
            pltpu.VMEM((size_b, 2 * piece, 2 * LANES), bf16),
            dma((3,)),
        ],
        compiler_params=pltpu.CompilerParams(vmem_limit_bytes=FINISH_MIB * 1024 * 1024),
    )(*[pltpu.with_memory_space_constraint(part, pltpu.VMEM) for part in parts])


def chosen(mesh, probe_modes, *others):
    rows, modes = mesh.shape["rows"], mesh.shape["modes"]
    size = probe_modes.shape[3]
    fits = modes == 2 and probe_modes.shape[0] == 2 * modes and size == rows * FACTOR_A == RADIX * LANES
    body = fused_local if fits else local
    return jax.shard_map(
        body,
        mesh=mesh,
        in_specs=(P("modes", None, "rows", None), P(None, "rows", None), P("rows", None), P(), P()),
        out_specs=P("modes", None, "rows", None),
        check_vma=False,
    )(probe_modes, *others)


def solution(mesh):
    return functools.partial(chosen, mesh)
```

```python
import functools
import math

import jax
import jax.numpy as jnp
import numpy as np
from jax import lax
from jax.experimental import pallas as pl
from jax.experimental.pallas import tpu as pltpu
from jax.sharding import PartitionSpec as P

FACTOR_A = 128


def make_block(length, flip):
    indices = jnp.arange(length, dtype=jnp.int32)
    product = indices[:, None] * indices[None, :] % length
    angles = product.astype(jnp.float32) * (2.0 * math.pi / length)
    cosine = jnp.cos(angles)
    sine = flip * jnp.sin(angles)
    matrix = jnp.stack([jnp.stack([cosine, -sine]), jnp.stack([sine, cosine])])
    return matrix.astype(jnp.bfloat16)


def dft_tables(size_b, size_a, inverse):
    flip = 1.0 if inverse else -1.0
    outer = jnp.arange(size_b, dtype=jnp.int32)
    inner = jnp.arange(size_a, dtype=jnp.int32)
    product = outer[:, None] * inner[None, :] % (size_a * size_b)
    angles = product.astype(jnp.float32) * (2.0 * math.pi / (size_a * size_b))
    return (
        make_block(size_b, flip),
        make_block(size_a, flip),
        jnp.cos(angles),
        flip * jnp.sin(angles),
    )


def phase_tables(phase, size_a, size_b):
    ordered = phase.reshape(size_a, size_b).T
    return (jnp.cos(ordered), jnp.sin(ordered))


def rotate_by(values, cosine, sine):
    real_part = values[:, 0]
    imag_part = values[:, 1]
    return jnp.stack(
        [real_part * cosine - imag_part * sine, real_part * sine + imag_part * cosine], axis=1
    )


def transform(values, tables, inverse, layout):
    matrix_b, matrix_a, cosine, sine = tables
    if layout == "cols":
        along_b = "pqkn,mqrna->mprka"
        along_a = "pqkn,mqrbn->mprbk"
    else:
        along_b = "pqkn,mqnas->mpkas"
        along_a = "pqkn,mqbns->mpbks"
        cosine = cosine[:, :, None]
        sine = sine[:, :, None]
    scale = 1.0 / math.sqrt(matrix_a.shape[-1] * matrix_b.shape[-1])
    if inverse:
        middle = jnp.einsum(along_a, matrix_a, values, preferred_element_type=jnp.float32)
        middle = rotate_by(middle, cosine, sine).astype(jnp.bfloat16)
        return jnp.einsum(along_b, matrix_b, middle, preferred_element_type=jnp.float32) * scale
    middle = jnp.einsum(along_b, matrix_b, values, preferred_element_type=jnp.float32)
    middle = rotate_by(middle, cosine, sine).astype(jnp.bfloat16)
    return jnp.einsum(along_a, matrix_a, middle, preferred_element_type=jnp.float32) * scale


def propagate(field, forward_tables, inverse_tables, cosine, sine, layout):
    full_shape = field.shape
    size_b = forward_tables[0].shape[-1]
    size_a = forward_tables[1].shape[-1]
    if layout == "cols":
        split_shape = full_shape[:3] + (size_b, size_a)
        phase_cos, phase_sin = (cosine, sine)
    else:
        split_shape = full_shape[:2] + (size_b, size_a, full_shape[3])
        phase_cos, phase_sin = (cosine[:, :, None], sine[:, :, None])
    spectrum = transform(field.reshape(split_shape), forward_tables, False, layout)
    spectrum = rotate_by(spectrum, phase_cos, phase_sin).astype(jnp.bfloat16)
    return transform(spectrum, inverse_tables, True, layout).reshape(full_shape)


def complex_product(field, transmission):
    field_re = field[:, 0].astype(jnp.float32)
    field_im = field[:, 1].astype(jnp.float32)
    trans_re = transmission[0].astype(jnp.float32)
    trans_im = transmission[1].astype(jnp.float32)
    return jnp.stack(
        [field_re * trans_re - field_im * trans_im, field_re * trans_im + field_im * trans_re],
        axis=1,
    ).astype(jnp.bfloat16)


def apply_step(field, transmission, gradient):
    trans_re = transmission[0].astype(jnp.float32)
    trans_im = transmission[1].astype(jnp.float32)
    grad_re = gradient[:, 0]
    grad_im = gradient[:, 1]
    new_re = field[:, 0].astype(jnp.float32) - (trans_re * grad_re + trans_im * grad_im)
    new_im = field[:, 1].astype(jnp.float32) - (trans_re * grad_im - trans_im * grad_re)
    return jnp.stack([new_re, new_im], axis=1).astype(jnp.bfloat16)


def modulus_factor(detector, measured):
    values = detector.astype(jnp.float32)
    partial_sum = jnp.sum(values * values, axis=(0, 1))
    flattened = partial_sum.reshape(-1)
    measured_flat = measured.reshape(-1)
    summed = lax.psum(flattened.astype(jnp.bfloat16), "modes").astype(jnp.float32)
    factor = 1.0 - jnp.sqrt(measured_flat) / jnp.sqrt(jnp.maximum(summed, 1.0))
    return factor.reshape(partial_sum.shape)


def local(probe_modes, transmission, hologram, phase_cols, phase_rows):
    size_a = FACTOR_A
    size_b = probe_modes.shape[3] // size_a
    forward_tables = dft_tables(size_b, size_a, False)
    inverse_tables = dft_tables(size_b, size_a, True)
    col_cos, col_sin = phase_tables(phase_cols, size_a, size_b)
    row_cos, row_sin = phase_tables(phase_rows, size_a, size_b)
    exit_wave = complex_product(probe_modes, transmission)
    after_cols = propagate(
        exit_wave, forward_tables, inverse_tables, col_cos, col_sin, "cols"
    ).astype(jnp.bfloat16)
    detector_turned = propagate(
        lax.all_to_all(after_cols, "rows", split_axis=3, concat_axis=2, tiled=True),
        forward_tables,
        inverse_tables,
        row_cos,
        row_sin,
        "rows",
    ).astype(jnp.bfloat16)
    measured = lax.all_to_all(
        hologram.astype(jnp.bfloat16), "rows", split_axis=1, concat_axis=0, tiled=True
    ).astype(hologram.dtype)
    factor = modulus_factor(detector_turned, measured)
    residual_wave = (detector_turned.astype(jnp.float32) * factor).astype(jnp.bfloat16)
    back_turned = propagate(
        residual_wave, forward_tables, inverse_tables, row_cos, -row_sin, "rows"
    ).astype(jnp.bfloat16)
    back_rows = lax.all_to_all(back_turned, "rows", split_axis=2, concat_axis=3, tiled=True)
    gradient = propagate(back_rows, forward_tables, inverse_tables, col_cos, -col_sin, "cols")
    return apply_step(probe_modes, transmission, gradient)


MESH = pl.DeviceIdType.MESH
LANES = 128
RADIX = 16
HALVES = 2
PIECES = 4
GROUP = 8
LIMIT_MIB = 40
FINISH_MIB = 12
WORK = jnp.bfloat16
CHUNK = 16


def rounded(value):
    return float(np.asarray(value, np.float32).astype(jnp.bfloat16).astype(np.float32))


def butterfly4(values, sign):
    (r0, i0), (r1, i1), (r2, i2), (r3, i3) = values
    ar, ai, br, bi = r0 + r2, i0 + i2, r0 - r2, i0 - i2
    cr, ci, dr, di = r1 + r3, i1 + i3, r1 - r3, i1 - i3
    low = (br - di, bi + dr)
    high = (br + di, bi - dr)
    first, third = (low, high) if sign > 0 else (high, low)
    return [(ar + cr, ai + ci), first, (ar - cr, ai - ci), third]


def butterfly16(values, sign):
    middle = [[None] * 4 for _ in range(4)]
    for n0 in range(4):
        for k1, (re, im) in enumerate(butterfly4([values[n0 + 4 * n1] for n1 in range(4)], sign)):
            turn = n0 * k1
            if turn == 4:
                re, im = (-im, re) if sign > 0 else (im, -re)
            elif turn:
                c = rounded(math.cos(2.0 * math.pi * turn / RADIX))
                s = sign * rounded(math.sin(2.0 * math.pi * turn / RADIX))
                re, im = re * c - im * s, re * s + im * c
            middle[n0][k1] = (re, im)
    result = [None] * RADIX
    for k1 in range(4):
        for k0, pair in enumerate(butterfly4([middle[n0][k1] for n0 in range(4)], sign)):
            result[k1 + 4 * k0] = pair
    return result


def turn_by(pair, c, s):
    re, im = pair
    return re * c - im * s, re * s + im * c


def constant_tables(size_a, size_b):
    index = np.arange(size_a)
    angle = (index[:, None] * index[None, :] % size_a).astype(np.float32) * np.float32(2.0 * math.pi / size_a)
    c, s = np.cos(angle), np.sin(angle)
    right_f = np.block([[c, -s], [s, c]])
    right_i = np.block([[c, s], [-s, c]])
    mats = np.stack([right_f, right_i, right_f.T, right_i.T]).astype(jnp.bfloat16)
    size = size_a * size_b
    product = np.arange(size_b)[:, None] * index[None, :] % size
    angle = product.astype(np.float32) * np.float32(2.0 * math.pi / size)
    return mats, np.cos(angle).astype(np.float32), np.sin(angle).astype(np.float32)


def at_rows(start):
    return pl.ds(pl.multiple_of(start, CHUNK), CHUNK)


def lanes_of(k):
    return slice(k * LANES, (k + 1) * LANES)


def dot(a, b):
    return jnp.dot(a, b, preferred_element_type=jnp.float32)


def middle_cols(g, sign, uc, mats, tw, phc):
    bf16 = jnp.bfloat16
    scale = 1.0 / math.sqrt(RADIX * LANES)
    depth = uc.shape[1]
    base = pl.multiple_of(g * GROUP, GROUP)
    group = pl.ds(base, GROUP)
    y = dot(uc[group].reshape(GROUP * depth, 2 * LANES), mats[0]).reshape(GROUP, depth, 2 * LANES)
    pc, ps = phc[0, group, :][:, None, :], phc[1, group, :][:, None, :] * sign
    re, im = turn_by((y[:, :, :LANES], y[:, :, LANES:]), pc, ps)
    y = jnp.concatenate([re.astype(bf16), im.astype(bf16)], axis=2).reshape(GROUP * depth, 2 * LANES)
    z = dot(y, mats[1]).reshape(GROUP, depth, 2 * LANES)
    c, s = tw[0, group, :][:, None, :] * scale, tw[1, group, :][:, None, :] * scale
    return [turn_by((z[k, :, :LANES], z[k, :, LANES:]), c[k], s[k]) for k in range(GROUP)]


def back_piece(load, store, top, height, uc, probe, trans, kernels):
    f32, bf16 = jnp.float32, jnp.bfloat16
    chunks = height // CHUNK
    lane = lax.broadcasted_iota(jnp.int32, (height, LANES), 1)

    @pl.loop(0, 2 * chunks)
    def _(t):
        side, j = t // chunks, lax.rem(t, chunks)
        at = at_rows(j * CHUNK)
        values = [(load(side, n2, 0, at).astype(WORK), load(side, n2, 1, at).astype(WORK)) for n2 in range(RADIX)]
        dst = at_rows(side * height + j * CHUNK)
        for k2, (re, im) in enumerate(butterfly16(values, -1)):
            uc[k2, dst, 0:LANES] = re.astype(bf16)
            uc[k2, dst, LANES : 2 * LANES] = im.astype(bf16)

    @pl.loop(0, RADIX, unroll=4)
    def _(k2):
        tops, bottoms = [], []
        for part in range(2):
            low = uc[k2, 0:height, lanes_of(part)].astype(f32)
            high = uc[k2, height : 2 * height, lanes_of(part)].astype(f32)
            tops.append(jnp.where(lane < LANES // 2, low, pltpu.roll(high, LANES // 2, 1)).astype(bf16))
            bottoms.append(jnp.where(lane < LANES // 2, pltpu.roll(low, LANES // 2, 1), high).astype(bf16))
        whole = jnp.concatenate([jnp.concatenate(tops, axis=1), jnp.concatenate(bottoms, axis=1)], axis=0)
        uc[k2] = dot(whole, kernels[k2]).astype(bf16)

    @pl.loop(0, 2 * chunks)
    def _(t):
        mode, j = t // chunks, lax.rem(t, chunks)
        src = at_rows(mode * height + j * CHUNK)
        at = at_rows(top + j * CHUNK)
        values = [
            (uc[k2, src, 0:LANES].astype(WORK), uc[k2, src, LANES : 2 * LANES].astype(WORK)) for k2 in range(RADIX)
        ]
        for n2, (gr, gi) in enumerate(butterfly16(values, 1)):
            gr, gi = gr.astype(f32), gi.astype(f32)
            tr, ti = trans[0, at, lanes_of(n2)].astype(f32), trans[1, at, lanes_of(n2)].astype(f32)
            pr, pi = probe[mode, 0, at, lanes_of(n2)].astype(f32), probe[mode, 1, at, lanes_of(n2)].astype(f32)
            store(mode, 0, j, n2, (pr - (tr * gr + ti * gi)).astype(bf16))
            store(mode, 1, j, n2, (pi - (tr * gi - ti * gr)).astype(bf16))


def fused_kernel(
    probe_hbm, trans_hbm, holo_hbm, mats_hbm, tw_hbm, twt_hbm, phase_c_hbm, phase_r_hbm,
    probe, trans, kc, tail,
    angles, holo, mats, tw, twt, phc, pht, kf, kb, snd1, rcv1, snd2, rcv2, hsnd, hbuf, isnd, ircv, uc, ur, det, tables,
    send1, recv1, send2, recv2, hsend, hrecv, xsend, xrecv, isend, irecv, load_sem, piece_sem,
):
    f32, bf16 = jnp.float32, jnp.bfloat16
    x, me = lax.axis_index("modes"), lax.axis_index("rows")
    other = 1 - x
    rows = RADIX
    half_rows = probe.shape[2] // PIECES
    per_half = half_rows // CHUNK
    deep = probe.shape[2] // HALVES
    scale = 1.0 / math.sqrt(RADIX * LANES)
    pairs = deep // CHUNK
    lane = lax.broadcasted_iota(jnp.int32, (half_rows, LANES), 1)
    lane_h = lax.broadcasted_iota(jnp.int32, (deep, LANES), 1)
    lane_c = lax.broadcasted_iota(jnp.int32, (CHUNK, LANES), 1)

    def piece_loads(h):
        at = pl.ds(h * half_rows, half_rows)
        return [
            pltpu.make_async_copy(probe_hbm.at[:, :, at], probe.at[:, :, at], piece_sem.at[0, h]),
            pltpu.make_async_copy(trans_hbm.at[:, at], trans.at[:, at], piece_sem.at[1, h]),
        ]

    loads = [piece_loads(h) for h in range(PIECES)]
    load_tw = pltpu.make_async_copy(tw_hbm, tw, load_sem.at[0])
    load_mats = pltpu.make_async_copy(mats_hbm, mats, load_sem.at[1])
    load_twt = pltpu.make_async_copy(twt_hbm, twt, load_sem.at[2])
    load_holo = pltpu.make_async_copy(holo_hbm, holo, load_sem.at[3])
    load_phases = [
        pltpu.make_async_copy(phase, angles.at[i], load_sem.at[4 + i])
        for i, phase in enumerate((phase_c_hbm, phase_r_hbm))
    ]
    for copy in load_phases + [load_holo] + loads[0] + [load_tw, load_mats] + sum(loads[1:], []) + [load_twt]:
        copy.start()

    barrier = pltpu.get_barrier_semaphore()

    @pl.loop(1, rows)
    def _(k):
        pl.semaphore_signal(barrier, inc=1, device_id=(x, lax.rem(me + k, rows)), device_id_type=MESH)

    pl.semaphore_signal(barrier, inc=1, device_id=(other, me), device_id_type=MESH)

    def remote(src, dst, ss, rs, xd, d):
        return pltpu.make_async_remote_copy(
            src_ref=src, dst_ref=dst, send_sem=ss, recv_sem=rs, device_id=(xd, d), device_id_type=MESH
        )

    def send_rows(snd, rcv, ss, rs, g, h):
        pltpu.make_async_copy(snd.at[g, h, me], rcv.at[g, h, me], rs.at[g, h]).start()

        @pl.loop(1, rows)
        def _(k):
            d = lax.rem(me + k, rows)
            remote(snd.at[g, h, d], rcv.at[g, h, me], ss.at[g, h], rs.at[g, h], x, d).start()

    def wait_whole(ref, sem):
        pltpu.make_async_copy(ref, ref, sem).wait()

    def cols_forward(h):
        @pl.loop(0, 2 * per_half)
        def _(t):
            mode, j = t // per_half, lax.rem(t, per_half)
            at = at_rows(h * half_rows + j * CHUNK)
            values = []
            for n2 in range(RADIX):
                pr, pi = probe[mode, 0, at, lanes_of(n2)].astype(f32), probe[mode, 1, at, lanes_of(n2)].astype(f32)
                tr, ti = trans[0, at, lanes_of(n2)].astype(f32), trans[1, at, lanes_of(n2)].astype(f32)
                er, ei = pr * tr - pi * ti, pr * ti + pi * tr
                values.append((er.astype(bf16).astype(f32), ei.astype(bf16).astype(f32)))
            dst = at_rows(mode * half_rows + j * CHUNK)
            for k2, pair in enumerate(butterfly16(values, -1)):
                re, im = turn_by(pair, tw[0, k2 : k2 + 1, :], -tw[1, k2 : k2 + 1, :])
                uc[k2, dst, 0:LANES] = re.astype(bf16)
                uc[k2, dst, LANES : 2 * LANES] = im.astype(bf16)

        @pl.loop(0, RADIX // GROUP)
        def _(g):
            for k, pair in enumerate(middle_cols(g, 1.0, uc, mats, tw, phc)):
                k2 = g * GROUP + k
                for part, v in enumerate(pair):
                    a, b = v[:half_rows], v[half_rows:]
                    low = jnp.where(lane < LANES // 2, a, pltpu.roll(b, LANES // 2, 1))
                    high = jnp.where(lane < LANES // 2, pltpu.roll(a, LANES // 2, 1), b)
                    uc[k2, 0:half_rows, lanes_of(part)] = low.astype(bf16)
                    uc[k2, half_rows : 2 * half_rows, lanes_of(part)] = high.astype(bf16)

        @pl.loop(0, 2 * per_half)
        def _(t):
            side, j = t // per_half, lax.rem(t, per_half)
            src = at_rows(side * half_rows + j * CHUNK)
            dst = at_rows(j * CHUNK)
            values = [
                (uc[k2, src, 0:LANES].astype(f32), uc[k2, src, LANES : 2 * LANES].astype(f32)) for k2 in range(RADIX)
            ]
            for n2, (re, im) in enumerate(butterfly16(values, 1)):
                snd1[side, h, n2, 0, dst, :] = re.astype(bf16)
                snd1[side, h, n2, 1, dst, :] = im.astype(bf16)

    def cols_back(h):
        def load(side, n2, part, at):
            return rcv2[side, h, n2, part, at, :]

        def store(mode, part, j, n2, value):
            probe[mode, part, at_rows(h * half_rows + j * CHUNK), lanes_of(n2)] = value

        back_piece(load, store, h * half_rows, half_rows, uc, probe, trans, kc)

    def rows_first(load, h):
        @pl.loop(h * per_half, (h + 1) * per_half)
        def _(j):
            at, at_im = at_rows(j * CHUNK), at_rows(LANES + j * CHUNK)
            values = [load(j, n2) for n2 in range(RADIX)]
            for k2, (re, im) in enumerate(butterfly16(values, -1)):
                ur[k2, at, :] = re.astype(bf16)
                ur[k2, at_im, :] = im.astype(bf16)

    def rows_middle(kernels):
        @pl.loop(0, RADIX, unroll=4)
        def _(k2):
            ur[k2] = dot(kernels[k2], ur[k2]).astype(bf16)

    def rows_last(store, j):
        at, at_im = at_rows(j * CHUNK), at_rows(LANES + j * CHUNK)
        values = [(ur[k2, at, :].astype(WORK), ur[k2, at_im, :].astype(WORK)) for k2 in range(RADIX)]
        for n2, (re, im) in enumerate(butterfly16(values, 1)):
            store(j, n2, re.astype(bf16), im.astype(bf16))

    def set_phase(angle):
        for part, turn in enumerate((jnp.cos, jnp.sin)):
            pht[part] = turn(angle).T * scale
        for k2 in range(RADIX):
            for part in range(2):
                tables[2 + part, k2] = jnp.broadcast_to(pht[part, :, k2 : k2 + 1], (LANES, LANES))

    def build(kernels, sign):
        @pl.loop(0, RADIX)
        def _(k2):
            c, s = mats[2, 0:LANES, 0:LANES].astype(f32), mats[2, 0:LANES, LANES : 2 * LANES].astype(f32)
            re, im = turn_by((c, -s), tables[2, k2], tables[3, k2] * sign)
            re, im = turn_by((re, im), tw[0, pl.ds(k2, 1), :], -tw[1, pl.ds(k2, 1), :])
            z = dot(mats[3], jnp.concatenate([re.astype(bf16), im.astype(bf16)], axis=0))
            re, im = turn_by((z[:LANES], z[LANES:]), tables[0, k2] * scale, tables[1, k2] * scale)
            kernels[k2, 0:LANES, 0:LANES] = re.astype(bf16)
            kernels[k2, LANES : 2 * LANES, 0:LANES] = im.astype(bf16)
            kernels[k2, 0:LANES, LANES : 2 * LANES] = (-im).astype(bf16)
            kernels[k2, LANES : 2 * LANES, LANES : 2 * LANES] = re.astype(bf16)

    def own_power(g, n2, at):
        re, im = det[g, n2, 0, at, :].astype(f32), det[g, n2, 1, at, :].astype(f32)
        return re * re + im * im

    def partner(g, j):
        return remote(isnd.at[g, j], ircv.at[g, j], isend.at[g, j], irecv.at[g, j], other, me)

    def rows_forward(g):
        def load(j, n2):
            h, at = j // per_half, at_rows(lax.rem(j, per_half) * CHUNK)
            return rcv1[g, h, n2, 0, at, :].astype(WORK), rcv1[g, h, n2, 1, at, :].astype(WORK)

        def store(j, n2, re, im):
            det[g, n2, 0, at_rows(j * CHUNK), :] = re
            det[g, n2, 1, at_rows(j * CHUNK), :] = im

        for h in range(PIECES):
            wait_whole(rcv1.at[g, h], recv1.at[g, h])
            rows_first(load, h)
        rows_middle(kf)

        @pl.loop(0, pairs)
        def _(j):
            rows_last(store, j)
            rows_last(store, j + pairs)
            for n2 in range(RADIX):
                a, b = own_power(g, n2, at_rows(j * CHUNK)), own_power(g, n2, at_rows((j + pairs) * CHUNK))
                first = lane_c < LANES // 2
                total = jnp.where(first, a, b) + pltpu.roll(jnp.where(first, b, a), LANES // 2, 1)
                isnd[g, j, n2] = total.astype(bf16)
            partner(g, j).start()

    def apply_factor(g):
        @pl.loop(0, pairs)
        def _(j):
            wait_whole(ircv.at[g, j], irecv.at[g, j])
            for n2 in range(RADIX):
                total = isnd[g, j, n2].astype(f32) + ircv[g, j, n2].astype(f32)
                measured = hbuf[g, n2, at_rows(j * CHUNK), :].astype(f32)
                factor = 1.0 - jnp.sqrt(measured) * lax.rsqrt(jnp.maximum(total, 1.0))
                swapped = pltpu.roll(factor, LANES // 2, 1)
                first = lane_c < LANES // 2
                for at, f in (
                    (at_rows(j * CHUNK), jnp.where(first, factor, swapped)),
                    (at_rows((j + pairs) * CHUNK), jnp.where(first, swapped, factor)),
                ):
                    for q in range(2):
                        det[g, n2, q, at, :] = (det[g, n2, q, at, :].astype(f32) * f).astype(bf16)

    def rows_back(g):
        def load(j, n2):
            at = at_rows(j * CHUNK)
            return det[g, n2, 0, at, :].astype(WORK), det[g, n2, 1, at, :].astype(WORK)

        def store(j, n2, re, im):
            h, at = j // per_half, at_rows(lax.rem(j, per_half) * CHUNK)
            snd2[g, h, n2, 0, at, :] = re
            snd2[g, h, n2, 1, at, :] = im

        for h in range(PIECES):
            rows_first(load, h)
        rows_middle(kb)
        for h in range(PIECES):
            @pl.loop(h * per_half, (h + 1) * per_half)
            def _(j):
                rows_last(store, j)

            send_rows(snd2, rcv2, send2, recv2, g, h)

    def spectral(natural):
        r = lax.broadcasted_iota(jnp.int32, (rows, LANES), 0)
        c = lax.broadcasted_iota(jnp.int32, (rows, LANES), 1)
        per = LANES // RADIX
        spread = jnp.where(c // per == r, 1.0, 0.0).astype(f32)
        picked = jnp.where(lax.rem(c, RADIX) == r, 1.0, 0.0).astype(f32)
        wide_r = lax.broadcasted_iota(jnp.int32, (LANES, LANES), 0)
        wide_c = lax.broadcasted_iota(jnp.int32, (LANES, LANES), 1)
        exact = lax.Precision.HIGHEST
        full = jnp.dot(natural.T, spread, precision=exact, preferred_element_type=f32)
        full = jnp.where(wide_r // RADIX == lax.rem(wide_c, per), full, 0.0)
        return jnp.dot(picked, full, precision=exact, preferred_element_type=f32)

    load_holo.wait()
    for n2 in range(RADIX):
        upper, lower = holo[0:deep, lanes_of(n2)], holo[deep : 2 * deep, lanes_of(n2)]
        low = jnp.where(lane_h < LANES // 2, upper, pltpu.roll(lower, LANES // 2, 1))
        high = jnp.where(lane_h < LANES // 2, pltpu.roll(upper, LANES // 2, 1), lower)
        hsnd[n2] = jnp.where(x == 0, low, high).astype(bf16)
    for copy in load_phases:
        copy.wait()
    angle = spectral(angles[0])
    for part, turn in enumerate((jnp.cos, jnp.sin)):
        phc[part] = turn(angle) * scale
    pl.semaphore_wait(barrier, rows)
    pltpu.make_async_copy(hsnd.at[me], hbuf.at[x, me], hrecv).start()

    @pl.loop(1, rows)
    def _(k):
        d = lax.rem(me + k, rows)
        remote(hsnd.at[d], hbuf.at[x, me], hsend, hrecv, x, d).start()

    for copy in [load_tw, load_mats]:
        copy.wait()
    for h in range(PIECES):
        for copy in loads[h]:
            copy.wait()
        cols_forward(h)
        send_rows(snd1, rcv1, send1, recv1, 0, h)
    for h in range(PIECES):
        send_rows(snd1, rcv1, send1, recv1, 1, h)

    wait_whole(hbuf.at[x], hrecv)
    forward = remote(hbuf.at[x], hbuf.at[x], xsend, xrecv, other, me)
    forward.start()

    load_twt.wait()
    for k2 in range(RADIX):
        for part in range(2):
            tables[part, k2] = jnp.broadcast_to(twt[part, :, k2 : k2 + 1], (LANES, LANES))
    set_phase(spectral(angles[1]))
    build(kf, 1.0)
    build(kb, -1.0)
    set_phase(spectral(angles[0]))
    build(kc, 1.0)
    wait_whole(hbuf.at[other], xrecv)

    for g in range(HALVES):
        rows_forward(g)
        apply_factor(g)
        rows_back(g)

    for h in range(PIECES):
        for side in range(2):
            wait_whole(rcv2.at[side, h], recv2.at[side, h])
        if h < PIECES - 1:
            cols_back(h)
    keep = pltpu.make_async_copy(rcv2.at[:, PIECES - 1], tail, load_sem.at[0])
    keep.start()

    fewer = pl.ds(0, rows - 1)
    for h in range(PIECES):
        for snd, sem in ((snd1, send1), (snd2, send2)):
            for g in range(2):
                wait_whole(snd.at[g, h, fewer], sem.at[g, h])
    wait_whole(hsnd.at[fewer], hsend)
    forward.wait_send()
    for g in range(2):
        for j in range(pairs):
            partner(g, j).wait_send()
    keep.wait()


def finish_kernel(probe, trans, kc, tail, out, last, uc, sems):
    height = tail.shape[3]
    top = probe.shape[2] - height
    done = pl.ds(0, top)
    early = [
        pltpu.make_async_copy(probe.at[m, :, done], out.at[m, :, done], sems.at[m]) for m in range(probe.shape[0])
    ]
    for copy in early:
        copy.start()

    def load(side, n2, part, at):
        return tail[side, n2, part, at, :]

    def store(mode, part, j, n2, value):
        last[mode, part, at_rows(j * CHUNK), lanes_of(n2)] = value

    back_piece(load, store, top, height, uc, probe, trans, kc)
    late = pltpu.make_async_copy(last, out.at[:, :, pl.ds(top, height)], sems.at[2])
    late.start()
    for copy in early + [late]:
        copy.wait()


def fused_local(probe_modes, transmission, hologram, phase_cols, phase_rows):
    size_a = FACTOR_A
    size_b = probe_modes.shape[3] // size_a
    mats, cosine, sine = constant_tables(size_a, size_b)
    tw = np.stack([cosine, sine])
    twt = np.stack([cosine.T, sine.T])
    angles = [phase.reshape(size_b, size_a) for phase in (phase_cols, phase_rows)]
    rows = hologram.shape[0]
    field = (2, PIECES, size_b, 2, rows // PIECES, LANES)
    bf16, dma = jnp.bfloat16, pltpu.SemaphoreType.DMA
    vmem, hbm = pl.BlockSpec(memory_space=pltpu.VMEM), pl.BlockSpec(memory_space=pltpu.MemorySpace.HBM)
    shared = (2, rows // HALVES // CHUNK, size_b, CHUNK, LANES)
    piece = rows // PIECES
    large = [probe_modes, transmission, hologram] + [jnp.asarray(table) for table in (mats, tw, twt)] + angles
    large = [pltpu.with_memory_space_constraint(array, pltpu.HBM) for array in large]
    kept = [
        (probe_modes.shape, bf16),
        (transmission.shape, bf16),
        ((size_b, 2 * LANES, 2 * LANES), bf16),
        ((2, size_b, 2, piece, LANES), bf16),
    ]
    parts = pl.pallas_call(
        fused_kernel,
        out_shape=[pltpu.VMEM(shape, kind) for shape, kind in kept],
        in_specs=[hbm] * len(large),
        out_specs=[vmem] * len(kept),
        scratch_shapes=[
            pltpu.VMEM((2, size_b, size_a), jnp.float32),
            pltpu.VMEM(hologram.shape, jnp.float32),
            pltpu.VMEM(mats.shape, bf16),
            pltpu.VMEM(tw.shape, jnp.float32),
            pltpu.VMEM(twt.shape, jnp.float32),
            pltpu.VMEM((2, size_b, LANES), jnp.float32),
            pltpu.VMEM((2, LANES, size_b), jnp.float32),
            pltpu.VMEM((size_b, 2 * LANES, 2 * LANES), bf16),
            pltpu.VMEM((size_b, 2 * LANES, 2 * LANES), bf16),
            pltpu.VMEM(field, bf16),
            pltpu.VMEM(field, bf16),
            pltpu.VMEM(field, bf16),
            pltpu.VMEM(field, bf16),
            pltpu.VMEM((size_b, rows // HALVES, LANES), bf16),
            pltpu.VMEM((2, size_b, rows // HALVES, LANES), bf16),
            pltpu.VMEM(shared, bf16),
            pltpu.VMEM(shared, bf16),
            pltpu.VMEM((size_b, 2 * (rows // PIECES), 2 * LANES), bf16),
            pltpu.VMEM((size_b, 2 * LANES, LANES), bf16),
            pltpu.VMEM((2, size_b, 2, LANES, LANES), bf16),
            pltpu.VMEM((4, size_b, LANES, LANES), jnp.float32),
            dma((2, PIECES)),
            dma((2, PIECES)),
            dma((2, PIECES)),
            dma((2, PIECES)),
            dma,
            dma,
            dma,
            dma,
            dma(shared[:2]),
            dma(shared[:2]),
            dma((6,)),
            dma((2, PIECES)),
        ],
        compiler_params=pltpu.CompilerParams(
            collective_id=0, has_side_effects=True, vmem_limit_bytes=LIMIT_MIB * 1024 * 1024
        ),
    )(*large)
    return pl.pallas_call(
        finish_kernel,
        out_shape=jax.ShapeDtypeStruct(probe_modes.shape, bf16),
        in_specs=[vmem] * len(kept),
        out_specs=hbm,
        scratch_shapes=[
            pltpu.VMEM((2, 2, piece, probe_modes.shape[3]), bf16),
            pltpu.VMEM((size_b, 2 * piece, 2 * LANES), bf16),
            dma((3,)),
        ],
        compiler_params=pltpu.CompilerParams(vmem_limit_bytes=FINISH_MIB * 1024 * 1024),
    )(*[pltpu.with_memory_space_constraint(part, pltpu.VMEM) for part in parts])


def chosen(mesh, probe_modes, *others):
    rows, modes = mesh.shape["rows"], mesh.shape["modes"]
    size = probe_modes.shape[3]
    fits = modes == 2 and probe_modes.shape[0] == 2 * modes and size == rows * FACTOR_A == RADIX * LANES
    body = fused_local if fits else local
    return jax.shard_map(
        body,
        mesh=mesh,
        in_specs=(P("modes", None, "rows", None), P(None, "rows", None), P("rows", None), P(), P()),
        out_specs=P("modes", None, "rows", None),
        check_vma=False,
    )(probe_modes, *others)


def solution(mesh):
    return functools.partial(chosen, mesh)
```

```python
import functools
import math

import jax
import jax.numpy as jnp
import numpy as np
from jax import lax
from jax.experimental import pallas as pl
from jax.experimental.pallas import tpu as pltpu
from jax.sharding import PartitionSpec as P

FACTOR_A = 128


def make_block(length, flip):
    indices = jnp.arange(length, dtype=jnp.int32)
    product = indices[:, None] * indices[None, :] % length
    angles = product.astype(jnp.float32) * (2.0 * math.pi / length)
    cosine = jnp.cos(angles)
    sine = flip * jnp.sin(angles)
    matrix = jnp.stack([jnp.stack([cosine, -sine]), jnp.stack([sine, cosine])])
    return matrix.astype(jnp.bfloat16)


def dft_tables(size_b, size_a, inverse):
    flip = 1.0 if inverse else -1.0
    outer = jnp.arange(size_b, dtype=jnp.int32)
    inner = jnp.arange(size_a, dtype=jnp.int32)
    product = outer[:, None] * inner[None, :] % (size_a * size_b)
    angles = product.astype(jnp.float32) * (2.0 * math.pi / (size_a * size_b))
    return (
        make_block(size_b, flip),
        make_block(size_a, flip),
        jnp.cos(angles),
        flip * jnp.sin(angles),
    )


def phase_tables(phase, size_a, size_b):
    ordered = phase.reshape(size_a, size_b).T
    return (jnp.cos(ordered), jnp.sin(ordered))


def rotate_by(values, cosine, sine):
    real_part = values[:, 0]
    imag_part = values[:, 1]
    return jnp.stack(
        [real_part * cosine - imag_part * sine, real_part * sine + imag_part * cosine], axis=1
    )


def transform(values, tables, inverse, layout):
    matrix_b, matrix_a, cosine, sine = tables
    if layout == "cols":
        along_b = "pqkn,mqrna->mprka"
        along_a = "pqkn,mqrbn->mprbk"
    else:
        along_b = "pqkn,mqnas->mpkas"
        along_a = "pqkn,mqbns->mpbks"
        cosine = cosine[:, :, None]
        sine = sine[:, :, None]
    scale = 1.0 / math.sqrt(matrix_a.shape[-1] * matrix_b.shape[-1])
    if inverse:
        middle = jnp.einsum(along_a, matrix_a, values, preferred_element_type=jnp.float32)
        middle = rotate_by(middle, cosine, sine).astype(jnp.bfloat16)
        return jnp.einsum(along_b, matrix_b, middle, preferred_element_type=jnp.float32) * scale
    middle = jnp.einsum(along_b, matrix_b, values, preferred_element_type=jnp.float32)
    middle = rotate_by(middle, cosine, sine).astype(jnp.bfloat16)
    return jnp.einsum(along_a, matrix_a, middle, preferred_element_type=jnp.float32) * scale


def propagate(field, forward_tables, inverse_tables, cosine, sine, layout):
    full_shape = field.shape
    size_b = forward_tables[0].shape[-1]
    size_a = forward_tables[1].shape[-1]
    if layout == "cols":
        split_shape = full_shape[:3] + (size_b, size_a)
        phase_cos, phase_sin = (cosine, sine)
    else:
        split_shape = full_shape[:2] + (size_b, size_a, full_shape[3])
        phase_cos, phase_sin = (cosine[:, :, None], sine[:, :, None])
    spectrum = transform(field.reshape(split_shape), forward_tables, False, layout)
    spectrum = rotate_by(spectrum, phase_cos, phase_sin).astype(jnp.bfloat16)
    return transform(spectrum, inverse_tables, True, layout).reshape(full_shape)


def complex_product(field, transmission):
    field_re = field[:, 0].astype(jnp.float32)
    field_im = field[:, 1].astype(jnp.float32)
    trans_re = transmission[0].astype(jnp.float32)
    trans_im = transmission[1].astype(jnp.float32)
    return jnp.stack(
        [field_re * trans_re - field_im * trans_im, field_re * trans_im + field_im * trans_re],
        axis=1,
    ).astype(jnp.bfloat16)


def apply_step(field, transmission, gradient):
    trans_re = transmission[0].astype(jnp.float32)
    trans_im = transmission[1].astype(jnp.float32)
    grad_re = gradient[:, 0]
    grad_im = gradient[:, 1]
    new_re = field[:, 0].astype(jnp.float32) - (trans_re * grad_re + trans_im * grad_im)
    new_im = field[:, 1].astype(jnp.float32) - (trans_re * grad_im - trans_im * grad_re)
    return jnp.stack([new_re, new_im], axis=1).astype(jnp.bfloat16)


def modulus_factor(detector, measured):
    values = detector.astype(jnp.float32)
    partial_sum = jnp.sum(values * values, axis=(0, 1))
    flattened = partial_sum.reshape(-1)
    measured_flat = measured.reshape(-1)
    summed = lax.psum(flattened.astype(jnp.bfloat16), "modes").astype(jnp.float32)
    factor = 1.0 - jnp.sqrt(measured_flat) / jnp.sqrt(jnp.maximum(summed, 1.0))
    return factor.reshape(partial_sum.shape)


def local(probe_modes, transmission, hologram, phase_cols, phase_rows):
    size_a = FACTOR_A
    size_b = probe_modes.shape[3] // size_a
    forward_tables = dft_tables(size_b, size_a, False)
    inverse_tables = dft_tables(size_b, size_a, True)
    col_cos, col_sin = phase_tables(phase_cols, size_a, size_b)
    row_cos, row_sin = phase_tables(phase_rows, size_a, size_b)
    exit_wave = complex_product(probe_modes, transmission)
    after_cols = propagate(
        exit_wave, forward_tables, inverse_tables, col_cos, col_sin, "cols"
    ).astype(jnp.bfloat16)
    detector_turned = propagate(
        lax.all_to_all(after_cols, "rows", split_axis=3, concat_axis=2, tiled=True),
        forward_tables,
        inverse_tables,
        row_cos,
        row_sin,
        "rows",
    ).astype(jnp.bfloat16)
    measured = lax.all_to_all(
        hologram.astype(jnp.bfloat16), "rows", split_axis=1, concat_axis=0, tiled=True
    ).astype(hologram.dtype)
    factor = modulus_factor(detector_turned, measured)
    residual_wave = (detector_turned.astype(jnp.float32) * factor).astype(jnp.bfloat16)
    back_turned = propagate(
        residual_wave, forward_tables, inverse_tables, row_cos, -row_sin, "rows"
    ).astype(jnp.bfloat16)
    back_rows = lax.all_to_all(back_turned, "rows", split_axis=2, concat_axis=3, tiled=True)
    gradient = propagate(back_rows, forward_tables, inverse_tables, col_cos, -col_sin, "cols")
    return apply_step(probe_modes, transmission, gradient)


MESH = pl.DeviceIdType.MESH
LANES = 128
RADIX = 16
HALVES = 2
PIECES = 4
GROUP = 8
LIMIT_MIB = 40
FINISH_MIB = 12
WORK = jnp.bfloat16
CHUNK = 16


def rounded(value):
    return float(np.asarray(value, np.float32).astype(jnp.bfloat16).astype(np.float32))


def butterfly4(values, sign):
    (r0, i0), (r1, i1), (r2, i2), (r3, i3) = values
    ar, ai, br, bi = r0 + r2, i0 + i2, r0 - r2, i0 - i2
    cr, ci, dr, di = r1 + r3, i1 + i3, r1 - r3, i1 - i3
    low = (br - di, bi + dr)
    high = (br + di, bi - dr)
    first, third = (low, high) if sign > 0 else (high, low)
    return [(ar + cr, ai + ci), first, (ar - cr, ai - ci), third]


def butterfly16(values, sign):
    middle = [[None] * 4 for _ in range(4)]
    for n0 in range(4):
        for k1, (re, im) in enumerate(butterfly4([values[n0 + 4 * n1] for n1 in range(4)], sign)):
            turn = n0 * k1
            if turn == 4:
                re, im = (-im, re) if sign > 0 else (im, -re)
            elif turn:
                c = rounded(math.cos(2.0 * math.pi * turn / RADIX))
                s = sign * rounded(math.sin(2.0 * math.pi * turn / RADIX))
                re, im = re * c - im * s, re * s + im * c
            middle[n0][k1] = (re, im)
    result = [None] * RADIX
    for k1 in range(4):
        for k0, pair in enumerate(butterfly4([middle[n0][k1] for n0 in range(4)], sign)):
            result[k1 + 4 * k0] = pair
    return result


def turn_by(pair, c, s):
    re, im = pair
    return re * c - im * s, re * s + im * c


def constant_tables(size_a, size_b):
    index = np.arange(size_a)
    angle = (index[:, None] * index[None, :] % size_a).astype(np.float32) * np.float32(2.0 * math.pi / size_a)
    c, s = np.cos(angle), np.sin(angle)
    right_f = np.block([[c, -s], [s, c]])
    right_i = np.block([[c, s], [-s, c]])
    mats = np.stack([right_f, right_i, right_f.T, right_i.T]).astype(jnp.bfloat16)
    size = size_a * size_b
    product = np.arange(size_b)[:, None] * index[None, :] % size
    angle = product.astype(np.float32) * np.float32(2.0 * math.pi / size)
    return mats, np.cos(angle).astype(np.float32), np.sin(angle).astype(np.float32)


def at_rows(start):
    return pl.ds(pl.multiple_of(start, CHUNK), CHUNK)


def lanes_of(k):
    return slice(k * LANES, (k + 1) * LANES)


def dot(a, b):
    return jnp.dot(a, b, preferred_element_type=jnp.float32)


def middle_cols(g, sign, uc, mats, tw, phc):
    bf16 = jnp.bfloat16
    scale = 1.0 / math.sqrt(RADIX * LANES)
    depth = uc.shape[1]
    base = pl.multiple_of(g * GROUP, GROUP)
    group = pl.ds(base, GROUP)
    y = dot(uc[group].reshape(GROUP * depth, 2 * LANES), mats[0]).reshape(GROUP, depth, 2 * LANES)
    pc, ps = phc[0, group, :][:, None, :], phc[1, group, :][:, None, :] * sign
    re, im = turn_by((y[:, :, :LANES], y[:, :, LANES:]), pc, ps)
    y = jnp.concatenate([re.astype(bf16), im.astype(bf16)], axis=2).reshape(GROUP * depth, 2 * LANES)
    z = dot(y, mats[1]).reshape(GROUP, depth, 2 * LANES)
    c, s = tw[0, group, :][:, None, :] * scale, tw[1, group, :][:, None, :] * scale
    return [turn_by((z[k, :, :LANES], z[k, :, LANES:]), c[k], s[k]) for k in range(GROUP)]


def back_piece(load, store, done, top, height, uc, probe, trans, kernels):
    f32, bf16 = jnp.float32, jnp.bfloat16
    chunks = height // CHUNK
    lane = lax.broadcasted_iota(jnp.int32, (height, LANES), 1)

    @pl.loop(0, 2 * chunks)
    def _(t):
        side, j = t // chunks, lax.rem(t, chunks)
        at = at_rows(j * CHUNK)
        values = [(load(side, n2, 0, at).astype(WORK), load(side, n2, 1, at).astype(WORK)) for n2 in range(RADIX)]
        dst = at_rows(side * height + j * CHUNK)
        for k2, (re, im) in enumerate(butterfly16(values, -1)):
            uc[k2, dst, 0:LANES] = re.astype(bf16)
            uc[k2, dst, LANES : 2 * LANES] = im.astype(bf16)

    for k2 in range(RADIX):
        tops, bottoms = [], []
        for part in range(2):
            low = uc[k2, 0:height, lanes_of(part)].astype(f32)
            high = uc[k2, height : 2 * height, lanes_of(part)].astype(f32)
            tops.append(jnp.where(lane < LANES // 2, low, pltpu.roll(high, LANES // 2, 1)).astype(bf16))
            bottoms.append(jnp.where(lane < LANES // 2, pltpu.roll(low, LANES // 2, 1), high).astype(bf16))
        whole = jnp.concatenate([jnp.concatenate(tops, axis=1), jnp.concatenate(bottoms, axis=1)], axis=0)
        uc[k2] = dot(whole, kernels[k2]).astype(bf16)

    for mode in range(2):

        @pl.loop(0, chunks)
        def _(j):
            src = at_rows(mode * height + j * CHUNK)
            at = at_rows(top + j * CHUNK)
            values = [
                (uc[k2, src, 0:LANES].astype(WORK), uc[k2, src, LANES : 2 * LANES].astype(WORK)) for k2 in range(RADIX)
            ]
            for n2, (gr, gi) in enumerate(butterfly16(values, 1)):
                tr, ti = trans[0, at, lanes_of(n2)].astype(WORK), trans[1, at, lanes_of(n2)].astype(WORK)
                pr, pi = probe[mode, 0, at, lanes_of(n2)].astype(WORK), probe[mode, 1, at, lanes_of(n2)].astype(WORK)
                store(mode, 0, j, n2, (pr - (tr * gr + ti * gi)).astype(bf16))
                store(mode, 1, j, n2, (pi - (tr * gi - ti * gr)).astype(bf16))

        done(mode)


def fused_kernel(
    probe_hbm, trans_hbm, holo_hbm, mats_hbm, tw_hbm, twt_hbm, phase_c_hbm, phase_r_hbm,
    probe, trans, kc, tail,
    angles, holo, mats, tw, twt, phc, pht, kf, kb, snd1, rcv1, snd2, rcv2, hsnd, hbuf, isnd, ircv, uc, ur, det, tables,
    send1, recv1, send2, recv2, hsend, hrecv, xsend, xrecv, isend, irecv, load_sem, piece_sem,
):
    f32, bf16 = jnp.float32, jnp.bfloat16
    x, me = lax.axis_index("modes"), lax.axis_index("rows")
    other = 1 - x
    rows = RADIX
    half_rows = probe.shape[2] // PIECES
    per_half = half_rows // CHUNK
    deep = probe.shape[2] // HALVES
    scale = 1.0 / math.sqrt(RADIX * LANES)
    pairs = deep // CHUNK
    lane = lax.broadcasted_iota(jnp.int32, (half_rows, LANES), 1)
    lane_h = lax.broadcasted_iota(jnp.int32, (deep, LANES), 1)
    lane_c = lax.broadcasted_iota(jnp.int32, (CHUNK, LANES), 1)

    def piece_loads(h):
        at = pl.ds(h * half_rows, half_rows)
        return [
            pltpu.make_async_copy(probe_hbm.at[:, :, at], probe.at[:, :, at], piece_sem.at[0, h]),
            pltpu.make_async_copy(trans_hbm.at[:, at], trans.at[:, at], piece_sem.at[1, h]),
        ]

    loads = [piece_loads(h) for h in range(PIECES)]
    load_tw = pltpu.make_async_copy(tw_hbm, tw, load_sem.at[0])
    load_mats = pltpu.make_async_copy(mats_hbm, mats, load_sem.at[1])
    load_twt = pltpu.make_async_copy(twt_hbm, twt, load_sem.at[2])
    load_holo = pltpu.make_async_copy(holo_hbm, holo, load_sem.at[3])
    load_phases = [
        pltpu.make_async_copy(phase, angles.at[i], load_sem.at[4 + i])
        for i, phase in enumerate((phase_c_hbm, phase_r_hbm))
    ]
    for copy in load_phases + [load_holo] + loads[0] + [load_tw, load_mats] + sum(loads[1:], []) + [load_twt]:
        copy.start()

    barrier = pltpu.get_barrier_semaphore()

    @pl.loop(1, rows)
    def _(k):
        pl.semaphore_signal(barrier, inc=1, device_id=(x, lax.rem(me + k, rows)), device_id_type=MESH)

    pl.semaphore_signal(barrier, inc=1, device_id=(other, me), device_id_type=MESH)

    def remote(src, dst, ss, rs, xd, d):
        return pltpu.make_async_remote_copy(
            src_ref=src, dst_ref=dst, send_sem=ss, recv_sem=rs, device_id=(xd, d), device_id_type=MESH
        )

    def send_rows(snd, rcv, ss, rs, g, h):
        pltpu.make_async_copy(snd.at[g, h, me], rcv.at[g, h, me], rs.at[g, h]).start()

        @pl.loop(1, rows)
        def _(k):
            d = lax.rem(me + k, rows)
            remote(snd.at[g, h, d], rcv.at[g, h, me], ss.at[g, h], rs.at[g, h], x, d).start()

    def wait_whole(ref, sem):
        pltpu.make_async_copy(ref, ref, sem).wait()

    def cols_forward(h):
        @pl.loop(0, 2 * per_half)
        def _(t):
            mode, j = t // per_half, lax.rem(t, per_half)
            at = at_rows(h * half_rows + j * CHUNK)
            values = []
            for n2 in range(RADIX):
                pr, pi = probe[mode, 0, at, lanes_of(n2)].astype(f32), probe[mode, 1, at, lanes_of(n2)].astype(f32)
                tr, ti = trans[0, at, lanes_of(n2)].astype(f32), trans[1, at, lanes_of(n2)].astype(f32)
                er, ei = pr * tr - pi * ti, pr * ti + pi * tr
                values.append((er.astype(bf16).astype(f32), ei.astype(bf16).astype(f32)))
            dst = at_rows(mode * half_rows + j * CHUNK)
            for k2, pair in enumerate(butterfly16(values, -1)):
                re, im = turn_by(pair, tw[0, k2 : k2 + 1, :], -tw[1, k2 : k2 + 1, :])
                uc[k2, dst, 0:LANES] = re.astype(bf16)
                uc[k2, dst, LANES : 2 * LANES] = im.astype(bf16)

        @pl.loop(0, RADIX // GROUP)
        def _(g):
            for k, pair in enumerate(middle_cols(g, 1.0, uc, mats, tw, phc)):
                k2 = g * GROUP + k
                for part, v in enumerate(pair):
                    a, b = v[:half_rows], v[half_rows:]
                    low = jnp.where(lane < LANES // 2, a, pltpu.roll(b, LANES // 2, 1))
                    high = jnp.where(lane < LANES // 2, pltpu.roll(a, LANES // 2, 1), b)
                    uc[k2, 0:half_rows, lanes_of(part)] = low.astype(bf16)
                    uc[k2, half_rows : 2 * half_rows, lanes_of(part)] = high.astype(bf16)

        @pl.loop(0, 2 * per_half)
        def _(t):
            side, j = t // per_half, lax.rem(t, per_half)
            src = at_rows(side * half_rows + j * CHUNK)
            dst = at_rows(j * CHUNK)
            values = [
                (uc[k2, src, 0:LANES].astype(f32), uc[k2, src, LANES : 2 * LANES].astype(f32)) for k2 in range(RADIX)
            ]
            for n2, (re, im) in enumerate(butterfly16(values, 1)):
                snd1[side, h, n2, 0, dst, :] = re.astype(bf16)
                snd1[side, h, n2, 1, dst, :] = im.astype(bf16)

    def cols_back(h):
        def load(side, n2, part, at):
            return rcv2[side, h, n2, part, at, :]

        def store(mode, part, j, n2, value):
            probe[mode, part, at_rows(h * half_rows + j * CHUNK), lanes_of(n2)] = value

        back_piece(load, store, lambda mode: None, h * half_rows, half_rows, uc, probe, trans, kc)

    def rows_first(load, h):
        @pl.loop(h * per_half, (h + 1) * per_half)
        def _(j):
            at, at_im = at_rows(j * CHUNK), at_rows(LANES + j * CHUNK)
            values = [load(j, n2) for n2 in range(RADIX)]
            for k2, (re, im) in enumerate(butterfly16(values, -1)):
                ur[k2, at, :] = re.astype(bf16)
                ur[k2, at_im, :] = im.astype(bf16)

    def rows_middle(kernels):
        for k2 in range(RADIX):
            ur[k2] = dot(kernels[k2], ur[k2]).astype(bf16)

    def rows_last(store, j):
        at, at_im = at_rows(j * CHUNK), at_rows(LANES + j * CHUNK)
        values = [(ur[k2, at, :].astype(WORK), ur[k2, at_im, :].astype(WORK)) for k2 in range(RADIX)]
        for n2, (re, im) in enumerate(butterfly16(values, 1)):
            store(j, n2, re.astype(bf16), im.astype(bf16))

    def set_phase(angle):
        for part, turn in enumerate((jnp.cos, jnp.sin)):
            pht[part] = turn(angle).T * scale
        for k2 in range(RADIX):
            for part in range(2):
                tables[2 + part, k2] = jnp.broadcast_to(pht[part, :, k2 : k2 + 1], (LANES, LANES))

    def build(kernels, sign):
        @pl.loop(0, RADIX)
        def _(k2):
            c, s = mats[2, 0:LANES, 0:LANES].astype(f32), mats[2, 0:LANES, LANES : 2 * LANES].astype(f32)
            re, im = turn_by((c, -s), tables[2, k2], tables[3, k2] * sign)
            re, im = turn_by((re, im), tw[0, pl.ds(k2, 1), :], -tw[1, pl.ds(k2, 1), :])
            z = dot(mats[3], jnp.concatenate([re.astype(bf16), im.astype(bf16)], axis=0))
            re, im = turn_by((z[:LANES], z[LANES:]), tables[0, k2] * scale, tables[1, k2] * scale)
            kernels[k2, 0:LANES, 0:LANES] = re.astype(bf16)
            kernels[k2, LANES : 2 * LANES, 0:LANES] = im.astype(bf16)
            kernels[k2, 0:LANES, LANES : 2 * LANES] = (-im).astype(bf16)
            kernels[k2, LANES : 2 * LANES, LANES : 2 * LANES] = re.astype(bf16)

    def own_power(g, n2, at):
        re, im = det[g, n2, 0, at, :].astype(f32), det[g, n2, 1, at, :].astype(f32)
        return re * re + im * im

    def partner(g, j):
        return remote(isnd.at[g, j], ircv.at[g, j], isend.at[g, j], irecv.at[g, j], other, me)

    def rows_forward(g):
        def load(j, n2):
            h, at = j // per_half, at_rows(lax.rem(j, per_half) * CHUNK)
            return rcv1[g, h, n2, 0, at, :].astype(WORK), rcv1[g, h, n2, 1, at, :].astype(WORK)

        def store(j, n2, re, im):
            det[g, n2, 0, at_rows(j * CHUNK), :] = re
            det[g, n2, 1, at_rows(j * CHUNK), :] = im

        for h in range(PIECES):
            wait_whole(rcv1.at[g, h], recv1.at[g, h])
            rows_first(load, h)
        rows_middle(kf)

        @pl.loop(0, pairs)
        def _(j):
            rows_last(store, j)
            rows_last(store, j + pairs)
            for n2 in range(RADIX):
                a, b = own_power(g, n2, at_rows(j * CHUNK)), own_power(g, n2, at_rows((j + pairs) * CHUNK))
                first = lane_c < LANES // 2
                total = jnp.where(first, a, b) + pltpu.roll(jnp.where(first, b, a), LANES // 2, 1)
                isnd[g, j, n2] = total.astype(bf16)
            partner(g, j).start()

    def apply_factor(g):
        @pl.loop(0, pairs)
        def _(j):
            wait_whole(ircv.at[g, j], irecv.at[g, j])
            for n2 in range(RADIX):
                total = isnd[g, j, n2].astype(f32) + ircv[g, j, n2].astype(f32)
                measured = hbuf[g, n2, at_rows(j * CHUNK), :].astype(f32)
                factor = 1.0 - jnp.sqrt(measured) * lax.rsqrt(jnp.maximum(total, 1.0))
                swapped = pltpu.roll(factor, LANES // 2, 1)
                first = lane_c < LANES // 2
                for at, f in (
                    (at_rows(j * CHUNK), jnp.where(first, factor, swapped)),
                    (at_rows((j + pairs) * CHUNK), jnp.where(first, swapped, factor)),
                ):
                    for q in range(2):
                        det[g, n2, q, at, :] = (det[g, n2, q, at, :].astype(f32) * f).astype(bf16)

    def rows_back(g):
        def load(j, n2):
            at = at_rows(j * CHUNK)
            return det[g, n2, 0, at, :].astype(WORK), det[g, n2, 1, at, :].astype(WORK)

        def store(j, n2, re, im):
            h, at = j // per_half, at_rows(lax.rem(j, per_half) * CHUNK)
            snd2[g, h, n2, 0, at, :] = re
            snd2[g, h, n2, 1, at, :] = im

        for h in range(PIECES):
            rows_first(load, h)
        rows_middle(kb)
        for h in range(PIECES):
            @pl.loop(h * per_half, (h + 1) * per_half)
            def _(j):
                rows_last(store, j)

            send_rows(snd2, rcv2, send2, recv2, g, h)

    def spectral(natural):
        r = lax.broadcasted_iota(jnp.int32, (rows, LANES), 0)
        c = lax.broadcasted_iota(jnp.int32, (rows, LANES), 1)
        per = LANES // RADIX
        spread = jnp.where(c // per == r, 1.0, 0.0).astype(f32)
        picked = jnp.where(lax.rem(c, RADIX) == r, 1.0, 0.0).astype(f32)
        wide_r = lax.broadcasted_iota(jnp.int32, (LANES, LANES), 0)
        wide_c = lax.broadcasted_iota(jnp.int32, (LANES, LANES), 1)
        exact = lax.Precision.HIGHEST
        full = jnp.dot(natural.T, spread, precision=exact, preferred_element_type=f32)
        full = jnp.where(wide_r // RADIX == lax.rem(wide_c, per), full, 0.0)
        return jnp.dot(picked, full, precision=exact, preferred_element_type=f32)

    load_holo.wait()
    for n2 in range(RADIX):
        upper, lower = holo[0:deep, lanes_of(n2)], holo[deep : 2 * deep, lanes_of(n2)]
        low = jnp.where(lane_h < LANES // 2, upper, pltpu.roll(lower, LANES // 2, 1))
        high = jnp.where(lane_h < LANES // 2, pltpu.roll(upper, LANES // 2, 1), lower)
        hsnd[n2] = jnp.where(x == 0, low, high).astype(bf16)
    for copy in load_phases:
        copy.wait()
    angle = spectral(angles[0])
    for part, turn in enumerate((jnp.cos, jnp.sin)):
        phc[part] = turn(angle) * scale
    pl.semaphore_wait(barrier, rows)
    pltpu.make_async_copy(hsnd.at[me], hbuf.at[x, me], hrecv).start()

    @pl.loop(1, rows)
    def _(k):
        d = lax.rem(me + k, rows)
        remote(hsnd.at[d], hbuf.at[x, me], hsend, hrecv, x, d).start()

    for copy in [load_tw, load_mats]:
        copy.wait()
    for h in range(PIECES):
        for copy in loads[h]:
            copy.wait()
        cols_forward(h)
        send_rows(snd1, rcv1, send1, recv1, 0, h)
    for h in range(PIECES):
        send_rows(snd1, rcv1, send1, recv1, 1, h)

    wait_whole(hbuf.at[x], hrecv)
    forward = remote(hbuf.at[x], hbuf.at[x], xsend, xrecv, other, me)
    forward.start()

    load_twt.wait()
    for k2 in range(RADIX):
        for part in range(2):
            tables[part, k2] = jnp.broadcast_to(twt[part, :, k2 : k2 + 1], (LANES, LANES))
    set_phase(spectral(angles[1]))
    build(kf, 1.0)
    build(kb, -1.0)
    set_phase(spectral(angles[0]))
    build(kc, 1.0)
    wait_whole(hbuf.at[other], xrecv)

    for g in range(HALVES):
        rows_forward(g)
        apply_factor(g)
        rows_back(g)

    for h in range(PIECES):
        for side in range(2):
            wait_whole(rcv2.at[side, h], recv2.at[side, h])
        if h < PIECES - 1:
            cols_back(h)
    keep = pltpu.make_async_copy(rcv2.at[:, PIECES - 1], tail, load_sem.at[0])
    keep.start()

    fewer = pl.ds(0, rows - 1)
    for h in range(PIECES):
        for snd, sem in ((snd1, send1), (snd2, send2)):
            for g in range(2):
                wait_whole(snd.at[g, h, fewer], sem.at[g, h])
    wait_whole(hsnd.at[fewer], hsend)
    forward.wait_send()
    for g in range(2):
        for j in range(pairs):
            partner(g, j).wait_send()
    keep.wait()


def finish_kernel(probe, trans, kc, tail, out, last, uc, sems):
    height = tail.shape[3]
    top = probe.shape[2] - height
    done = pl.ds(0, top)
    early = [
        pltpu.make_async_copy(probe.at[m, :, done], out.at[m, :, done], sems.at[m]) for m in range(probe.shape[0])
    ]
    for copy in early:
        copy.start()

    def load(side, n2, part, at):
        return tail[side, n2, part, at, :]

    def store(mode, part, j, n2, value):
        last[mode, part, at_rows(j * CHUNK), lanes_of(n2)] = value

    late = [
        pltpu.make_async_copy(last.at[m], out.at[m, :, pl.ds(top, height)], sems.at[2 + m]) for m in range(probe.shape[0])
    ]
    back_piece(load, store, lambda mode: late[mode].start(), top, height, uc, probe, trans, kc)
    for copy in early + late:
        copy.wait()


def fused_local(probe_modes, transmission, hologram, phase_cols, phase_rows):
    size_a = FACTOR_A
    size_b = probe_modes.shape[3] // size_a
    mats, cosine, sine = constant_tables(size_a, size_b)
    tw = np.stack([cosine, sine])
    twt = np.stack([cosine.T, sine.T])
    angles = [phase.reshape(size_b, size_a) for phase in (phase_cols, phase_rows)]
    rows = hologram.shape[0]
    field = (2, PIECES, size_b, 2, rows // PIECES, LANES)
    bf16, dma = jnp.bfloat16, pltpu.SemaphoreType.DMA
    vmem, hbm = pl.BlockSpec(memory_space=pltpu.VMEM), pl.BlockSpec(memory_space=pltpu.MemorySpace.HBM)
    shared = (2, rows // HALVES // CHUNK, size_b, CHUNK, LANES)
    piece = rows // PIECES
    large = [probe_modes, transmission, hologram] + [jnp.asarray(table) for table in (mats, tw, twt)] + angles
    large = [pltpu.with_memory_space_constraint(array, pltpu.HBM) for array in large]
    kept = [
        (probe_modes.shape, bf16),
        (transmission.shape, bf16),
        ((size_b, 2 * LANES, 2 * LANES), bf16),
        ((2, size_b, 2, piece, LANES), bf16),
    ]
    parts = pl.pallas_call(
        fused_kernel,
        out_shape=[pltpu.VMEM(shape, kind) for shape, kind in kept],
        in_specs=[hbm] * len(large),
        out_specs=[vmem] * len(kept),
        scratch_shapes=[
            pltpu.VMEM((2, size_b, size_a), jnp.float32),
            pltpu.VMEM(hologram.shape, jnp.float32),
            pltpu.VMEM(mats.shape, bf16),
            pltpu.VMEM(tw.shape, jnp.float32),
            pltpu.VMEM(twt.shape, jnp.float32),
            pltpu.VMEM((2, size_b, LANES), jnp.float32),
            pltpu.VMEM((2, LANES, size_b), jnp.float32),
            pltpu.VMEM((size_b, 2 * LANES, 2 * LANES), bf16),
            pltpu.VMEM((size_b, 2 * LANES, 2 * LANES), bf16),
            pltpu.VMEM(field, bf16),
            pltpu.VMEM(field, bf16),
            pltpu.VMEM(field, bf16),
            pltpu.VMEM(field, bf16),
            pltpu.VMEM((size_b, rows // HALVES, LANES), bf16),
            pltpu.VMEM((2, size_b, rows // HALVES, LANES), bf16),
            pltpu.VMEM(shared, bf16),
            pltpu.VMEM(shared, bf16),
            pltpu.VMEM((size_b, 2 * (rows // PIECES), 2 * LANES), bf16),
            pltpu.VMEM((size_b, 2 * LANES, LANES), bf16),
            pltpu.VMEM((2, size_b, 2, LANES, LANES), bf16),
            pltpu.VMEM((4, size_b, LANES, LANES), jnp.float32),
            dma((2, PIECES)),
            dma((2, PIECES)),
            dma((2, PIECES)),
            dma((2, PIECES)),
            dma,
            dma,
            dma,
            dma,
            dma(shared[:2]),
            dma(shared[:2]),
            dma((6,)),
            dma((2, PIECES)),
        ],
        compiler_params=pltpu.CompilerParams(
            collective_id=0, has_side_effects=True, vmem_limit_bytes=LIMIT_MIB * 1024 * 1024
        ),
    )(*large)
    return pl.pallas_call(
        finish_kernel,
        out_shape=jax.ShapeDtypeStruct(probe_modes.shape, bf16),
        in_specs=[vmem] * len(kept),
        out_specs=hbm,
        scratch_shapes=[
            pltpu.VMEM((2, 2, piece, probe_modes.shape[3]), bf16),
            pltpu.VMEM((size_b, 2 * piece, 2 * LANES), bf16),
            dma((4,)),
        ],
        compiler_params=pltpu.CompilerParams(vmem_limit_bytes=FINISH_MIB * 1024 * 1024),
    )(*[pltpu.with_memory_space_constraint(part, pltpu.VMEM) for part in parts])


def chosen(mesh, probe_modes, *others):
    rows, modes = mesh.shape["rows"], mesh.shape["modes"]
    size = probe_modes.shape[3]
    fits = modes == 2 and probe_modes.shape[0] == 2 * modes and size == rows * FACTOR_A == RADIX * LANES
    body = fused_local if fits else local
    return jax.shard_map(
        body,
        mesh=mesh,
        in_specs=(P("modes", None, "rows", None), P(None, "rows", None), P("rows", None), P(), P()),
        out_specs=P("modes", None, "rows", None),
        check_vma=False,
    )(probe_modes, *others)


def solution(mesh):
    return functools.partial(chosen, mesh)
```

```python
import functools
import math

import jax
import jax.numpy as jnp
import numpy as np
from jax import lax
from jax.experimental import pallas as pl
from jax.experimental.pallas import tpu as pltpu
from jax.sharding import PartitionSpec as P

FACTOR_A = 128


def make_block(length, flip):
    indices = jnp.arange(length, dtype=jnp.int32)
    product = indices[:, None] * indices[None, :] % length
    angles = product.astype(jnp.float32) * (2.0 * math.pi / length)
    cosine = jnp.cos(angles)
    sine = flip * jnp.sin(angles)
    matrix = jnp.stack([jnp.stack([cosine, -sine]), jnp.stack([sine, cosine])])
    return matrix.astype(jnp.bfloat16)


def dft_tables(size_b, size_a, inverse):
    flip = 1.0 if inverse else -1.0
    outer = jnp.arange(size_b, dtype=jnp.int32)
    inner = jnp.arange(size_a, dtype=jnp.int32)
    product = outer[:, None] * inner[None, :] % (size_a * size_b)
    angles = product.astype(jnp.float32) * (2.0 * math.pi / (size_a * size_b))
    return (
        make_block(size_b, flip),
        make_block(size_a, flip),
        jnp.cos(angles),
        flip * jnp.sin(angles),
    )


def phase_tables(phase, size_a, size_b):
    ordered = phase.reshape(size_a, size_b).T
    return (jnp.cos(ordered), jnp.sin(ordered))


def rotate_by(values, cosine, sine):
    real_part = values[:, 0]
    imag_part = values[:, 1]
    return jnp.stack(
        [real_part * cosine - imag_part * sine, real_part * sine + imag_part * cosine], axis=1
    )


def transform(values, tables, inverse, layout):
    matrix_b, matrix_a, cosine, sine = tables
    if layout == "cols":
        along_b = "pqkn,mqrna->mprka"
        along_a = "pqkn,mqrbn->mprbk"
    else:
        along_b = "pqkn,mqnas->mpkas"
        along_a = "pqkn,mqbns->mpbks"
        cosine = cosine[:, :, None]
        sine = sine[:, :, None]
    scale = 1.0 / math.sqrt(matrix_a.shape[-1] * matrix_b.shape[-1])
    if inverse:
        middle = jnp.einsum(along_a, matrix_a, values, preferred_element_type=jnp.float32)
        middle = rotate_by(middle, cosine, sine).astype(jnp.bfloat16)
        return jnp.einsum(along_b, matrix_b, middle, preferred_element_type=jnp.float32) * scale
    middle = jnp.einsum(along_b, matrix_b, values, preferred_element_type=jnp.float32)
    middle = rotate_by(middle, cosine, sine).astype(jnp.bfloat16)
    return jnp.einsum(along_a, matrix_a, middle, preferred_element_type=jnp.float32) * scale


def propagate(field, forward_tables, inverse_tables, cosine, sine, layout):
    full_shape = field.shape
    size_b = forward_tables[0].shape[-1]
    size_a = forward_tables[1].shape[-1]
    if layout == "cols":
        split_shape = full_shape[:3] + (size_b, size_a)
        phase_cos, phase_sin = (cosine, sine)
    else:
        split_shape = full_shape[:2] + (size_b, size_a, full_shape[3])
        phase_cos, phase_sin = (cosine[:, :, None], sine[:, :, None])
    spectrum = transform(field.reshape(split_shape), forward_tables, False, layout)
    spectrum = rotate_by(spectrum, phase_cos, phase_sin).astype(jnp.bfloat16)
    return transform(spectrum, inverse_tables, True, layout).reshape(full_shape)


def complex_product(field, transmission):
    field_re = field[:, 0].astype(jnp.float32)
    field_im = field[:, 1].astype(jnp.float32)
    trans_re = transmission[0].astype(jnp.float32)
    trans_im = transmission[1].astype(jnp.float32)
    return jnp.stack(
        [field_re * trans_re - field_im * trans_im, field_re * trans_im + field_im * trans_re],
        axis=1,
    ).astype(jnp.bfloat16)


def apply_step(field, transmission, gradient):
    trans_re = transmission[0].astype(jnp.float32)
    trans_im = transmission[1].astype(jnp.float32)
    grad_re = gradient[:, 0]
    grad_im = gradient[:, 1]
    new_re = field[:, 0].astype(jnp.float32) - (trans_re * grad_re + trans_im * grad_im)
    new_im = field[:, 1].astype(jnp.float32) - (trans_re * grad_im - trans_im * grad_re)
    return jnp.stack([new_re, new_im], axis=1).astype(jnp.bfloat16)


def modulus_factor(detector, measured):
    values = detector.astype(jnp.float32)
    partial_sum = jnp.sum(values * values, axis=(0, 1))
    flattened = partial_sum.reshape(-1)
    measured_flat = measured.reshape(-1)
    summed = lax.psum(flattened.astype(jnp.bfloat16), "modes").astype(jnp.float32)
    factor = 1.0 - jnp.sqrt(measured_flat) / jnp.sqrt(jnp.maximum(summed, 1.0))
    return factor.reshape(partial_sum.shape)


def local(probe_modes, transmission, hologram, phase_cols, phase_rows):
    size_a = FACTOR_A
    size_b = probe_modes.shape[3] // size_a
    forward_tables = dft_tables(size_b, size_a, False)
    inverse_tables = dft_tables(size_b, size_a, True)
    col_cos, col_sin = phase_tables(phase_cols, size_a, size_b)
    row_cos, row_sin = phase_tables(phase_rows, size_a, size_b)
    exit_wave = complex_product(probe_modes, transmission)
    after_cols = propagate(
        exit_wave, forward_tables, inverse_tables, col_cos, col_sin, "cols"
    ).astype(jnp.bfloat16)
    detector_turned = propagate(
        lax.all_to_all(after_cols, "rows", split_axis=3, concat_axis=2, tiled=True),
        forward_tables,
        inverse_tables,
        row_cos,
        row_sin,
        "rows",
    ).astype(jnp.bfloat16)
    measured = lax.all_to_all(
        hologram.astype(jnp.bfloat16), "rows", split_axis=1, concat_axis=0, tiled=True
    ).astype(hologram.dtype)
    factor = modulus_factor(detector_turned, measured)
    residual_wave = (detector_turned.astype(jnp.float32) * factor).astype(jnp.bfloat16)
    back_turned = propagate(
        residual_wave, forward_tables, inverse_tables, row_cos, -row_sin, "rows"
    ).astype(jnp.bfloat16)
    back_rows = lax.all_to_all(back_turned, "rows", split_axis=2, concat_axis=3, tiled=True)
    gradient = propagate(back_rows, forward_tables, inverse_tables, col_cos, -col_sin, "cols")
    return apply_step(probe_modes, transmission, gradient)


MESH = pl.DeviceIdType.MESH
LANES = 128
RADIX = 16
HALVES = 2
PIECES = 4
GROUP = 8
LIMIT_MIB = 40
FINISH_MIB = 12
WORK = jnp.bfloat16
CHUNK = 16


def rounded(value):
    return float(np.asarray(value, np.float32).astype(jnp.bfloat16).astype(np.float32))


def butterfly4(values, sign):
    (r0, i0), (r1, i1), (r2, i2), (r3, i3) = values
    ar, ai, br, bi = r0 + r2, i0 + i2, r0 - r2, i0 - i2
    cr, ci, dr, di = r1 + r3, i1 + i3, r1 - r3, i1 - i3
    low = (br - di, bi + dr)
    high = (br + di, bi - dr)
    first, third = (low, high) if sign > 0 else (high, low)
    return [(ar + cr, ai + ci), first, (ar - cr, ai - ci), third]


def butterfly16(values, sign):
    middle = [[None] * 4 for _ in range(4)]
    for n0 in range(4):
        for k1, (re, im) in enumerate(butterfly4([values[n0 + 4 * n1] for n1 in range(4)], sign)):
            turn = n0 * k1
            if turn == 4:
                re, im = (-im, re) if sign > 0 else (im, -re)
            elif turn:
                c = rounded(math.cos(2.0 * math.pi * turn / RADIX))
                s = sign * rounded(math.sin(2.0 * math.pi * turn / RADIX))
                re, im = re * c - im * s, re * s + im * c
            middle[n0][k1] = (re, im)
    result = [None] * RADIX
    for k1 in range(4):
        for k0, pair in enumerate(butterfly4([middle[n0][k1] for n0 in range(4)], sign)):
            result[k1 + 4 * k0] = pair
    return result


def turn_by(pair, c, s):
    re, im = pair
    return re * c - im * s, re * s + im * c


def constant_tables(size_a, size_b):
    index = np.arange(size_a)
    angle = (index[:, None] * index[None, :] % size_a).astype(np.float32) * np.float32(2.0 * math.pi / size_a)
    c, s = np.cos(angle), np.sin(angle)
    right_f = np.block([[c, -s], [s, c]])
    right_i = np.block([[c, s], [-s, c]])
    mats = np.stack([right_f, right_i, right_f.T, right_i.T]).astype(jnp.bfloat16)
    size = size_a * size_b
    product = np.arange(size_b)[:, None] * index[None, :] % size
    angle = product.astype(np.float32) * np.float32(2.0 * math.pi / size)
    return mats, np.cos(angle).astype(np.float32), np.sin(angle).astype(np.float32)


def at_rows(start):
    return pl.ds(pl.multiple_of(start, CHUNK), CHUNK)


def lanes_of(k):
    return slice(k * LANES, (k + 1) * LANES)


def dot(a, b):
    return jnp.dot(a, b, preferred_element_type=jnp.float32)


def middle_cols(g, sign, uc, mats, tw, phc):
    bf16 = jnp.bfloat16
    scale = 1.0 / math.sqrt(RADIX * LANES)
    depth = uc.shape[1]
    base = pl.multiple_of(g * GROUP, GROUP)
    group = pl.ds(base, GROUP)
    y = dot(uc[group].reshape(GROUP * depth, 2 * LANES), mats[0]).reshape(GROUP, depth, 2 * LANES)
    pc, ps = phc[0, group, :][:, None, :], phc[1, group, :][:, None, :] * sign
    re, im = turn_by((y[:, :, :LANES], y[:, :, LANES:]), pc, ps)
    y = jnp.concatenate([re.astype(bf16), im.astype(bf16)], axis=2).reshape(GROUP * depth, 2 * LANES)
    z = dot(y, mats[1]).reshape(GROUP, depth, 2 * LANES)
    c, s = tw[0, group, :][:, None, :] * scale, tw[1, group, :][:, None, :] * scale
    return [turn_by((z[k, :, :LANES], z[k, :, LANES:]), c[k], s[k]) for k in range(GROUP)]


def back_piece(load, store, done, top, height, uc, probe, trans, kernels):
    f32, bf16 = jnp.float32, jnp.bfloat16
    chunks = height // CHUNK
    lane = lax.broadcasted_iota(jnp.int32, (height, LANES), 1)

    @pl.loop(0, 2 * chunks)
    def _(t):
        side, j = t // chunks, lax.rem(t, chunks)
        at = at_rows(j * CHUNK)
        values = [(load(side, n2, 0, at).astype(WORK), load(side, n2, 1, at).astype(WORK)) for n2 in range(RADIX)]
        dst = at_rows(side * height + j * CHUNK)
        for k2, (re, im) in enumerate(butterfly16(values, -1)):
            uc[k2, dst, 0:LANES] = re.astype(bf16)
            uc[k2, dst, LANES : 2 * LANES] = im.astype(bf16)

    for k2 in range(RADIX):
        tops, bottoms = [], []
        for part in range(2):
            low = uc[k2, 0:height, lanes_of(part)].astype(f32)
            high = uc[k2, height : 2 * height, lanes_of(part)].astype(f32)
            tops.append(jnp.where(lane < LANES // 2, low, pltpu.roll(high, LANES // 2, 1)).astype(bf16))
            bottoms.append(jnp.where(lane < LANES // 2, pltpu.roll(low, LANES // 2, 1), high).astype(bf16))
        whole = jnp.concatenate([jnp.concatenate(tops, axis=1), jnp.concatenate(bottoms, axis=1)], axis=0)
        uc[k2] = dot(whole, kernels[k2]).astype(bf16)

    for mode in range(2):

        @pl.loop(0, chunks)
        def _(j):
            src = at_rows(mode * height + j * CHUNK)
            at = at_rows(top + j * CHUNK)
            values = [
                (uc[k2, src, 0:LANES].astype(WORK), uc[k2, src, LANES : 2 * LANES].astype(WORK)) for k2 in range(RADIX)
            ]
            for n2, (gr, gi) in enumerate(butterfly16(values, 1)):
                tr, ti = trans[0, at, lanes_of(n2)].astype(WORK), trans[1, at, lanes_of(n2)].astype(WORK)
                pr, pi = probe[mode, 0, at, lanes_of(n2)].astype(WORK), probe[mode, 1, at, lanes_of(n2)].astype(WORK)
                store(mode, 0, j, n2, (pr - (tr * gr + ti * gi)).astype(bf16))
                store(mode, 1, j, n2, (pi - (tr * gi - ti * gr)).astype(bf16))

        done(mode)


def fused_kernel(
    probe_hbm, trans_hbm, holo_hbm, mats_hbm, tw_hbm, twt_hbm, phase_c_hbm, phase_r_hbm,
    probe, trans, kc, tail,
    angles, holo, mats, tw, twt, phc, pht, kf, kb, snd1, rcv1, snd2, rcv2, hsnd, hbuf, isnd, ircv, uc, ur, det, tables,
    send1, recv1, send2, recv2, hsend, hrecv, xsend, xrecv, isend, irecv, load_sem, piece_sem,
):
    f32, bf16 = jnp.float32, jnp.bfloat16
    x, me = lax.axis_index("modes"), lax.axis_index("rows")
    other = 1 - x
    rows = RADIX
    half_rows = probe.shape[2] // PIECES
    per_half = half_rows // CHUNK
    deep = probe.shape[2] // HALVES
    scale = 1.0 / math.sqrt(RADIX * LANES)
    pairs = deep // CHUNK
    lane = lax.broadcasted_iota(jnp.int32, (half_rows, LANES), 1)
    lane_h = lax.broadcasted_iota(jnp.int32, (deep, LANES), 1)
    lane_c = lax.broadcasted_iota(jnp.int32, (CHUNK, LANES), 1)

    def piece_loads(h):
        at = pl.ds(h * half_rows, half_rows)
        return [
            pltpu.make_async_copy(probe_hbm.at[:, :, at], probe.at[:, :, at], piece_sem.at[0, h]),
            pltpu.make_async_copy(trans_hbm.at[:, at], trans.at[:, at], piece_sem.at[1, h]),
        ]

    loads = [piece_loads(h) for h in range(PIECES)]
    load_tw = pltpu.make_async_copy(tw_hbm, tw, load_sem.at[0])
    load_mats = pltpu.make_async_copy(mats_hbm, mats, load_sem.at[1])
    load_twt = pltpu.make_async_copy(twt_hbm, twt, load_sem.at[2])
    load_holo = pltpu.make_async_copy(holo_hbm, holo, load_sem.at[3])
    barrier = pltpu.get_barrier_semaphore()

    @pl.loop(1, rows)
    def _(k):
        pl.semaphore_signal(barrier, inc=1, device_id=(x, lax.rem(me + k, rows)), device_id_type=MESH)

    pl.semaphore_signal(barrier, inc=1, device_id=(other, me), device_id_type=MESH)
    load_phases = [
        pltpu.make_async_copy(phase, angles.at[i], load_sem.at[4 + i])
        for i, phase in enumerate((phase_c_hbm, phase_r_hbm))
    ]
    for copy in [load_holo] + load_phases + loads[0] + [load_tw, load_mats] + sum(loads[1:], []) + [load_twt]:
        copy.start()


    def remote(src, dst, ss, rs, xd, d):
        return pltpu.make_async_remote_copy(
            src_ref=src, dst_ref=dst, send_sem=ss, recv_sem=rs, device_id=(xd, d), device_id_type=MESH
        )

    def send_rows(snd, rcv, ss, rs, g, h):
        pltpu.make_async_copy(snd.at[g, h, me], rcv.at[g, h, me], rs.at[g, h]).start()

        @pl.loop(1, rows)
        def _(k):
            d = lax.rem(me + k, rows)
            remote(snd.at[g, h, d], rcv.at[g, h, me], ss.at[g, h], rs.at[g, h], x, d).start()

    def wait_whole(ref, sem):
        pltpu.make_async_copy(ref, ref, sem).wait()

    def cols_forward(h):
        @pl.loop(0, 2 * per_half)
        def _(t):
            mode, j = t // per_half, lax.rem(t, per_half)
            at = at_rows(h * half_rows + j * CHUNK)
            values = []
            for n2 in range(RADIX):
                pr, pi = probe[mode, 0, at, lanes_of(n2)].astype(f32), probe[mode, 1, at, lanes_of(n2)].astype(f32)
                tr, ti = trans[0, at, lanes_of(n2)].astype(f32), trans[1, at, lanes_of(n2)].astype(f32)
                er, ei = pr * tr - pi * ti, pr * ti + pi * tr
                values.append((er.astype(bf16).astype(f32), ei.astype(bf16).astype(f32)))
            dst = at_rows(mode * half_rows + j * CHUNK)
            for k2, pair in enumerate(butterfly16(values, -1)):
                re, im = turn_by(pair, tw[0, k2 : k2 + 1, :], -tw[1, k2 : k2 + 1, :])
                uc[k2, dst, 0:LANES] = re.astype(bf16)
                uc[k2, dst, LANES : 2 * LANES] = im.astype(bf16)

        @pl.loop(0, RADIX // GROUP)
        def _(g):
            for k, pair in enumerate(middle_cols(g, 1.0, uc, mats, tw, phc)):
                k2 = g * GROUP + k
                for part, v in enumerate(pair):
                    a, b = v[:half_rows], v[half_rows:]
                    low = jnp.where(lane < LANES // 2, a, pltpu.roll(b, LANES // 2, 1))
                    high = jnp.where(lane < LANES // 2, pltpu.roll(a, LANES // 2, 1), b)
                    uc[k2, 0:half_rows, lanes_of(part)] = low.astype(bf16)
                    uc[k2, half_rows : 2 * half_rows, lanes_of(part)] = high.astype(bf16)

        @pl.loop(0, 2 * per_half)
        def _(t):
            side, j = t // per_half, lax.rem(t, per_half)
            src = at_rows(side * half_rows + j * CHUNK)
            dst = at_rows(j * CHUNK)
            values = [
                (uc[k2, src, 0:LANES].astype(f32), uc[k2, src, LANES : 2 * LANES].astype(f32)) for k2 in range(RADIX)
            ]
            for n2, (re, im) in enumerate(butterfly16(values, 1)):
                snd1[side, h, n2, 0, dst, :] = re.astype(bf16)
                snd1[side, h, n2, 1, dst, :] = im.astype(bf16)

    def cols_back(h):
        def load(side, n2, part, at):
            return rcv2[side, h, n2, part, at, :]

        def store(mode, part, j, n2, value):
            probe[mode, part, at_rows(h * half_rows + j * CHUNK), lanes_of(n2)] = value

        back_piece(load, store, lambda mode: None, h * half_rows, half_rows, uc, probe, trans, kc)

    def rows_first(load, h):
        @pl.loop(h * per_half, (h + 1) * per_half)
        def _(j):
            at, at_im = at_rows(j * CHUNK), at_rows(LANES + j * CHUNK)
            values = [load(j, n2) for n2 in range(RADIX)]
            for k2, (re, im) in enumerate(butterfly16(values, -1)):
                ur[k2, at, :] = re.astype(bf16)
                ur[k2, at_im, :] = im.astype(bf16)

    def rows_middle(kernels):
        for k2 in range(RADIX):
            ur[k2] = dot(kernels[k2], ur[k2]).astype(bf16)

    def rows_last(store, j):
        at, at_im = at_rows(j * CHUNK), at_rows(LANES + j * CHUNK)
        values = [(ur[k2, at, :].astype(WORK), ur[k2, at_im, :].astype(WORK)) for k2 in range(RADIX)]
        for n2, (re, im) in enumerate(butterfly16(values, 1)):
            store(j, n2, re.astype(bf16), im.astype(bf16))

    def set_phase(angle):
        for part, turn in enumerate((jnp.cos, jnp.sin)):
            pht[part] = turn(angle).T * scale
        for k2 in range(RADIX):
            for part in range(2):
                tables[2 + part, k2] = jnp.broadcast_to(pht[part, :, k2 : k2 + 1], (LANES, LANES))

    def build(kernels, sign):
        @pl.loop(0, RADIX)
        def _(k2):
            c, s = mats[2, 0:LANES, 0:LANES].astype(f32), mats[2, 0:LANES, LANES : 2 * LANES].astype(f32)
            re, im = turn_by((c, -s), tables[2, k2], tables[3, k2] * sign)
            re, im = turn_by((re, im), tw[0, pl.ds(k2, 1), :], -tw[1, pl.ds(k2, 1), :])
            z = dot(mats[3], jnp.concatenate([re.astype(bf16), im.astype(bf16)], axis=0))
            re, im = turn_by((z[:LANES], z[LANES:]), tables[0, k2] * scale, tables[1, k2] * scale)
            kernels[k2, 0:LANES, 0:LANES] = re.astype(bf16)
            kernels[k2, LANES : 2 * LANES, 0:LANES] = im.astype(bf16)
            kernels[k2, 0:LANES, LANES : 2 * LANES] = (-im).astype(bf16)
            kernels[k2, LANES : 2 * LANES, LANES : 2 * LANES] = re.astype(bf16)

    def own_power(g, n2, at):
        re, im = det[g, n2, 0, at, :].astype(f32), det[g, n2, 1, at, :].astype(f32)
        return re * re + im * im

    def partner(g, j):
        return remote(isnd.at[g, j], ircv.at[g, j], isend.at[g, j], irecv.at[g, j], other, me)

    def rows_forward(g):
        def load(j, n2):
            h, at = j // per_half, at_rows(lax.rem(j, per_half) * CHUNK)
            return rcv1[g, h, n2, 0, at, :].astype(WORK), rcv1[g, h, n2, 1, at, :].astype(WORK)

        def store(j, n2, re, im):
            det[g, n2, 0, at_rows(j * CHUNK), :] = re
            det[g, n2, 1, at_rows(j * CHUNK), :] = im

        for h in range(PIECES):
            wait_whole(rcv1.at[g, h], recv1.at[g, h])
            rows_first(load, h)
        rows_middle(kf)

        @pl.loop(0, pairs)
        def _(j):
            rows_last(store, j)
            rows_last(store, j + pairs)
            for n2 in range(RADIX):
                a, b = own_power(g, n2, at_rows(j * CHUNK)), own_power(g, n2, at_rows((j + pairs) * CHUNK))
                first = lane_c < LANES // 2
                total = jnp.where(first, a, b) + pltpu.roll(jnp.where(first, b, a), LANES // 2, 1)
                isnd[g, j, n2] = total.astype(bf16)
            partner(g, j).start()

    def apply_factor(g):
        @pl.loop(0, pairs)
        def _(j):
            wait_whole(ircv.at[g, j], irecv.at[g, j])
            for n2 in range(RADIX):
                total = isnd[g, j, n2].astype(f32) + ircv[g, j, n2].astype(f32)
                measured = hbuf[g, n2, at_rows(j * CHUNK), :].astype(f32)
                factor = 1.0 - jnp.sqrt(measured) * lax.rsqrt(jnp.maximum(total, 1.0))
                swapped = pltpu.roll(factor, LANES // 2, 1)
                first = lane_c < LANES // 2
                for at, f in (
                    (at_rows(j * CHUNK), jnp.where(first, factor, swapped)),
                    (at_rows((j + pairs) * CHUNK), jnp.where(first, swapped, factor)),
                ):
                    for q in range(2):
                        det[g, n2, q, at, :] = (det[g, n2, q, at, :].astype(f32) * f).astype(bf16)

    def rows_back(g):
        def load(j, n2):
            at = at_rows(j * CHUNK)
            return det[g, n2, 0, at, :].astype(WORK), det[g, n2, 1, at, :].astype(WORK)

        def store(j, n2, re, im):
            h, at = j // per_half, at_rows(lax.rem(j, per_half) * CHUNK)
            snd2[g, h, n2, 0, at, :] = re
            snd2[g, h, n2, 1, at, :] = im

        for h in range(PIECES):
            rows_first(load, h)
        rows_middle(kb)
        for h in range(PIECES):
            @pl.loop(h * per_half, (h + 1) * per_half)
            def _(j):
                rows_last(store, j)

            send_rows(snd2, rcv2, send2, recv2, g, h)

    def spectral(natural):
        r = lax.broadcasted_iota(jnp.int32, (rows, LANES), 0)
        c = lax.broadcasted_iota(jnp.int32, (rows, LANES), 1)
        per = LANES // RADIX
        spread = jnp.where(c // per == r, 1.0, 0.0).astype(f32)
        picked = jnp.where(lax.rem(c, RADIX) == r, 1.0, 0.0).astype(f32)
        wide_r = lax.broadcasted_iota(jnp.int32, (LANES, LANES), 0)
        wide_c = lax.broadcasted_iota(jnp.int32, (LANES, LANES), 1)
        exact = lax.Precision.HIGHEST
        full = jnp.dot(natural.T, spread, precision=exact, preferred_element_type=f32)
        full = jnp.where(wide_r // RADIX == lax.rem(wide_c, per), full, 0.0)
        return jnp.dot(picked, full, precision=exact, preferred_element_type=f32)

    load_holo.wait()
    for n2 in range(RADIX):
        upper, lower = holo[0:deep, lanes_of(n2)], holo[deep : 2 * deep, lanes_of(n2)]
        low = jnp.where(lane_h < LANES // 2, upper, pltpu.roll(lower, LANES // 2, 1))
        high = jnp.where(lane_h < LANES // 2, pltpu.roll(upper, LANES // 2, 1), lower)
        hsnd[n2] = jnp.where(x == 0, low, high).astype(bf16)
    pl.semaphore_wait(barrier, rows)
    pltpu.make_async_copy(hsnd.at[me], hbuf.at[x, me], hrecv).start()

    @pl.loop(1, rows)
    def _(k):
        d = lax.rem(me + k, rows)
        remote(hsnd.at[d], hbuf.at[x, me], hsend, hrecv, x, d).start()

    for copy in load_phases:
        copy.wait()
    angle = spectral(angles[0])
    for part, turn in enumerate((jnp.cos, jnp.sin)):
        phc[part] = turn(angle) * scale
    for copy in [load_tw, load_mats]:
        copy.wait()
    for h in range(PIECES):
        for copy in loads[h]:
            copy.wait()
        cols_forward(h)
        send_rows(snd1, rcv1, send1, recv1, 0, h)
    for h in range(PIECES):
        send_rows(snd1, rcv1, send1, recv1, 1, h)

    wait_whole(hbuf.at[x], hrecv)
    forward = remote(hbuf.at[x], hbuf.at[x], xsend, xrecv, other, me)
    forward.start()

    load_twt.wait()
    for k2 in range(RADIX):
        for part in range(2):
            tables[part, k2] = jnp.broadcast_to(twt[part, :, k2 : k2 + 1], (LANES, LANES))
    set_phase(spectral(angles[1]))
    build(kf, 1.0)
    build(kb, -1.0)
    set_phase(spectral(angles[0]))
    build(kc, 1.0)
    wait_whole(hbuf.at[other], xrecv)

    for g in range(HALVES):
        rows_forward(g)
        apply_factor(g)
        rows_back(g)

    for h in range(PIECES):
        for side in range(2):
            wait_whole(rcv2.at[side, h], recv2.at[side, h])
        if h < PIECES - 1:
            cols_back(h)
    keep = pltpu.make_async_copy(rcv2.at[:, PIECES - 1], tail, load_sem.at[0])
    keep.start()

    fewer = pl.ds(0, rows - 1)
    for h in range(PIECES):
        for snd, sem in ((snd1, send1), (snd2, send2)):
            for g in range(2):
                wait_whole(snd.at[g, h, fewer], sem.at[g, h])
    wait_whole(hsnd.at[fewer], hsend)
    forward.wait_send()
    for g in range(2):
        for j in range(pairs):
            partner(g, j).wait_send()
    keep.wait()


def finish_kernel(probe, trans, kc, tail, out, last, uc, sems):
    height = tail.shape[3]
    top = probe.shape[2] - height
    done = pl.ds(0, top)
    early = [
        pltpu.make_async_copy(probe.at[m, :, done], out.at[m, :, done], sems.at[m]) for m in range(probe.shape[0])
    ]
    for copy in early:
        copy.start()

    def load(side, n2, part, at):
        return tail[side, n2, part, at, :]

    def store(mode, part, j, n2, value):
        last[mode, part, at_rows(j * CHUNK), lanes_of(n2)] = value

    late = [
        pltpu.make_async_copy(last.at[m], out.at[m, :, pl.ds(top, height)], sems.at[2 + m]) for m in range(probe.shape[0])
    ]
    back_piece(load, store, lambda mode: late[mode].start(), top, height, uc, probe, trans, kc)
    for copy in early + late:
        copy.wait()


def fused_local(probe_modes, transmission, hologram, phase_cols, phase_rows):
    size_a = FACTOR_A
    size_b = probe_modes.shape[3] // size_a
    mats, cosine, sine = constant_tables(size_a, size_b)
    tw = np.stack([cosine, sine])
    twt = np.stack([cosine.T, sine.T])
    angles = [phase.reshape(size_b, size_a) for phase in (phase_cols, phase_rows)]
    rows = hologram.shape[0]
    field = (2, PIECES, size_b, 2, rows // PIECES, LANES)
    bf16, dma = jnp.bfloat16, pltpu.SemaphoreType.DMA
    vmem, hbm = pl.BlockSpec(memory_space=pltpu.VMEM), pl.BlockSpec(memory_space=pltpu.MemorySpace.HBM)
    shared = (2, rows // HALVES // CHUNK, size_b, CHUNK, LANES)
    piece = rows // PIECES
    large = [probe_modes, transmission, hologram] + [jnp.asarray(table) for table in (mats, tw, twt)] + angles
    large = [pltpu.with_memory_space_constraint(array, pltpu.HBM) for array in large]
    kept = [
        (probe_modes.shape, bf16),
        (transmission.shape, bf16),
        ((size_b, 2 * LANES, 2 * LANES), bf16),
        ((2, size_b, 2, piece, LANES), bf16),
    ]
    parts = pl.pallas_call(
        fused_kernel,
        out_shape=[pltpu.VMEM(shape, kind) for shape, kind in kept],
        in_specs=[hbm] * len(large),
        out_specs=[vmem] * len(kept),
        scratch_shapes=[
            pltpu.VMEM((2, size_b, size_a), jnp.float32),
            pltpu.VMEM(hologram.shape, jnp.float32),
            pltpu.VMEM(mats.shape, bf16),
            pltpu.VMEM(tw.shape, jnp.float32),
            pltpu.VMEM(twt.shape, jnp.float32),
            pltpu.VMEM((2, size_b, LANES), jnp.float32),
            pltpu.VMEM((2, LANES, size_b), jnp.float32),
            pltpu.VMEM((size_b, 2 * LANES, 2 * LANES), bf16),
            pltpu.VMEM((size_b, 2 * LANES, 2 * LANES), bf16),
            pltpu.VMEM(field, bf16),
            pltpu.VMEM(field, bf16),
            pltpu.VMEM(field, bf16),
            pltpu.VMEM(field, bf16),
            pltpu.VMEM((size_b, rows // HALVES, LANES), bf16),
            pltpu.VMEM((2, size_b, rows // HALVES, LANES), bf16),
            pltpu.VMEM(shared, bf16),
            pltpu.VMEM(shared, bf16),
            pltpu.VMEM((size_b, 2 * (rows // PIECES), 2 * LANES), bf16),
            pltpu.VMEM((size_b, 2 * LANES, LANES), bf16),
            pltpu.VMEM((2, size_b, 2, LANES, LANES), bf16),
            pltpu.VMEM((4, size_b, LANES, LANES), jnp.float32),
            dma((2, PIECES)),
            dma((2, PIECES)),
            dma((2, PIECES)),
            dma((2, PIECES)),
            dma,
            dma,
            dma,
            dma,
            dma(shared[:2]),
            dma(shared[:2]),
            dma((6,)),
            dma((2, PIECES)),
        ],
        compiler_params=pltpu.CompilerParams(
            collective_id=0, has_side_effects=True, vmem_limit_bytes=LIMIT_MIB * 1024 * 1024
        ),
    )(*large)
    return pl.pallas_call(
        finish_kernel,
        out_shape=jax.ShapeDtypeStruct(probe_modes.shape, bf16),
        in_specs=[vmem] * len(kept),
        out_specs=hbm,
        scratch_shapes=[
            pltpu.VMEM((2, 2, piece, probe_modes.shape[3]), bf16),
            pltpu.VMEM((size_b, 2 * piece, 2 * LANES), bf16),
            dma((4,)),
        ],
        compiler_params=pltpu.CompilerParams(vmem_limit_bytes=FINISH_MIB * 1024 * 1024),
    )(*[pltpu.with_memory_space_constraint(part, pltpu.VMEM) for part in parts])


def chosen(mesh, probe_modes, *others):
    rows, modes = mesh.shape["rows"], mesh.shape["modes"]
    size = probe_modes.shape[3]
    fits = modes == 2 and probe_modes.shape[0] == 2 * modes and size == rows * FACTOR_A == RADIX * LANES
    body = fused_local if fits else local
    return jax.shard_map(
        body,
        mesh=mesh,
        in_specs=(P("modes", None, "rows", None), P(None, "rows", None), P("rows", None), P(), P()),
        out_specs=P("modes", None, "rows", None),
        check_vma=False,
    )(probe_modes, *others)


def solution(mesh):
    return functools.partial(chosen, mesh)
```

```python
import functools
import math

import jax
import jax.numpy as jnp
import numpy as np
from jax import lax
from jax.experimental import pallas as pl
from jax.experimental.pallas import tpu as pltpu
from jax.sharding import PartitionSpec as P

FACTOR_A = 128


def make_block(length, flip):
    indices = jnp.arange(length, dtype=jnp.int32)
    product = indices[:, None] * indices[None, :] % length
    angles = product.astype(jnp.float32) * (2.0 * math.pi / length)
    cosine = jnp.cos(angles)
    sine = flip * jnp.sin(angles)
    matrix = jnp.stack([jnp.stack([cosine, -sine]), jnp.stack([sine, cosine])])
    return matrix.astype(jnp.bfloat16)


def dft_tables(size_b, size_a, inverse):
    flip = 1.0 if inverse else -1.0
    outer = jnp.arange(size_b, dtype=jnp.int32)
    inner = jnp.arange(size_a, dtype=jnp.int32)
    product = outer[:, None] * inner[None, :] % (size_a * size_b)
    angles = product.astype(jnp.float32) * (2.0 * math.pi / (size_a * size_b))
    return (
        make_block(size_b, flip),
        make_block(size_a, flip),
        jnp.cos(angles),
        flip * jnp.sin(angles),
    )


def phase_tables(phase, size_a, size_b):
    ordered = phase.reshape(size_a, size_b).T
    return (jnp.cos(ordered), jnp.sin(ordered))


def rotate_by(values, cosine, sine):
    real_part = values[:, 0]
    imag_part = values[:, 1]
    return jnp.stack(
        [real_part * cosine - imag_part * sine, real_part * sine + imag_part * cosine], axis=1
    )


def transform(values, tables, inverse, layout):
    matrix_b, matrix_a, cosine, sine = tables
    if layout == "cols":
        along_b = "pqkn,mqrna->mprka"
        along_a = "pqkn,mqrbn->mprbk"
    else:
        along_b = "pqkn,mqnas->mpkas"
        along_a = "pqkn,mqbns->mpbks"
        cosine = cosine[:, :, None]
        sine = sine[:, :, None]
    scale = 1.0 / math.sqrt(matrix_a.shape[-1] * matrix_b.shape[-1])
    if inverse:
        middle = jnp.einsum(along_a, matrix_a, values, preferred_element_type=jnp.float32)
        middle = rotate_by(middle, cosine, sine).astype(jnp.bfloat16)
        return jnp.einsum(along_b, matrix_b, middle, preferred_element_type=jnp.float32) * scale
    middle = jnp.einsum(along_b, matrix_b, values, preferred_element_type=jnp.float32)
    middle = rotate_by(middle, cosine, sine).astype(jnp.bfloat16)
    return jnp.einsum(along_a, matrix_a, middle, preferred_element_type=jnp.float32) * scale


def propagate(field, forward_tables, inverse_tables, cosine, sine, layout):
    full_shape = field.shape
    size_b = forward_tables[0].shape[-1]
    size_a = forward_tables[1].shape[-1]
    if layout == "cols":
        split_shape = full_shape[:3] + (size_b, size_a)
        phase_cos, phase_sin = (cosine, sine)
    else:
        split_shape = full_shape[:2] + (size_b, size_a, full_shape[3])
        phase_cos, phase_sin = (cosine[:, :, None], sine[:, :, None])
    spectrum = transform(field.reshape(split_shape), forward_tables, False, layout)
    spectrum = rotate_by(spectrum, phase_cos, phase_sin).astype(jnp.bfloat16)
    return transform(spectrum, inverse_tables, True, layout).reshape(full_shape)


def complex_product(field, transmission):
    field_re = field[:, 0].astype(jnp.float32)
    field_im = field[:, 1].astype(jnp.float32)
    trans_re = transmission[0].astype(jnp.float32)
    trans_im = transmission[1].astype(jnp.float32)
    return jnp.stack(
        [field_re * trans_re - field_im * trans_im, field_re * trans_im + field_im * trans_re],
        axis=1,
    ).astype(jnp.bfloat16)


def apply_step(field, transmission, gradient):
    trans_re = transmission[0].astype(jnp.float32)
    trans_im = transmission[1].astype(jnp.float32)
    grad_re = gradient[:, 0]
    grad_im = gradient[:, 1]
    new_re = field[:, 0].astype(jnp.float32) - (trans_re * grad_re + trans_im * grad_im)
    new_im = field[:, 1].astype(jnp.float32) - (trans_re * grad_im - trans_im * grad_re)
    return jnp.stack([new_re, new_im], axis=1).astype(jnp.bfloat16)


def modulus_factor(detector, measured):
    values = detector.astype(jnp.float32)
    partial_sum = jnp.sum(values * values, axis=(0, 1))
    flattened = partial_sum.reshape(-1)
    measured_flat = measured.reshape(-1)
    summed = lax.psum(flattened.astype(jnp.bfloat16), "modes").astype(jnp.float32)
    factor = 1.0 - jnp.sqrt(measured_flat) / jnp.sqrt(jnp.maximum(summed, 1.0))
    return factor.reshape(partial_sum.shape)


def local(probe_modes, transmission, hologram, phase_cols, phase_rows):
    size_a = FACTOR_A
    size_b = probe_modes.shape[3] // size_a
    forward_tables = dft_tables(size_b, size_a, False)
    inverse_tables = dft_tables(size_b, size_a, True)
    col_cos, col_sin = phase_tables(phase_cols, size_a, size_b)
    row_cos, row_sin = phase_tables(phase_rows, size_a, size_b)
    exit_wave = complex_product(probe_modes, transmission)
    after_cols = propagate(
        exit_wave, forward_tables, inverse_tables, col_cos, col_sin, "cols"
    ).astype(jnp.bfloat16)
    detector_turned = propagate(
        lax.all_to_all(after_cols, "rows", split_axis=3, concat_axis=2, tiled=True),
        forward_tables,
        inverse_tables,
        row_cos,
        row_sin,
        "rows",
    ).astype(jnp.bfloat16)
    measured = lax.all_to_all(
        hologram.astype(jnp.bfloat16), "rows", split_axis=1, concat_axis=0, tiled=True
    ).astype(hologram.dtype)
    factor = modulus_factor(detector_turned, measured)
    residual_wave = (detector_turned.astype(jnp.float32) * factor).astype(jnp.bfloat16)
    back_turned = propagate(
        residual_wave, forward_tables, inverse_tables, row_cos, -row_sin, "rows"
    ).astype(jnp.bfloat16)
    back_rows = lax.all_to_all(back_turned, "rows", split_axis=2, concat_axis=3, tiled=True)
    gradient = propagate(back_rows, forward_tables, inverse_tables, col_cos, -col_sin, "cols")
    return apply_step(probe_modes, transmission, gradient)


MESH = pl.DeviceIdType.MESH
LANES = 128
RADIX = 16
HALVES = 2
PIECES = 4
GROUP = 8
LIMIT_MIB = 40
FINISH_MIB = 12
WORK = jnp.bfloat16
CHUNK = 16


def rounded(value):
    return float(np.asarray(value, np.float32).astype(jnp.bfloat16).astype(np.float32))


def butterfly4(values, sign):
    (r0, i0), (r1, i1), (r2, i2), (r3, i3) = values
    ar, ai, br, bi = r0 + r2, i0 + i2, r0 - r2, i0 - i2
    cr, ci, dr, di = r1 + r3, i1 + i3, r1 - r3, i1 - i3
    low = (br - di, bi + dr)
    high = (br + di, bi - dr)
    first, third = (low, high) if sign > 0 else (high, low)
    return [(ar + cr, ai + ci), first, (ar - cr, ai - ci), third]


def butterfly16(values, sign):
    middle = [[None] * 4 for _ in range(4)]
    for n0 in range(4):
        for k1, (re, im) in enumerate(butterfly4([values[n0 + 4 * n1] for n1 in range(4)], sign)):
            turn = n0 * k1
            if turn == 4:
                re, im = (-im, re) if sign > 0 else (im, -re)
            elif turn:
                c = rounded(math.cos(2.0 * math.pi * turn / RADIX))
                s = sign * rounded(math.sin(2.0 * math.pi * turn / RADIX))
                re, im = re * c - im * s, re * s + im * c
            middle[n0][k1] = (re, im)
    result = [None] * RADIX
    for k1 in range(4):
        for k0, pair in enumerate(butterfly4([middle[n0][k1] for n0 in range(4)], sign)):
            result[k1 + 4 * k0] = pair
    return result


def turn_by(pair, c, s):
    re, im = pair
    return re * c - im * s, re * s + im * c


def constant_tables(size_a, size_b):
    index = np.arange(size_a)
    angle = (index[:, None] * index[None, :] % size_a).astype(np.float32) * np.float32(2.0 * math.pi / size_a)
    c, s = np.cos(angle), np.sin(angle)
    right_f = np.block([[c, -s], [s, c]])
    right_i = np.block([[c, s], [-s, c]])
    mats = np.stack([right_f, right_i, right_f.T, right_i.T]).astype(jnp.bfloat16)
    size = size_a * size_b
    product = np.arange(size_b)[:, None] * index[None, :] % size
    angle = product.astype(np.float32) * np.float32(2.0 * math.pi / size)
    return mats, np.cos(angle).astype(np.float32), np.sin(angle).astype(np.float32)


def at_rows(start):
    return pl.ds(pl.multiple_of(start, CHUNK), CHUNK)


def lanes_of(k):
    return slice(k * LANES, (k + 1) * LANES)


def dot(a, b):
    return jnp.dot(a, b, preferred_element_type=jnp.float32)


def middle_cols(g, sign, uc, mats, tw, phc):
    bf16 = jnp.bfloat16
    scale = 1.0 / math.sqrt(RADIX * LANES)
    depth = uc.shape[1]
    base = pl.multiple_of(g * GROUP, GROUP)
    group = pl.ds(base, GROUP)
    y = dot(uc[group].reshape(GROUP * depth, 2 * LANES), mats[0]).reshape(GROUP, depth, 2 * LANES)
    pc, ps = phc[0, group, :][:, None, :], phc[1, group, :][:, None, :] * sign
    re, im = turn_by((y[:, :, :LANES], y[:, :, LANES:]), pc, ps)
    y = jnp.concatenate([re.astype(bf16), im.astype(bf16)], axis=2).reshape(GROUP * depth, 2 * LANES)
    z = dot(y, mats[1]).reshape(GROUP, depth, 2 * LANES)
    c, s = tw[0, group, :][:, None, :] * scale, tw[1, group, :][:, None, :] * scale
    return [turn_by((z[k, :, :LANES], z[k, :, LANES:]), c[k], s[k]) for k in range(GROUP)]


def back_first(load, side, target, top, height):
    bf16 = jnp.bfloat16

    @pl.loop(0, height // CHUNK)
    def _(j):
        at = at_rows(j * CHUNK)
        values = [(load(side, n2, 0, at).astype(WORK), load(side, n2, 1, at).astype(WORK)) for n2 in range(RADIX)]
        dst = at_rows(top + j * CHUNK)
        for k2, (re, im) in enumerate(butterfly16(values, -1)):
            target[k2, dst, 0:LANES] = re.astype(bf16)
            target[k2, dst, LANES : 2 * LANES] = im.astype(bf16)


def back_rest(store, done, top, height, lows, uc, probe, trans, kernels):
    f32, bf16 = jnp.float32, jnp.bfloat16
    chunks = height // CHUNK
    lane = lax.broadcasted_iota(jnp.int32, (height, LANES), 1)

    for k2 in range(RADIX):
        tops, bottoms = [], []
        for part in range(2):
            low = lows[k2, 0:height, lanes_of(part)].astype(f32)
            high = uc[k2, height : 2 * height, lanes_of(part)].astype(f32)
            tops.append(jnp.where(lane < LANES // 2, low, pltpu.roll(high, LANES // 2, 1)).astype(bf16))
            bottoms.append(jnp.where(lane < LANES // 2, pltpu.roll(low, LANES // 2, 1), high).astype(bf16))
        whole = jnp.concatenate([jnp.concatenate(tops, axis=1), jnp.concatenate(bottoms, axis=1)], axis=0)
        uc[k2] = dot(whole, kernels[k2]).astype(bf16)

    for mode in range(2):

        @pl.loop(0, chunks)
        def _(j):
            src = at_rows(mode * height + j * CHUNK)
            at = at_rows(top + j * CHUNK)
            values = [
                (uc[k2, src, 0:LANES].astype(WORK), uc[k2, src, LANES : 2 * LANES].astype(WORK)) for k2 in range(RADIX)
            ]
            for n2, (gr, gi) in enumerate(butterfly16(values, 1)):
                tr, ti = trans[0, at, lanes_of(n2)].astype(WORK), trans[1, at, lanes_of(n2)].astype(WORK)
                pr, pi = probe[mode, 0, at, lanes_of(n2)].astype(WORK), probe[mode, 1, at, lanes_of(n2)].astype(WORK)
                store(mode, 0, j, n2, (pr - (tr * gr + ti * gi)).astype(bf16))
                store(mode, 1, j, n2, (pi - (tr * gi - ti * gr)).astype(bf16))

        done(mode)


def fused_kernel(
    probe_hbm, trans_hbm, holo_hbm, mats_hbm, tw_hbm, twt_hbm, phase_c_hbm, phase_r_hbm,
    probe, trans, kc, started, tail,
    angles, holo, mats, tw, twt, phc, pht, kf, kb, snd1, rcv1, snd2, rcv2, hsnd, hbuf, isnd, ircv, uc, ur, det, tables,
    send1, recv1, send2, recv2, hsend, hrecv, xsend, xrecv, isend, irecv, load_sem, piece_sem,
):
    f32, bf16 = jnp.float32, jnp.bfloat16
    x, me = lax.axis_index("modes"), lax.axis_index("rows")
    other = 1 - x
    rows = RADIX
    half_rows = probe.shape[2] // PIECES
    per_half = half_rows // CHUNK
    deep = probe.shape[2] // HALVES
    scale = 1.0 / math.sqrt(RADIX * LANES)
    pairs = deep // CHUNK
    lane = lax.broadcasted_iota(jnp.int32, (half_rows, LANES), 1)
    lane_h = lax.broadcasted_iota(jnp.int32, (deep, LANES), 1)
    lane_c = lax.broadcasted_iota(jnp.int32, (CHUNK, LANES), 1)

    def piece_loads(h):
        at = pl.ds(h * half_rows, half_rows)
        return [
            pltpu.make_async_copy(probe_hbm.at[:, :, at], probe.at[:, :, at], piece_sem.at[0, h]),
            pltpu.make_async_copy(trans_hbm.at[:, at], trans.at[:, at], piece_sem.at[1, h]),
        ]

    loads = [piece_loads(h) for h in range(PIECES)]
    load_tw = pltpu.make_async_copy(tw_hbm, tw, load_sem.at[0])
    load_mats = pltpu.make_async_copy(mats_hbm, mats, load_sem.at[1])
    load_twt = pltpu.make_async_copy(twt_hbm, twt, load_sem.at[2])
    load_holo = pltpu.make_async_copy(holo_hbm, holo, load_sem.at[3])
    barrier = pltpu.get_barrier_semaphore()

    @pl.loop(1, rows)
    def _(k):
        pl.semaphore_signal(barrier, inc=1, device_id=(x, lax.rem(me + k, rows)), device_id_type=MESH)

    pl.semaphore_signal(barrier, inc=1, device_id=(other, me), device_id_type=MESH)
    load_phases = [
        pltpu.make_async_copy(phase, angles.at[i], load_sem.at[4 + i])
        for i, phase in enumerate((phase_c_hbm, phase_r_hbm))
    ]
    for copy in [load_holo] + load_phases + loads[0] + [load_tw, load_mats] + sum(loads[1:], []) + [load_twt]:
        copy.start()


    def remote(src, dst, ss, rs, xd, d):
        return pltpu.make_async_remote_copy(
            src_ref=src, dst_ref=dst, send_sem=ss, recv_sem=rs, device_id=(xd, d), device_id_type=MESH
        )

    def send_rows(snd, rcv, ss, rs, g, h):
        pltpu.make_async_copy(snd.at[g, h, me], rcv.at[g, h, me], rs.at[g, h]).start()

        @pl.loop(1, rows)
        def _(k):
            d = lax.rem(me + k, rows)
            remote(snd.at[g, h, d], rcv.at[g, h, me], ss.at[g, h], rs.at[g, h], x, d).start()

    def wait_whole(ref, sem):
        pltpu.make_async_copy(ref, ref, sem).wait()

    def cols_forward(h):
        @pl.loop(0, 2 * per_half)
        def _(t):
            mode, j = t // per_half, lax.rem(t, per_half)
            at = at_rows(h * half_rows + j * CHUNK)
            values = []
            for n2 in range(RADIX):
                pr, pi = probe[mode, 0, at, lanes_of(n2)].astype(f32), probe[mode, 1, at, lanes_of(n2)].astype(f32)
                tr, ti = trans[0, at, lanes_of(n2)].astype(f32), trans[1, at, lanes_of(n2)].astype(f32)
                er, ei = pr * tr - pi * ti, pr * ti + pi * tr
                values.append((er.astype(bf16).astype(f32), ei.astype(bf16).astype(f32)))
            dst = at_rows(mode * half_rows + j * CHUNK)
            for k2, pair in enumerate(butterfly16(values, -1)):
                re, im = turn_by(pair, tw[0, k2 : k2 + 1, :], -tw[1, k2 : k2 + 1, :])
                uc[k2, dst, 0:LANES] = re.astype(bf16)
                uc[k2, dst, LANES : 2 * LANES] = im.astype(bf16)

        @pl.loop(0, RADIX // GROUP)
        def _(g):
            for k, pair in enumerate(middle_cols(g, 1.0, uc, mats, tw, phc)):
                k2 = g * GROUP + k
                for part, v in enumerate(pair):
                    a, b = v[:half_rows], v[half_rows:]
                    low = jnp.where(lane < LANES // 2, a, pltpu.roll(b, LANES // 2, 1))
                    high = jnp.where(lane < LANES // 2, pltpu.roll(a, LANES // 2, 1), b)
                    uc[k2, 0:half_rows, lanes_of(part)] = low.astype(bf16)
                    uc[k2, half_rows : 2 * half_rows, lanes_of(part)] = high.astype(bf16)

        @pl.loop(0, 2 * per_half)
        def _(t):
            side, j = t // per_half, lax.rem(t, per_half)
            src = at_rows(side * half_rows + j * CHUNK)
            dst = at_rows(j * CHUNK)
            values = [
                (uc[k2, src, 0:LANES].astype(f32), uc[k2, src, LANES : 2 * LANES].astype(f32)) for k2 in range(RADIX)
            ]
            for n2, (re, im) in enumerate(butterfly16(values, 1)):
                snd1[side, h, n2, 0, dst, :] = re.astype(bf16)
                snd1[side, h, n2, 1, dst, :] = im.astype(bf16)

    def cols_back(h):
        def load(side, n2, part, at):
            return rcv2[side, h, n2, part, at, :]

        def store(mode, part, j, n2, value):
            probe[mode, part, at_rows(h * half_rows + j * CHUNK), lanes_of(n2)] = value

        for side in range(2):
            back_first(load, side, uc, side * half_rows, half_rows)
        back_rest(store, lambda mode: None, h * half_rows, half_rows, uc, uc, probe, trans, kc)

    def rows_first(load, h):
        @pl.loop(h * per_half, (h + 1) * per_half)
        def _(j):
            at, at_im = at_rows(j * CHUNK), at_rows(LANES + j * CHUNK)
            values = [load(j, n2) for n2 in range(RADIX)]
            for k2, (re, im) in enumerate(butterfly16(values, -1)):
                ur[k2, at, :] = re.astype(bf16)
                ur[k2, at_im, :] = im.astype(bf16)

    def rows_middle(kernels):
        for k2 in range(RADIX):
            ur[k2] = dot(kernels[k2], ur[k2]).astype(bf16)

    def rows_last(store, j):
        at, at_im = at_rows(j * CHUNK), at_rows(LANES + j * CHUNK)
        values = [(ur[k2, at, :].astype(WORK), ur[k2, at_im, :].astype(WORK)) for k2 in range(RADIX)]
        for n2, (re, im) in enumerate(butterfly16(values, 1)):
            store(j, n2, re.astype(bf16), im.astype(bf16))

    def set_phase(angle):
        for part, turn in enumerate((jnp.cos, jnp.sin)):
            pht[part] = turn(angle).T * scale
        for k2 in range(RADIX):
            for part in range(2):
                tables[2 + part, k2] = jnp.broadcast_to(pht[part, :, k2 : k2 + 1], (LANES, LANES))

    def build(kernels, sign):
        @pl.loop(0, RADIX)
        def _(k2):
            c, s = mats[2, 0:LANES, 0:LANES].astype(f32), mats[2, 0:LANES, LANES : 2 * LANES].astype(f32)
            re, im = turn_by((c, -s), tables[2, k2], tables[3, k2] * sign)
            re, im = turn_by((re, im), tw[0, pl.ds(k2, 1), :], -tw[1, pl.ds(k2, 1), :])
            z = dot(mats[3], jnp.concatenate([re.astype(bf16), im.astype(bf16)], axis=0))
            re, im = turn_by((z[:LANES], z[LANES:]), tables[0, k2] * scale, tables[1, k2] * scale)
            kernels[k2, 0:LANES, 0:LANES] = re.astype(bf16)
            kernels[k2, LANES : 2 * LANES, 0:LANES] = im.astype(bf16)
            kernels[k2, 0:LANES, LANES : 2 * LANES] = (-im).astype(bf16)
            kernels[k2, LANES : 2 * LANES, LANES : 2 * LANES] = re.astype(bf16)

    def own_power(g, n2, at):
        re, im = det[g, n2, 0, at, :].astype(f32), det[g, n2, 1, at, :].astype(f32)
        return re * re + im * im

    def partner(g, j):
        return remote(isnd.at[g, j], ircv.at[g, j], isend.at[g, j], irecv.at[g, j], other, me)

    def rows_forward(g):
        def load(j, n2):
            h, at = j // per_half, at_rows(lax.rem(j, per_half) * CHUNK)
            return rcv1[g, h, n2, 0, at, :].astype(WORK), rcv1[g, h, n2, 1, at, :].astype(WORK)

        def store(j, n2, re, im):
            det[g, n2, 0, at_rows(j * CHUNK), :] = re
            det[g, n2, 1, at_rows(j * CHUNK), :] = im

        for h in range(PIECES):
            wait_whole(rcv1.at[g, h], recv1.at[g, h])
            rows_first(load, h)
        rows_middle(kf)

        @pl.loop(0, pairs)
        def _(j):
            rows_last(store, j)
            rows_last(store, j + pairs)
            for n2 in range(RADIX):
                a, b = own_power(g, n2, at_rows(j * CHUNK)), own_power(g, n2, at_rows((j + pairs) * CHUNK))
                first = lane_c < LANES // 2
                total = jnp.where(first, a, b) + pltpu.roll(jnp.where(first, b, a), LANES // 2, 1)
                isnd[g, j, n2] = total.astype(bf16)
            partner(g, j).start()

    def apply_factor(g):
        @pl.loop(0, pairs)
        def _(j):
            wait_whole(ircv.at[g, j], irecv.at[g, j])
            for n2 in range(RADIX):
                total = isnd[g, j, n2].astype(f32) + ircv[g, j, n2].astype(f32)
                measured = hbuf[g, n2, at_rows(j * CHUNK), :].astype(f32)
                factor = 1.0 - jnp.sqrt(measured) * lax.rsqrt(jnp.maximum(total, 1.0))
                swapped = pltpu.roll(factor, LANES // 2, 1)
                first = lane_c < LANES // 2
                for at, f in (
                    (at_rows(j * CHUNK), jnp.where(first, factor, swapped)),
                    (at_rows((j + pairs) * CHUNK), jnp.where(first, swapped, factor)),
                ):
                    for q in range(2):
                        det[g, n2, q, at, :] = (det[g, n2, q, at, :].astype(f32) * f).astype(bf16)

    def rows_back(g):
        def load(j, n2):
            at = at_rows(j * CHUNK)
            return det[g, n2, 0, at, :].astype(WORK), det[g, n2, 1, at, :].astype(WORK)

        def store(j, n2, re, im):
            h, at = j // per_half, at_rows(lax.rem(j, per_half) * CHUNK)
            snd2[g, h, n2, 0, at, :] = re
            snd2[g, h, n2, 1, at, :] = im

        for h in range(PIECES):
            rows_first(load, h)
        rows_middle(kb)
        for h in range(PIECES):
            @pl.loop(h * per_half, (h + 1) * per_half)
            def _(j):
                rows_last(store, j)

            send_rows(snd2, rcv2, send2, recv2, g, h)

    def spectral(natural):
        r = lax.broadcasted_iota(jnp.int32, (rows, LANES), 0)
        c = lax.broadcasted_iota(jnp.int32, (rows, LANES), 1)
        per = LANES // RADIX
        spread = jnp.where(c // per == r, 1.0, 0.0).astype(f32)
        picked = jnp.where(lax.rem(c, RADIX) == r, 1.0, 0.0).astype(f32)
        wide_r = lax.broadcasted_iota(jnp.int32, (LANES, LANES), 0)
        wide_c = lax.broadcasted_iota(jnp.int32, (LANES, LANES), 1)
        exact = lax.Precision.HIGHEST
        full = jnp.dot(natural.T, spread, precision=exact, preferred_element_type=f32)
        full = jnp.where(wide_r // RADIX == lax.rem(wide_c, per), full, 0.0)
        return jnp.dot(picked, full, precision=exact, preferred_element_type=f32)

    load_holo.wait()
    for n2 in range(RADIX):
        upper, lower = holo[0:deep, lanes_of(n2)], holo[deep : 2 * deep, lanes_of(n2)]
        low = jnp.where(lane_h < LANES // 2, upper, pltpu.roll(lower, LANES // 2, 1))
        high = jnp.where(lane_h < LANES // 2, pltpu.roll(upper, LANES // 2, 1), lower)
        hsnd[n2] = jnp.where(x == 0, low, high).astype(bf16)
    pl.semaphore_wait(barrier, rows)
    pltpu.make_async_copy(hsnd.at[me], hbuf.at[x, me], hrecv).start()

    @pl.loop(1, rows)
    def _(k):
        d = lax.rem(me + k, rows)
        remote(hsnd.at[d], hbuf.at[x, me], hsend, hrecv, x, d).start()

    for copy in load_phases:
        copy.wait()
    angle = spectral(angles[0])
    for part, turn in enumerate((jnp.cos, jnp.sin)):
        phc[part] = turn(angle) * scale
    for copy in [load_tw, load_mats]:
        copy.wait()
    for h in range(PIECES):
        for copy in loads[h]:
            copy.wait()
        cols_forward(h)
        send_rows(snd1, rcv1, send1, recv1, 0, h)
    for h in range(PIECES):
        send_rows(snd1, rcv1, send1, recv1, 1, h)

    wait_whole(hbuf.at[x], hrecv)
    forward = remote(hbuf.at[x], hbuf.at[x], xsend, xrecv, other, me)
    forward.start()

    load_twt.wait()
    for k2 in range(RADIX):
        for part in range(2):
            tables[part, k2] = jnp.broadcast_to(twt[part, :, k2 : k2 + 1], (LANES, LANES))
    set_phase(spectral(angles[1]))
    build(kf, 1.0)
    build(kb, -1.0)
    set_phase(spectral(angles[0]))
    build(kc, 1.0)
    wait_whole(hbuf.at[other], xrecv)

    for g in range(HALVES):
        rows_forward(g)
        apply_factor(g)
        rows_back(g)

    final = PIECES - 1
    for h in range(final):
        for side in range(2):
            wait_whole(rcv2.at[side, h], recv2.at[side, h])
        cols_back(h)
    wait_whole(rcv2.at[0, final], recv2.at[0, final])
    back_first(lambda side, n2, part, at: rcv2[side, final, n2, part, at, :], 0, started, 0, half_rows)
    wait_whole(rcv2.at[1, final], recv2.at[1, final])
    keep = pltpu.make_async_copy(rcv2.at[1, final], tail, load_sem.at[0])
    keep.start()

    fewer = pl.ds(0, rows - 1)
    for h in range(PIECES):
        for snd, sem in ((snd1, send1), (snd2, send2)):
            for g in range(2):
                wait_whole(snd.at[g, h, fewer], sem.at[g, h])
    wait_whole(hsnd.at[fewer], hsend)
    forward.wait_send()
    for g in range(2):
        for j in range(pairs):
            partner(g, j).wait_send()
    keep.wait()


def finish_kernel(probe, trans, kc, started, tail, out, last, uc, sems):
    height = tail.shape[2]
    top = probe.shape[2] - height
    done = pl.ds(0, top)
    early = [
        pltpu.make_async_copy(probe.at[m, :, done], out.at[m, :, done], sems.at[m]) for m in range(probe.shape[0])
    ]
    for copy in early:
        copy.start()

    def load(side, n2, part, at):
        return tail[n2, part, at, :]

    def store(mode, part, j, n2, value):
        last[mode, part, at_rows(j * CHUNK), lanes_of(n2)] = value

    late = [
        pltpu.make_async_copy(last.at[m], out.at[m, :, pl.ds(top, height)], sems.at[2 + m]) for m in range(probe.shape[0])
    ]
    back_first(load, 1, uc, height, height)
    back_rest(store, lambda mode: late[mode].start(), top, height, started, uc, probe, trans, kc)
    for copy in early + late:
        copy.wait()


def fused_local(probe_modes, transmission, hologram, phase_cols, phase_rows):
    size_a = FACTOR_A
    size_b = probe_modes.shape[3] // size_a
    mats, cosine, sine = constant_tables(size_a, size_b)
    tw = np.stack([cosine, sine])
    twt = np.stack([cosine.T, sine.T])
    angles = [phase.reshape(size_b, size_a) for phase in (phase_cols, phase_rows)]
    rows = hologram.shape[0]
    field = (2, PIECES, size_b, 2, rows // PIECES, LANES)
    bf16, dma = jnp.bfloat16, pltpu.SemaphoreType.DMA
    vmem, hbm = pl.BlockSpec(memory_space=pltpu.VMEM), pl.BlockSpec(memory_space=pltpu.MemorySpace.HBM)
    shared = (2, rows // HALVES // CHUNK, size_b, CHUNK, LANES)
    piece = rows // PIECES
    large = [probe_modes, transmission, hologram] + [jnp.asarray(table) for table in (mats, tw, twt)] + angles
    large = [pltpu.with_memory_space_constraint(array, pltpu.HBM) for array in large]
    kept = [
        (probe_modes.shape, bf16),
        (transmission.shape, bf16),
        ((size_b, 2 * LANES, 2 * LANES), bf16),
        ((size_b, piece, 2 * LANES), bf16),
        ((size_b, 2, piece, LANES), bf16),
    ]
    parts = pl.pallas_call(
        fused_kernel,
        out_shape=[pltpu.VMEM(shape, kind) for shape, kind in kept],
        in_specs=[hbm] * len(large),
        out_specs=[vmem] * len(kept),
        scratch_shapes=[
            pltpu.VMEM((2, size_b, size_a), jnp.float32),
            pltpu.VMEM(hologram.shape, jnp.float32),
            pltpu.VMEM(mats.shape, bf16),
            pltpu.VMEM(tw.shape, jnp.float32),
            pltpu.VMEM(twt.shape, jnp.float32),
            pltpu.VMEM((2, size_b, LANES), jnp.float32),
            pltpu.VMEM((2, LANES, size_b), jnp.float32),
            pltpu.VMEM((size_b, 2 * LANES, 2 * LANES), bf16),
            pltpu.VMEM((size_b, 2 * LANES, 2 * LANES), bf16),
            pltpu.VMEM(field, bf16),
            pltpu.VMEM(field, bf16),
            pltpu.VMEM(field, bf16),
            pltpu.VMEM(field, bf16),
            pltpu.VMEM((size_b, rows // HALVES, LANES), bf16),
            pltpu.VMEM((2, size_b, rows // HALVES, LANES), bf16),
            pltpu.VMEM(shared, bf16),
            pltpu.VMEM(shared, bf16),
            pltpu.VMEM((size_b, 2 * (rows // PIECES), 2 * LANES), bf16),
            pltpu.VMEM((size_b, 2 * LANES, LANES), bf16),
            pltpu.VMEM((2, size_b, 2, LANES, LANES), bf16),
            pltpu.VMEM((4, size_b, LANES, LANES), jnp.float32),
            dma((2, PIECES)),
            dma((2, PIECES)),
            dma((2, PIECES)),
            dma((2, PIECES)),
            dma,
            dma,
            dma,
            dma,
            dma(shared[:2]),
            dma(shared[:2]),
            dma((6,)),
            dma((2, PIECES)),
        ],
        compiler_params=pltpu.CompilerParams(
            collective_id=0, has_side_effects=True, vmem_limit_bytes=LIMIT_MIB * 1024 * 1024
        ),
    )(*large)
    return pl.pallas_call(
        finish_kernel,
        out_shape=jax.ShapeDtypeStruct(probe_modes.shape, bf16),
        in_specs=[vmem] * len(kept),
        out_specs=hbm,
        scratch_shapes=[
            pltpu.VMEM((2, 2, piece, probe_modes.shape[3]), bf16),
            pltpu.VMEM((size_b, 2 * piece, 2 * LANES), bf16),
            dma((4,)),
        ],
        compiler_params=pltpu.CompilerParams(vmem_limit_bytes=FINISH_MIB * 1024 * 1024),
    )(*[pltpu.with_memory_space_constraint(part, pltpu.VMEM) for part in parts])


def chosen(mesh, probe_modes, *others):
    rows, modes = mesh.shape["rows"], mesh.shape["modes"]
    size = probe_modes.shape[3]
    fits = modes == 2 and probe_modes.shape[0] == 2 * modes and size == rows * FACTOR_A == RADIX * LANES
    body = fused_local if fits else local
    return jax.shard_map(
        body,
        mesh=mesh,
        in_specs=(P("modes", None, "rows", None), P(None, "rows", None), P("rows", None), P(), P()),
        out_specs=P("modes", None, "rows", None),
        check_vma=False,
    )(probe_modes, *others)


def solution(mesh):
    return functools.partial(chosen, mesh)
```

```python
import functools
import math

import jax
import jax.numpy as jnp
import numpy as np
from jax import lax
from jax.experimental import pallas as pl
from jax.experimental.pallas import tpu as pltpu
from jax.sharding import PartitionSpec as P

FACTOR_A = 128


def make_block(length, flip):
    indices = jnp.arange(length, dtype=jnp.int32)
    product = indices[:, None] * indices[None, :] % length
    angles = product.astype(jnp.float32) * (2.0 * math.pi / length)
    cosine = jnp.cos(angles)
    sine = flip * jnp.sin(angles)
    matrix = jnp.stack([jnp.stack([cosine, -sine]), jnp.stack([sine, cosine])])
    return matrix.astype(jnp.bfloat16)


def dft_tables(size_b, size_a, inverse):
    flip = 1.0 if inverse else -1.0
    outer = jnp.arange(size_b, dtype=jnp.int32)
    inner = jnp.arange(size_a, dtype=jnp.int32)
    product = outer[:, None] * inner[None, :] % (size_a * size_b)
    angles = product.astype(jnp.float32) * (2.0 * math.pi / (size_a * size_b))
    return (
        make_block(size_b, flip),
        make_block(size_a, flip),
        jnp.cos(angles),
        flip * jnp.sin(angles),
    )


def phase_tables(phase, size_a, size_b):
    ordered = phase.reshape(size_a, size_b).T
    return (jnp.cos(ordered), jnp.sin(ordered))


def rotate_by(values, cosine, sine):
    real_part = values[:, 0]
    imag_part = values[:, 1]
    return jnp.stack(
        [real_part * cosine - imag_part * sine, real_part * sine + imag_part * cosine], axis=1
    )


def transform(values, tables, inverse, layout):
    matrix_b, matrix_a, cosine, sine = tables
    if layout == "cols":
        along_b = "pqkn,mqrna->mprka"
        along_a = "pqkn,mqrbn->mprbk"
    else:
        along_b = "pqkn,mqnas->mpkas"
        along_a = "pqkn,mqbns->mpbks"
        cosine = cosine[:, :, None]
        sine = sine[:, :, None]
    scale = 1.0 / math.sqrt(matrix_a.shape[-1] * matrix_b.shape[-1])
    if inverse:
        middle = jnp.einsum(along_a, matrix_a, values, preferred_element_type=jnp.float32)
        middle = rotate_by(middle, cosine, sine).astype(jnp.bfloat16)
        return jnp.einsum(along_b, matrix_b, middle, preferred_element_type=jnp.float32) * scale
    middle = jnp.einsum(along_b, matrix_b, values, preferred_element_type=jnp.float32)
    middle = rotate_by(middle, cosine, sine).astype(jnp.bfloat16)
    return jnp.einsum(along_a, matrix_a, middle, preferred_element_type=jnp.float32) * scale


def propagate(field, forward_tables, inverse_tables, cosine, sine, layout):
    full_shape = field.shape
    size_b = forward_tables[0].shape[-1]
    size_a = forward_tables[1].shape[-1]
    if layout == "cols":
        split_shape = full_shape[:3] + (size_b, size_a)
        phase_cos, phase_sin = (cosine, sine)
    else:
        split_shape = full_shape[:2] + (size_b, size_a, full_shape[3])
        phase_cos, phase_sin = (cosine[:, :, None], sine[:, :, None])
    spectrum = transform(field.reshape(split_shape), forward_tables, False, layout)
    spectrum = rotate_by(spectrum, phase_cos, phase_sin).astype(jnp.bfloat16)
    return transform(spectrum, inverse_tables, True, layout).reshape(full_shape)


def complex_product(field, transmission):
    field_re = field[:, 0].astype(jnp.float32)
    field_im = field[:, 1].astype(jnp.float32)
    trans_re = transmission[0].astype(jnp.float32)
    trans_im = transmission[1].astype(jnp.float32)
    return jnp.stack(
        [field_re * trans_re - field_im * trans_im, field_re * trans_im + field_im * trans_re],
        axis=1,
    ).astype(jnp.bfloat16)


def apply_step(field, transmission, gradient):
    trans_re = transmission[0].astype(jnp.float32)
    trans_im = transmission[1].astype(jnp.float32)
    grad_re = gradient[:, 0]
    grad_im = gradient[:, 1]
    new_re = field[:, 0].astype(jnp.float32) - (trans_re * grad_re + trans_im * grad_im)
    new_im = field[:, 1].astype(jnp.float32) - (trans_re * grad_im - trans_im * grad_re)
    return jnp.stack([new_re, new_im], axis=1).astype(jnp.bfloat16)


def modulus_factor(detector, measured):
    values = detector.astype(jnp.float32)
    partial_sum = jnp.sum(values * values, axis=(0, 1))
    flattened = partial_sum.reshape(-1)
    measured_flat = measured.reshape(-1)
    summed = lax.psum(flattened.astype(jnp.bfloat16), "modes").astype(jnp.float32)
    factor = 1.0 - jnp.sqrt(measured_flat) / jnp.sqrt(jnp.maximum(summed, 1.0))
    return factor.reshape(partial_sum.shape)


def local(probe_modes, transmission, hologram, phase_cols, phase_rows):
    size_a = FACTOR_A
    size_b = probe_modes.shape[3] // size_a
    forward_tables = dft_tables(size_b, size_a, False)
    inverse_tables = dft_tables(size_b, size_a, True)
    col_cos, col_sin = phase_tables(phase_cols, size_a, size_b)
    row_cos, row_sin = phase_tables(phase_rows, size_a, size_b)
    exit_wave = complex_product(probe_modes, transmission)
    after_cols = propagate(
        exit_wave, forward_tables, inverse_tables, col_cos, col_sin, "cols"
    ).astype(jnp.bfloat16)
    detector_turned = propagate(
        lax.all_to_all(after_cols, "rows", split_axis=3, concat_axis=2, tiled=True),
        forward_tables,
        inverse_tables,
        row_cos,
        row_sin,
        "rows",
    ).astype(jnp.bfloat16)
    measured = lax.all_to_all(
        hologram.astype(jnp.bfloat16), "rows", split_axis=1, concat_axis=0, tiled=True
    ).astype(hologram.dtype)
    factor = modulus_factor(detector_turned, measured)
    residual_wave = (detector_turned.astype(jnp.float32) * factor).astype(jnp.bfloat16)
    back_turned = propagate(
        residual_wave, forward_tables, inverse_tables, row_cos, -row_sin, "rows"
    ).astype(jnp.bfloat16)
    back_rows = lax.all_to_all(back_turned, "rows", split_axis=2, concat_axis=3, tiled=True)
    gradient = propagate(back_rows, forward_tables, inverse_tables, col_cos, -col_sin, "cols")
    return apply_step(probe_modes, transmission, gradient)


MESH = pl.DeviceIdType.MESH
LANES = 128
RADIX = 16
HALVES = 2
PIECES = 4
GROUP = 8
LIMIT_MIB = 40
FINISH_MIB = 12
WORK = jnp.bfloat16
CHUNK = 16


def rounded(value):
    return float(np.asarray(value, np.float32).astype(jnp.bfloat16).astype(np.float32))


def butterfly4(values, sign):
    (r0, i0), (r1, i1), (r2, i2), (r3, i3) = values
    ar, ai, br, bi = r0 + r2, i0 + i2, r0 - r2, i0 - i2
    cr, ci, dr, di = r1 + r3, i1 + i3, r1 - r3, i1 - i3
    low = (br - di, bi + dr)
    high = (br + di, bi - dr)
    first, third = (low, high) if sign > 0 else (high, low)
    return [(ar + cr, ai + ci), first, (ar - cr, ai - ci), third]


def butterfly16(values, sign):
    middle = [[None] * 4 for _ in range(4)]
    for n0 in range(4):
        for k1, (re, im) in enumerate(butterfly4([values[n0 + 4 * n1] for n1 in range(4)], sign)):
            turn = n0 * k1
            if turn == 4:
                re, im = (-im, re) if sign > 0 else (im, -re)
            elif turn:
                c = rounded(math.cos(2.0 * math.pi * turn / RADIX))
                s = sign * rounded(math.sin(2.0 * math.pi * turn / RADIX))
                re, im = re * c - im * s, re * s + im * c
            middle[n0][k1] = (re, im)
    result = [None] * RADIX
    for k1 in range(4):
        for k0, pair in enumerate(butterfly4([middle[n0][k1] for n0 in range(4)], sign)):
            result[k1 + 4 * k0] = pair
    return result


def turn_by(pair, c, s):
    re, im = pair
    return re * c - im * s, re * s + im * c


def constant_tables(size_a, size_b):
    index = np.arange(size_a)
    angle = (index[:, None] * index[None, :] % size_a).astype(np.float32) * np.float32(2.0 * math.pi / size_a)
    c, s = np.cos(angle), np.sin(angle)
    right_f = np.block([[c, -s], [s, c]])
    right_i = np.block([[c, s], [-s, c]])
    mats = np.stack([right_f, right_i, right_f.T, right_i.T]).astype(jnp.bfloat16)
    size = size_a * size_b
    product = np.arange(size_b)[:, None] * index[None, :] % size
    angle = product.astype(np.float32) * np.float32(2.0 * math.pi / size)
    return mats, np.cos(angle).astype(np.float32), np.sin(angle).astype(np.float32)


def at_rows(start):
    return pl.ds(pl.multiple_of(start, CHUNK), CHUNK)


def lanes_of(k):
    return slice(k * LANES, (k + 1) * LANES)


def dot(a, b):
    return jnp.dot(a, b, preferred_element_type=jnp.float32)


def middle_cols(g, sign, uc, mats, tw, phc):
    bf16 = jnp.bfloat16
    scale = 1.0 / math.sqrt(RADIX * LANES)
    depth = uc.shape[1]
    base = pl.multiple_of(g * GROUP, GROUP)
    group = pl.ds(base, GROUP)
    y = dot(uc[group].reshape(GROUP * depth, 2 * LANES), mats[0]).reshape(GROUP, depth, 2 * LANES)
    pc, ps = phc[0, group, :][:, None, :], phc[1, group, :][:, None, :] * sign
    re, im = turn_by((y[:, :, :LANES], y[:, :, LANES:]), pc, ps)
    y = jnp.concatenate([re.astype(bf16), im.astype(bf16)], axis=2).reshape(GROUP * depth, 2 * LANES)
    z = dot(y, mats[1]).reshape(GROUP, depth, 2 * LANES)
    c, s = tw[0, group, :][:, None, :] * scale, tw[1, group, :][:, None, :] * scale
    return [turn_by((z[k, :, :LANES], z[k, :, LANES:]), c[k], s[k]) for k in range(GROUP)]


def back_first(load, side, target, top, height):
    bf16 = jnp.bfloat16

    @pl.loop(0, height // CHUNK)
    def _(j):
        at = at_rows(j * CHUNK)
        values = [(load(side, n2, 0, at).astype(WORK), load(side, n2, 1, at).astype(WORK)) for n2 in range(RADIX)]
        dst = at_rows(top + j * CHUNK)
        for k2, (re, im) in enumerate(butterfly16(values, -1)):
            target[k2, dst, 0:LANES] = re.astype(bf16)
            target[k2, dst, LANES : 2 * LANES] = im.astype(bf16)


def back_rest(store, done, top, height, lows, uc, probe, trans, kernels):
    f32, bf16 = jnp.float32, jnp.bfloat16
    chunks = height // CHUNK
    lane = lax.broadcasted_iota(jnp.int32, (height, LANES), 1)

    for k2 in range(RADIX):
        tops, bottoms = [], []
        for part in range(2):
            low = lows[k2, 0:height, lanes_of(part)].astype(f32)
            high = uc[k2, height : 2 * height, lanes_of(part)].astype(f32)
            tops.append(jnp.where(lane < LANES // 2, low, pltpu.roll(high, LANES // 2, 1)).astype(bf16))
            bottoms.append(jnp.where(lane < LANES // 2, pltpu.roll(low, LANES // 2, 1), high).astype(bf16))
        whole = jnp.concatenate([jnp.concatenate(tops, axis=1), jnp.concatenate(bottoms, axis=1)], axis=0)
        uc[k2] = dot(whole, kernels[k2]).astype(bf16)

    for mode in range(2):

        @pl.loop(0, chunks)
        def _(j):
            src = at_rows(mode * height + j * CHUNK)
            at = at_rows(top + j * CHUNK)
            values = [
                (uc[k2, src, 0:LANES].astype(WORK), uc[k2, src, LANES : 2 * LANES].astype(WORK)) for k2 in range(RADIX)
            ]
            for n2, (gr, gi) in enumerate(butterfly16(values, 1)):
                tr, ti = trans[0, at, lanes_of(n2)].astype(WORK), trans[1, at, lanes_of(n2)].astype(WORK)
                pr, pi = probe[mode, 0, at, lanes_of(n2)].astype(WORK), probe[mode, 1, at, lanes_of(n2)].astype(WORK)
                store(mode, 0, j, n2, (pr - (tr * gr + ti * gi)).astype(bf16))
                store(mode, 1, j, n2, (pi - (tr * gi - ti * gr)).astype(bf16))
            done(mode, j)


def fused_kernel(
    probe_hbm, trans_hbm, holo_hbm, mats_hbm, tw_hbm, twt_hbm, phase_c_hbm, phase_r_hbm,
    probe, trans, kc, started, tail,
    angles, holo, mats, tw, twt, phc, pht, kf, kb, snd1, rcv1, snd2, rcv2, hsnd, hbuf, isnd, ircv, uc, ur, det, tables,
    send1, recv1, send2, recv2, hsend, hrecv, xsend, xrecv, isend, irecv, load_sem, piece_sem,
):
    f32, bf16 = jnp.float32, jnp.bfloat16
    x, me = lax.axis_index("modes"), lax.axis_index("rows")
    other = 1 - x
    rows = RADIX
    half_rows = probe.shape[2] // PIECES
    per_half = half_rows // CHUNK
    deep = probe.shape[2] // HALVES
    scale = 1.0 / math.sqrt(RADIX * LANES)
    pairs = deep // CHUNK
    lane = lax.broadcasted_iota(jnp.int32, (half_rows, LANES), 1)
    lane_h = lax.broadcasted_iota(jnp.int32, (deep, LANES), 1)
    lane_c = lax.broadcasted_iota(jnp.int32, (CHUNK, LANES), 1)

    def piece_loads(h):
        at = pl.ds(h * half_rows, half_rows)
        return [
            pltpu.make_async_copy(probe_hbm.at[:, :, at], probe.at[:, :, at], piece_sem.at[0, h]),
            pltpu.make_async_copy(trans_hbm.at[:, at], trans.at[:, at], piece_sem.at[1, h]),
        ]

    loads = [piece_loads(h) for h in range(PIECES)]
    load_tw = pltpu.make_async_copy(tw_hbm, tw, load_sem.at[0])
    load_mats = pltpu.make_async_copy(mats_hbm, mats, load_sem.at[1])
    load_twt = pltpu.make_async_copy(twt_hbm, twt, load_sem.at[2])
    load_holo = pltpu.make_async_copy(holo_hbm, holo, load_sem.at[3])
    barrier = pltpu.get_barrier_semaphore()

    @pl.loop(1, rows)
    def _(k):
        pl.semaphore_signal(barrier, inc=1, device_id=(x, lax.rem(me + k, rows)), device_id_type=MESH)

    pl.semaphore_signal(barrier, inc=1, device_id=(other, me), device_id_type=MESH)
    load_phases = [
        pltpu.make_async_copy(phase, angles.at[i], load_sem.at[4 + i])
        for i, phase in enumerate((phase_c_hbm, phase_r_hbm))
    ]
    for copy in [load_holo] + load_phases + loads[0] + [load_tw, load_mats] + sum(loads[1:], []) + [load_twt]:
        copy.start()


    def remote(src, dst, ss, rs, xd, d):
        return pltpu.make_async_remote_copy(
            src_ref=src, dst_ref=dst, send_sem=ss, recv_sem=rs, device_id=(xd, d), device_id_type=MESH
        )

    def send_rows(snd, rcv, ss, rs, g, h):
        pltpu.make_async_copy(snd.at[g, h, me], rcv.at[g, h, me], rs.at[g, h]).start()

        @pl.loop(1, rows)
        def _(k):
            d = lax.rem(me + k, rows)
            remote(snd.at[g, h, d], rcv.at[g, h, me], ss.at[g, h], rs.at[g, h], x, d).start()

    def wait_whole(ref, sem):
        pltpu.make_async_copy(ref, ref, sem).wait()

    def cols_forward(h):
        @pl.loop(0, 2 * per_half)
        def _(t):
            mode, j = t // per_half, lax.rem(t, per_half)
            at = at_rows(h * half_rows + j * CHUNK)
            values = []
            for n2 in range(RADIX):
                pr, pi = probe[mode, 0, at, lanes_of(n2)].astype(f32), probe[mode, 1, at, lanes_of(n2)].astype(f32)
                tr, ti = trans[0, at, lanes_of(n2)].astype(f32), trans[1, at, lanes_of(n2)].astype(f32)
                er, ei = pr * tr - pi * ti, pr * ti + pi * tr
                values.append((er.astype(bf16).astype(f32), ei.astype(bf16).astype(f32)))
            dst = at_rows(mode * half_rows + j * CHUNK)
            for k2, pair in enumerate(butterfly16(values, -1)):
                re, im = turn_by(pair, tw[0, k2 : k2 + 1, :], -tw[1, k2 : k2 + 1, :])
                uc[k2, dst, 0:LANES] = re.astype(bf16)
                uc[k2, dst, LANES : 2 * LANES] = im.astype(bf16)

        @pl.loop(0, RADIX // GROUP)
        def _(g):
            for k, pair in enumerate(middle_cols(g, 1.0, uc, mats, tw, phc)):
                k2 = g * GROUP + k
                for part, v in enumerate(pair):
                    a, b = v[:half_rows], v[half_rows:]
                    low = jnp.where(lane < LANES // 2, a, pltpu.roll(b, LANES // 2, 1))
                    high = jnp.where(lane < LANES // 2, pltpu.roll(a, LANES // 2, 1), b)
                    uc[k2, 0:half_rows, lanes_of(part)] = low.astype(bf16)
                    uc[k2, half_rows : 2 * half_rows, lanes_of(part)] = high.astype(bf16)

        @pl.loop(0, 2 * per_half)
        def _(t):
            side, j = t // per_half, lax.rem(t, per_half)
            src = at_rows(side * half_rows + j * CHUNK)
            dst = at_rows(j * CHUNK)
            values = [
                (uc[k2, src, 0:LANES].astype(f32), uc[k2, src, LANES : 2 * LANES].astype(f32)) for k2 in range(RADIX)
            ]
            for n2, (re, im) in enumerate(butterfly16(values, 1)):
                snd1[side, h, n2, 0, dst, :] = re.astype(bf16)
                snd1[side, h, n2, 1, dst, :] = im.astype(bf16)

    def cols_back(h):
        def load(side, n2, part, at):
            return rcv2[side, h, n2, part, at, :]

        def store(mode, part, j, n2, value):
            probe[mode, part, at_rows(h * half_rows + j * CHUNK), lanes_of(n2)] = value

        for side in range(2):
            back_first(load, side, uc, side * half_rows, half_rows)
        back_rest(store, lambda mode, j: None, h * half_rows, half_rows, uc, uc, probe, trans, kc)

    def rows_first(load, h):
        @pl.loop(h * per_half, (h + 1) * per_half)
        def _(j):
            at, at_im = at_rows(j * CHUNK), at_rows(LANES + j * CHUNK)
            values = [load(j, n2) for n2 in range(RADIX)]
            for k2, (re, im) in enumerate(butterfly16(values, -1)):
                ur[k2, at, :] = re.astype(bf16)
                ur[k2, at_im, :] = im.astype(bf16)

    def rows_middle(kernels):
        for k2 in range(RADIX):
            ur[k2] = dot(kernels[k2], ur[k2]).astype(bf16)

    def rows_last(store, j):
        at, at_im = at_rows(j * CHUNK), at_rows(LANES + j * CHUNK)
        values = [(ur[k2, at, :].astype(WORK), ur[k2, at_im, :].astype(WORK)) for k2 in range(RADIX)]
        for n2, (re, im) in enumerate(butterfly16(values, 1)):
            store(j, n2, re.astype(bf16), im.astype(bf16))

    def set_phase(angle):
        for part, turn in enumerate((jnp.cos, jnp.sin)):
            pht[part] = turn(angle).T * scale
        for k2 in range(RADIX):
            for part in range(2):
                tables[2 + part, k2] = jnp.broadcast_to(pht[part, :, k2 : k2 + 1], (LANES, LANES))

    def build(kernels, sign):
        @pl.loop(0, RADIX)
        def _(k2):
            c, s = mats[2, 0:LANES, 0:LANES].astype(f32), mats[2, 0:LANES, LANES : 2 * LANES].astype(f32)
            re, im = turn_by((c, -s), tables[2, k2], tables[3, k2] * sign)
            re, im = turn_by((re, im), tw[0, pl.ds(k2, 1), :], -tw[1, pl.ds(k2, 1), :])
            z = dot(mats[3], jnp.concatenate([re.astype(bf16), im.astype(bf16)], axis=0))
            re, im = turn_by((z[:LANES], z[LANES:]), tables[0, k2] * scale, tables[1, k2] * scale)
            kernels[k2, 0:LANES, 0:LANES] = re.astype(bf16)
            kernels[k2, LANES : 2 * LANES, 0:LANES] = im.astype(bf16)
            kernels[k2, 0:LANES, LANES : 2 * LANES] = (-im).astype(bf16)
            kernels[k2, LANES : 2 * LANES, LANES : 2 * LANES] = re.astype(bf16)

    def own_power(g, n2, at):
        re, im = det[g, n2, 0, at, :].astype(f32), det[g, n2, 1, at, :].astype(f32)
        return re * re + im * im

    def partner(g, j):
        return remote(isnd.at[g, j], ircv.at[g, j], isend.at[g, j], irecv.at[g, j], other, me)

    def rows_forward(g):
        def load(j, n2):
            h, at = j // per_half, at_rows(lax.rem(j, per_half) * CHUNK)
            return rcv1[g, h, n2, 0, at, :].astype(WORK), rcv1[g, h, n2, 1, at, :].astype(WORK)

        def store(j, n2, re, im):
            det[g, n2, 0, at_rows(j * CHUNK), :] = re
            det[g, n2, 1, at_rows(j * CHUNK), :] = im

        for h in range(PIECES):
            wait_whole(rcv1.at[g, h], recv1.at[g, h])
            rows_first(load, h)
        rows_middle(kf)

        @pl.loop(0, pairs)
        def _(j):
            rows_last(store, j)
            rows_last(store, j + pairs)
            for n2 in range(RADIX):
                a, b = own_power(g, n2, at_rows(j * CHUNK)), own_power(g, n2, at_rows((j + pairs) * CHUNK))
                first = lane_c < LANES // 2
                total = jnp.where(first, a, b) + pltpu.roll(jnp.where(first, b, a), LANES // 2, 1)
                isnd[g, j, n2] = total.astype(bf16)
            partner(g, j).start()

    def apply_factor(g):
        @pl.loop(0, pairs)
        def _(j):
            wait_whole(ircv.at[g, j], irecv.at[g, j])
            for n2 in range(RADIX):
                total = isnd[g, j, n2].astype(f32) + ircv[g, j, n2].astype(f32)
                measured = hbuf[g, n2, at_rows(j * CHUNK), :].astype(f32)
                factor = 1.0 - jnp.sqrt(measured) * lax.rsqrt(jnp.maximum(total, 1.0))
                swapped = pltpu.roll(factor, LANES // 2, 1)
                first = lane_c < LANES // 2
                for at, f in (
                    (at_rows(j * CHUNK), jnp.where(first, factor, swapped)),
                    (at_rows((j + pairs) * CHUNK), jnp.where(first, swapped, factor)),
                ):
                    for q in range(2):
                        det[g, n2, q, at, :] = (det[g, n2, q, at, :].astype(f32) * f).astype(bf16)

    def rows_back(g):
        def load(j, n2):
            at = at_rows(j * CHUNK)
            return det[g, n2, 0, at, :].astype(WORK), det[g, n2, 1, at, :].astype(WORK)

        def store(j, n2, re, im):
            h, at = j // per_half, at_rows(lax.rem(j, per_half) * CHUNK)
            snd2[g, h, n2, 0, at, :] = re
            snd2[g, h, n2, 1, at, :] = im

        for h in range(PIECES):
            rows_first(load, h)
        rows_middle(kb)
        for h in range(PIECES):
            @pl.loop(h * per_half, (h + 1) * per_half)
            def _(j):
                rows_last(store, j)

            send_rows(snd2, rcv2, send2, recv2, g, h)

    def spectral(natural):
        r = lax.broadcasted_iota(jnp.int32, (rows, LANES), 0)
        c = lax.broadcasted_iota(jnp.int32, (rows, LANES), 1)
        per = LANES // RADIX
        spread = jnp.where(c // per == r, 1.0, 0.0).astype(f32)
        picked = jnp.where(lax.rem(c, RADIX) == r, 1.0, 0.0).astype(f32)
        wide_r = lax.broadcasted_iota(jnp.int32, (LANES, LANES), 0)
        wide_c = lax.broadcasted_iota(jnp.int32, (LANES, LANES), 1)
        exact = lax.Precision.HIGHEST
        full = jnp.dot(natural.T, spread, precision=exact, preferred_element_type=f32)
        full = jnp.where(wide_r // RADIX == lax.rem(wide_c, per), full, 0.0)
        return jnp.dot(picked, full, precision=exact, preferred_element_type=f32)

    load_holo.wait()
    for n2 in range(RADIX):
        upper, lower = holo[0:deep, lanes_of(n2)], holo[deep : 2 * deep, lanes_of(n2)]
        low = jnp.where(lane_h < LANES // 2, upper, pltpu.roll(lower, LANES // 2, 1))
        high = jnp.where(lane_h < LANES // 2, pltpu.roll(upper, LANES // 2, 1), lower)
        hsnd[n2] = jnp.where(x == 0, low, high).astype(bf16)
    pl.semaphore_wait(barrier, rows)
    pltpu.make_async_copy(hsnd.at[me], hbuf.at[x, me], hrecv).start()

    @pl.loop(1, rows)
    def _(k):
        d = lax.rem(me + k, rows)
        remote(hsnd.at[d], hbuf.at[x, me], hsend, hrecv, x, d).start()

    for copy in load_phases:
        copy.wait()
    angle = spectral(angles[0])
    for part, turn in enumerate((jnp.cos, jnp.sin)):
        phc[part] = turn(angle) * scale
    for copy in [load_tw, load_mats]:
        copy.wait()
    for h in range(PIECES):
        for copy in loads[h]:
            copy.wait()
        cols_forward(h)
        send_rows(snd1, rcv1, send1, recv1, 0, h)
    for h in range(PIECES):
        send_rows(snd1, rcv1, send1, recv1, 1, h)

    wait_whole(hbuf.at[x], hrecv)
    forward = remote(hbuf.at[x], hbuf.at[x], xsend, xrecv, other, me)
    forward.start()

    load_twt.wait()
    for k2 in range(RADIX):
        for part in range(2):
            tables[part, k2] = jnp.broadcast_to(twt[part, :, k2 : k2 + 1], (LANES, LANES))
    set_phase(spectral(angles[1]))
    build(kf, 1.0)
    build(kb, -1.0)
    set_phase(spectral(angles[0]))
    build(kc, 1.0)
    wait_whole(hbuf.at[other], xrecv)

    for g in range(HALVES):
        rows_forward(g)
        apply_factor(g)
        rows_back(g)

    final = PIECES - 1
    for h in range(final):
        for side in range(2):
            wait_whole(rcv2.at[side, h], recv2.at[side, h])
        cols_back(h)
    wait_whole(rcv2.at[0, final], recv2.at[0, final])
    back_first(lambda side, n2, part, at: rcv2[side, final, n2, part, at, :], 0, started, 0, half_rows)
    wait_whole(rcv2.at[1, final], recv2.at[1, final])
    keep = pltpu.make_async_copy(rcv2.at[1, final], tail, load_sem.at[0])
    keep.start()

    fewer = pl.ds(0, rows - 1)
    for h in range(PIECES):
        for snd, sem in ((snd1, send1), (snd2, send2)):
            for g in range(2):
                wait_whole(snd.at[g, h, fewer], sem.at[g, h])
    wait_whole(hsnd.at[fewer], hsend)
    forward.wait_send()
    for g in range(2):
        for j in range(pairs):
            partner(g, j).wait_send()
    keep.wait()


def finish_kernel(probe, trans, kc, started, tail, out, last, uc, sems):
    height = tail.shape[2]
    top = probe.shape[2] - height
    done = pl.ds(0, top)
    early = [
        pltpu.make_async_copy(probe.at[m, :, done], out.at[m, :, done], sems.at[m]) for m in range(probe.shape[0])
    ]
    for copy in early:
        copy.start()

    def load(side, n2, part, at):
        return tail[n2, part, at, :]

    def store(mode, part, j, n2, value):
        last[mode, part, at_rows(j * CHUNK), lanes_of(n2)] = value

    chunks = height // CHUNK

    def late(m, j):
        source, target = last.at[m, :, at_rows(j * CHUNK)], out.at[m, :, at_rows(top + j * CHUNK)]
        return pltpu.make_async_copy(source, target, sems.at[2 + m * chunks + j])

    back_first(load, 1, uc, height, height)
    back_rest(store, lambda mode, j: late(mode, j).start(), top, height, started, uc, probe, trans, kc)
    for copy in early + [late(m, j) for m in range(2) for j in range(chunks)]:
        copy.wait()


def fused_local(probe_modes, transmission, hologram, phase_cols, phase_rows):
    size_a = FACTOR_A
    size_b = probe_modes.shape[3] // size_a
    mats, cosine, sine = constant_tables(size_a, size_b)
    tw = np.stack([cosine, sine])
    twt = np.stack([cosine.T, sine.T])
    angles = [phase.reshape(size_b, size_a) for phase in (phase_cols, phase_rows)]
    rows = hologram.shape[0]
    field = (2, PIECES, size_b, 2, rows // PIECES, LANES)
    bf16, dma = jnp.bfloat16, pltpu.SemaphoreType.DMA
    vmem, hbm = pl.BlockSpec(memory_space=pltpu.VMEM), pl.BlockSpec(memory_space=pltpu.MemorySpace.HBM)
    shared = (2, rows // HALVES // CHUNK, size_b, CHUNK, LANES)
    piece = rows // PIECES
    large = [probe_modes, transmission, hologram] + [jnp.asarray(table) for table in (mats, tw, twt)] + angles
    large = [pltpu.with_memory_space_constraint(array, pltpu.HBM) for array in large]
    kept = [
        (probe_modes.shape, bf16),
        (transmission.shape, bf16),
        ((size_b, 2 * LANES, 2 * LANES), bf16),
        ((size_b, piece, 2 * LANES), bf16),
        ((size_b, 2, piece, LANES), bf16),
    ]
    parts = pl.pallas_call(
        fused_kernel,
        out_shape=[pltpu.VMEM(shape, kind) for shape, kind in kept],
        in_specs=[hbm] * len(large),
        out_specs=[vmem] * len(kept),
        scratch_shapes=[
            pltpu.VMEM((2, size_b, size_a), jnp.float32),
            pltpu.VMEM(hologram.shape, jnp.float32),
            pltpu.VMEM(mats.shape, bf16),
            pltpu.VMEM(tw.shape, jnp.float32),
            pltpu.VMEM(twt.shape, jnp.float32),
            pltpu.VMEM((2, size_b, LANES), jnp.float32),
            pltpu.VMEM((2, LANES, size_b), jnp.float32),
            pltpu.VMEM((size_b, 2 * LANES, 2 * LANES), bf16),
            pltpu.VMEM((size_b, 2 * LANES, 2 * LANES), bf16),
            pltpu.VMEM(field, bf16),
            pltpu.VMEM(field, bf16),
            pltpu.VMEM(field, bf16),
            pltpu.VMEM(field, bf16),
            pltpu.VMEM((size_b, rows // HALVES, LANES), bf16),
            pltpu.VMEM((2, size_b, rows // HALVES, LANES), bf16),
            pltpu.VMEM(shared, bf16),
            pltpu.VMEM(shared, bf16),
            pltpu.VMEM((size_b, 2 * (rows // PIECES), 2 * LANES), bf16),
            pltpu.VMEM((size_b, 2 * LANES, LANES), bf16),
            pltpu.VMEM((2, size_b, 2, LANES, LANES), bf16),
            pltpu.VMEM((4, size_b, LANES, LANES), jnp.float32),
            dma((2, PIECES)),
            dma((2, PIECES)),
            dma((2, PIECES)),
            dma((2, PIECES)),
            dma,
            dma,
            dma,
            dma,
            dma(shared[:2]),
            dma(shared[:2]),
            dma((6,)),
            dma((2, PIECES)),
        ],
        compiler_params=pltpu.CompilerParams(
            collective_id=0, has_side_effects=True, vmem_limit_bytes=LIMIT_MIB * 1024 * 1024
        ),
    )(*large)
    return pl.pallas_call(
        finish_kernel,
        out_shape=jax.ShapeDtypeStruct(probe_modes.shape, bf16),
        in_specs=[vmem] * len(kept),
        out_specs=hbm,
        scratch_shapes=[
            pltpu.VMEM((2, 2, piece, probe_modes.shape[3]), bf16),
            pltpu.VMEM((size_b, 2 * piece, 2 * LANES), bf16),
            dma((2 + 2 * (piece // CHUNK),)),
        ],
        compiler_params=pltpu.CompilerParams(vmem_limit_bytes=FINISH_MIB * 1024 * 1024),
    )(*[pltpu.with_memory_space_constraint(part, pltpu.VMEM) for part in parts])


def chosen(mesh, probe_modes, *others):
    rows, modes = mesh.shape["rows"], mesh.shape["modes"]
    size = probe_modes.shape[3]
    fits = modes == 2 and probe_modes.shape[0] == 2 * modes and size == rows * FACTOR_A == RADIX * LANES
    body = fused_local if fits else local
    return jax.shard_map(
        body,
        mesh=mesh,
        in_specs=(P("modes", None, "rows", None), P(None, "rows", None), P("rows", None), P(), P()),
        out_specs=P("modes", None, "rows", None),
        check_vma=False,
    )(probe_modes, *others)


def solution(mesh):
    return functools.partial(chosen, mesh)
```
